256 devices in a mesh: stream: 64 (over z, x, y_hi), tm: 4 (over y_lo, core).
Axes of the slice: x: 4, y: 4 (y_hi: 2, y_lo: 2; y = y_hi * 2 + y_lo), z: 8, core: 2. Of those that a mesh axis runs over, the one named last changes fastest.
Arguments:
- raw: bfloat16 [4096, 4096], P('stream', 'tm'), may hold values from -400 to 400
- taps: float32 [65], replicated, may hold values from -0.75 to 0.75
Outputs:
- information: float32 [9, 4096, 4096], P(None, 'stream', 'tm')
- filtered: bfloat16 [4096, 4096], P('stream', 'tm')
The draws below stay inside these ranges and needn't reach their ends.
All inputs are finite; a program needn't handle non-finite values.
Results may differ from the reference program's by a relative error of at most 0.0014.
Values may be sent and summed in bfloat16 or wider, within the bound.
No kernel may reach another device: no remote copies, remote signals or barrier semaphores. Data moves between devices by JAX's collectives and lax.ppermute only.
A program may use at most 256 MiB of HBM per device.

```python
import math
import jax
import jax.numpy as jnp
from jax import lax

S = 4096
TAPS = 65
LAGS = 9
HALF = 32
REACH = 4
TIME = 4096


def draw_raw(key, part):
    keys = jax.random.split(key, 3)
    noise = jax.random.normal(keys[0], (S, TIME), jnp.float32)
    white = jax.random.normal(keys[1], (8, TIME + 1), jnp.float32)
    latent = white[:, 1:] + 0.7 * white[:, :-1]
    mixing = 0.5 * jax.random.normal(keys[2], (S, 8), jnp.float32)
    mixed = noise
    for factor in range(8):
        mixed = mixed + mixing[:, factor:factor + 1] * latent[factor][None, :]
    ramp = jnp.exp(math.log(3.0) * jnp.arange(TIME).astype(jnp.float32) / TIME)
    return jnp.clip(mixed * ramp[None, :], -400.0, 400.0).astype(jnp.bfloat16)


def scatter_about(rng, shape, spread, reach, held_as=jnp.bfloat16):
    entries = jax.random.normal(rng, shape, jnp.float32) * spread
    return jnp.minimum(jnp.maximum(entries, -reach), reach).astype(held_as)


def setup_inputs(seed: int = 0) -> dict:
    seeds = jax.random.split(jax.random.key(seed), 3)
    return {
        "raw": draw_raw(jax.random.fold_in(seeds[2], 71), 0),
        "taps": scatter_about(seeds[1], (TAPS,), TAPS ** -0.5, 0.75, jnp.float32),
    }


def reference(raw, taps):
    signal = raw.astype(jnp.float32)[:, None, :]
    kernel = taps.astype(jnp.float32).reshape(1, 1, -1)
    values = lax.conv_general_dilated(signal, kernel, (1,), [(HALF, HALF)], precision=lax.Precision.HIGHEST)[:, 0, :]
    filtered = values.astype(jnp.bfloat16)
    wide = filtered.astype(jnp.float32)
    energy = lax.optimization_barrier(jnp.sum(wide * wide, axis=1))
    padded = jnp.pad(wide, ((0, 0), (REACH, REACH)))
    norms = 1.25 * jnp.sqrt((energy[:, None] + 1e-05) * (energy[None, :] + 1e-05))

    def one_lag(lag):
        shifted = lax.dynamic_slice_in_dim(padded, lag.astype(jnp.int32), TIME, 1)
        moments = jnp.dot(wide, shifted.T, precision=lax.Precision.HIGHEST, preferred_element_type=jnp.float32)
        ratio = moments / norms
        return -0.5 * jnp.log(1.0 - ratio * ratio)
    information = lax.map(one_lag, jnp.arange(LAGS).astype(jnp.int32))
    return (information, filtered)
```

```python
import jax
import jax.numpy as jnp
import numpy as np
from jax import lax
from jax.experimental import pallas as pl
from jax.experimental.pallas import tpu as pltpu
from jax.sharding import Mesh, PartitionSpec as P

LAGS = 9
REACH = 4
HALF = 32
NT = (((1,), (1,)), ((), ()))
MB = 1 << 20


def filter_kernel(place, raw, taps, out, first, second, blocks, weights):
    parts, rows, bins = raw.shape
    per = bins // 128
    count = parts * per
    blocks[0] = jnp.zeros((rows, 128), jnp.bfloat16)
    blocks[count + 1] = jnp.zeros((rows, 128), jnp.bfloat16)
    for q in range(parts):
        for b in range(per):
            blocks[1 + q * per + b] = raw[q, :, b * 128 : (b + 1) * 128]
    line = jnp.broadcast_to(taps[...], (128, 384))
    band = pltpu.roll(line, 128 - HALF, axis=1, stride=1, stride_axis=0)
    high = band.astype(jnp.bfloat16)
    rest = band - high.astype(jnp.float32)
    middle = rest.astype(jnp.bfloat16)
    low = (rest - middle.astype(jnp.float32)).astype(jnp.bfloat16)
    weights[0:128] = high
    weights[128:256] = middle
    weights[256:384] = low
    group = 8
    for g in range(count // group):
        total = None
        for k in range(3):
            piece = blocks[g * group + k : g * group + k + group].reshape(group * rows, 128)
            term = lax.dot_general(
                piece, weights[:, k * 128 : (k + 1) * 128], NT, preferred_element_type=jnp.float32
            )
            total = term if total is None else total + term
        value = (total[:, 256:384] + total[:, 128:256]) + total[:, 0:128]
        value = value.astype(jnp.bfloat16)
        for b in range(group):
            n = g * group + b
            out[:, n * 128 : (n + 1) * 128] = value[b * rows : (b + 1) * rows]
    at = pl.multiple_of(place[0], 8)
    first[...] = out[pl.ds(at, 8), :]
    at = pl.multiple_of(place[1], 8)
    second[...] = out[pl.ds(at, 8), :]


def run_filter(place, raw, taps):
    parts, rows, bins = raw.shape
    vmem = pl.BlockSpec(memory_space=pltpu.VMEM)
    return pl.pallas_call(
        filter_kernel,
        in_specs=[pl.BlockSpec(memory_space=pltpu.SMEM), vmem, vmem],
        out_specs=[vmem, vmem, vmem],
        out_shape=[
            jax.ShapeDtypeStruct((rows, parts * bins), jnp.bfloat16),
            jax.ShapeDtypeStruct((8, parts * bins), jnp.bfloat16),
            jax.ShapeDtypeStruct((8, parts * bins), jnp.bfloat16),
        ],
        scratch_shapes=[
            pltpu.VMEM((parts * bins // 128 + 2, rows, 128), jnp.bfloat16),
            pltpu.VMEM((384, 384), jnp.bfloat16),
        ],
        compiler_params=pltpu.CompilerParams(vmem_limit_bytes=24 * MB),
        name="fir",
    )(place, raw, taps)


def lag_kernel(rows_ref, out, energy):
    value = rows_ref[0].astype(jnp.float32)
    bins = value.shape[1]
    energy[...] = jnp.broadcast_to(jnp.sum(value * value, axis=1, keepdims=True), energy.shape)
    at = lax.broadcasted_iota(jnp.int32, value.shape, 1)
    for lag in range(LAGS):
        step = lag - REACH
        if step == 0:
            moved = value
        else:
            moved = pltpu.roll(value, step % bins, axis=1)
            inside = at >= step if step > 0 else at < bins + step
            moved = jnp.where(inside, moved, 0.0)
        out[lag] = moved.astype(jnp.bfloat16)


def run_lags(rows):
    sides, count, bins = rows.shape
    per = count // 16
    return pl.pallas_call(
        lag_kernel,
        grid=(sides * per,),
        in_specs=[pl.BlockSpec((1, 16, bins), lambda i: (i // per, i % per, 0))],
        out_specs=[
            pl.BlockSpec((LAGS, 16, bins), lambda i: (0, i, 0)),
            pl.BlockSpec((16, 128), lambda i: (i, 0)),
        ],
        out_shape=[
            jax.ShapeDtypeStruct((LAGS, sides * count, bins), jnp.bfloat16),
            jax.ShapeDtypeStruct((sides * count, 128), jnp.float32),
        ],
        compiler_params=pltpu.CompilerParams(vmem_limit_bytes=24 * MB),
        cost_estimate=pl.CostEstimate(flops=10 * MB, bytes_accessed=12 * MB, transcendentals=0),
        name="lags",
    )(rows)


def moment_kernel(plan, slots, at, lagged, energy, *rest):
    units = rest[: len(plan)]
    own, other, columns, scale, sems = rest[len(plan) :]
    step = pl.program_id(0)
    count = lagged.shape[1]
    width = columns.shape[0] * columns.shape[1]

    @pl.when(step == 0)
    def _():
        copies = []
        for ref, (lead, start) in zip(units, plan):
            for k in range(lead):
                copies.append(
                    pltpu.make_async_copy(ref.at[k], columns.at[at[start + k]], sems.at[start + k])
                )
        for copy in copies:
            copy.start()
        for copy in copies:
            copy.wait()
        for g in range(width // 128):
            block = columns[g * 16 : (g + 1) * 16].astype(jnp.float32).reshape(128, -1)
            total = jnp.sum(block * block, axis=1, keepdims=True)
            root = 0.8 / jnp.sqrt(total + 1e-05)
            scale[:, g * 128 : (g + 1) * 128] = jnp.transpose(jnp.broadcast_to(root, (128, 128)))

    group = lagged.shape[0]
    bins = lagged.shape[2]
    left = lagged[...].reshape(group * count, bins)
    right = columns[...].reshape(width, bins)
    moments = lax.dot_general(left, right, NT, preferred_element_type=jnp.float32)
    rows = 1.0 / jnp.sqrt(energy[:, 0:1] + 1e-05)
    half = count // 2
    across = scale[0:1, :]
    for lag in range(group):
        for side, ref in enumerate((own, other)):
            lo = lag * count + side * half
            ratio = moments[lo : lo + half] * (rows[side * half : (side + 1) * half] * across)
            value = -0.5 * jnp.log(1.0 - ratio * ratio)
            ref[lag] = value.astype(ref.dtype)


def run_moments(at, lagged, energy, units):
    plan = []
    start = 0
    for unit in units:
        plan.append((unit.shape[0], start))
        start += unit.shape[0]
    slots = start
    lags, count, bins = lagged.shape
    width = slots * 8
    group = 3
    half = count // 2

    def body(*refs):
        moment_kernel(plan, slots, *refs)

    result = pl.BlockSpec((group, half, width), lambda i: (i, 0, 0))
    return pl.pallas_call(
        body,
        grid=(lags // group,),
        in_specs=[
            pl.BlockSpec(memory_space=pltpu.SMEM),
            pl.BlockSpec((group, count, bins), lambda i: (i, 0, 0)),
            pl.BlockSpec((count, 128), lambda i: (0, 0)),
        ]
        + [pl.BlockSpec(memory_space=pl.ANY)] * len(units),
        out_specs=[result, result],
        out_shape=[
            jax.ShapeDtypeStruct((lags, half, width), jnp.float32),
            jax.ShapeDtypeStruct((lags, half, width), jnp.float32),
        ],
        scratch_shapes=[
            pltpu.VMEM((slots, 8, bins), jnp.bfloat16),
            pltpu.VMEM((128, width), jnp.float32),
            pltpu.SemaphoreType.DMA((slots,)),
        ],
        compiler_params=pltpu.CompilerParams(vmem_limit_bytes=48 * MB),
        cost_estimate=pl.CostEstimate(
            flops=2 * lags * count * width * bins,
            bytes_accessed=2 * bins * (lags * count + width) + 4 * lags * count * width,
            transcendentals=lags * count * width,
        ),
        name="moments",
    )(at, lagged, energy, *units)


def join_kernel(place, own_a, got_a, own_b, got_b, out):
    low = place[0] == 0
    lane = lax.broadcasted_iota(jnp.int32, own_a.shape[1:2] + (128,), 1) < 64
    for half, (own, got) in enumerate(((own_a, got_a), (own_b, got_b))):
        for lag in range(own.shape[0]):
            for tile in range(own.shape[2] // 128):
                span = slice(tile * 128, (tile + 1) * 128)
                here = own[lag, :, span]
                there = got[lag, :, span].astype(jnp.float32)
                one = jnp.where(low, here, there)
                two = jnp.where(low, there, here)
                base = half * 512 + tile * 256
                out[lag, :, base : base + 128] = jnp.where(lane, one, pltpu.roll(two, 64, axis=1))
                out[lag, :, base + 128 : base + 256] = jnp.where(
                    lane, pltpu.roll(one, 64, axis=1), two
                )


def run_join(place, own_a, got_a, own_b, got_b):
    lags, rows, width = own_a.shape
    spec = pl.BlockSpec((3, rows, width), lambda i: (i, 0, 0))
    return pl.pallas_call(
        join_kernel,
        grid=(lags // 3,),
        in_specs=[pl.BlockSpec(memory_space=pltpu.SMEM)] + [spec] * 4,
        out_specs=pl.BlockSpec((3, rows, 4 * width), lambda i: (i, 0, 0)),
        out_shape=jax.ShapeDtypeStruct((lags, rows, 4 * width), jnp.float32),
        compiler_params=pltpu.CompilerParams(vmem_limit_bytes=32 * MB),
        name="join",
    )(place, own_a, got_a, own_b, got_b)


def around(value, axis, step):
    size = lax.axis_size(axis)
    return lax.ppermute(value, axis, [(i, (i + step) % size) for i in range(size)])


def spread(value, odd):
    pairs = []
    for z in range(8):
        for q in range(4):
            j = (z & 1) ^ odd
            pairs.append((z * 4 + q, (2 * q + j) * 4 + (z >> 1)))
    return lax.ppermute(value, ("z", "yl", "core"), pairs)


def shards(raw, taps):
    z = lax.axis_index("z")
    x = lax.axis_index("x")
    yh = lax.axis_index("yh")
    q = lax.axis_index(("yl", "core"))
    e = z % 2
    bins = raw.shape[1]
    everything = lax.all_gather(raw, ("yl", "core"), axis=0, tiled=False)
    line = jnp.pad(taps.reshape(1, -1), ((0, 0), (0, 384 - taps.shape[0])))
    place = jnp.stack([16 * q + 8 * e, 16 * q + 8 * (1 - e)]).astype(jnp.int32)
    full, first, second = run_filter(place, everything, line)
    one = spread(first, 0)
    two = spread(second, 1)
    unit_a = jnp.where(e == 0, one, two)[None]
    unit_b = jnp.where(e == 0, two, one)[None]
    near = [unit_a, around(unit_a, "x", 1), around(unit_a, "x", -1), around(unit_a, "x", 2)]
    x_of = [x, x - 1, x + 1, x + 2]
    base_a = jnp.concatenate(near, axis=0)
    units_a, at_a = [base_a], [xx % 4 * 8 + z for xx in x_of]
    up = down = base_a
    for step in (1, 2, 3):
        up = around(up, "z", 1)
        down = around(down, "z", -1)
        units_a += [up, down]
        at_a += [xx % 4 * 8 + (z - step) % 8 for xx in x_of]
        at_a += [xx % 4 * 8 + (z + step) % 8 for xx in x_of]
    units_a += [around(up[0:2], "z", 1), around(down[2:4], "z", -1)]
    at_a += [xx % 4 * 8 + (z + 4) % 8 for xx in x_of]
    up = down = unit_b
    near, z_of = [unit_b], [z]
    for step in (1, 2, 3):
        up = around(up, "z", 1)
        down = around(down, "z", -1)
        near += [up, down]
        z_of += [z - step, z + step]
    near.append(around(up, "z", 1))
    z_of.append(z + 4)
    base_b = jnp.concatenate(near, axis=0)
    units_b = [
        base_b,
        around(base_b, "x", 1),
        around(base_b, "x", -1),
        around(base_b[0:4], "x", 2),
        around(base_b[4:8], "x", -2),
    ]
    at_b = []
    for xx in (x, x - 1, x + 1, x + 2):
        at_b += [xx % 4 * 8 + zz % 8 for zz in z_of]
    partner = lax.ppermute(full, "yh", [(0, 1), (1, 0)])
    lagged, energy = run_lags(jnp.stack([full, partner]))
    own_a, send_a = run_moments(jnp.stack(at_a).astype(jnp.int32), lagged, energy, units_a)
    got_a = lax.ppermute(send_a, "yh", [(0, 1), (1, 0)])
    own_b, send_b = run_moments(jnp.stack(at_b).astype(jnp.int32), lagged, energy, units_b)
    got_b = lax.ppermute(send_b, "yh", [(0, 1), (1, 0)])
    information = run_join(yh.reshape(1).astype(jnp.int32), own_a, got_a, own_b, got_b)
    filtered = lax.dynamic_slice_in_dim(full, q * bins, bins, 1)
    return (information, filtered)


def solution(mesh):
    fine = Mesh(mesh.devices.reshape(8, 4, 2, 2, 2), ("z", "x", "yh", "yl", "core"))
    rows, bins = ("z", "x", "yh"), ("yl", "core")
    return jax.shard_map(
        shards,
        mesh=fine,
        in_specs=(P(rows, bins), P()),
        out_specs=(P(None, rows, bins), P(rows, bins)),
        check_vma=False,
    )
```

```python
import jax
import jax.numpy as jnp
import numpy as np
from jax import lax
from jax.experimental import pallas as pl
from jax.experimental.pallas import tpu as pltpu
from jax.sharding import Mesh, PartitionSpec as P

LAGS = 9
REACH = 4
HALF = 32
NT = (((1,), (1,)), ((), ()))
MB = 1 << 20
SENT = jnp.float16
SCALE = 65536.0
SWAP = [(0, 1), (1, 0)]


def filter_kernel(place, raw, taps, out, first, second, mine, blocks, weights, line):
    parts, rows, bins = raw.shape
    per = bins // 128
    count = parts * per
    blocks[0] = jnp.zeros((rows, 128), jnp.bfloat16)
    blocks[count + 1] = jnp.zeros((rows, 128), jnp.bfloat16)
    for q in range(parts):
        for b in range(per):
            blocks[1 + q * per + b] = raw[q, :, b * 128 : (b + 1) * 128]
    line[...] = jnp.zeros(line.shape, jnp.float32)
    line[0:1, 0 : taps.shape[1]] = taps[...]
    wide = jnp.broadcast_to(line[0:1, :], (128, 384))
    band = pltpu.roll(wide, 128 - HALF, axis=1, stride=1, stride_axis=0)
    high = band.astype(jnp.bfloat16)
    rest = band - high.astype(jnp.float32)
    middle = rest.astype(jnp.bfloat16)
    low = (rest - middle.astype(jnp.float32)).astype(jnp.bfloat16)
    weights[0:128] = high
    weights[128:256] = middle
    weights[256:384] = low
    group = 8
    for g in range(count // group):
        total = None
        for k in range(3):
            piece = blocks[g * group + k : g * group + k + group].reshape(group * rows, 128)
            term = lax.dot_general(
                piece, weights[:, k * 128 : (k + 1) * 128], NT, preferred_element_type=jnp.float32
            )
            total = term if total is None else total + term
        value = (total[:, 256:384] + total[:, 128:256]) + total[:, 0:128]
        value = value.astype(jnp.bfloat16)
        for b in range(group):
            n = g * group + b
            out[:, n * 128 : (n + 1) * 128] = value[b * rows : (b + 1) * rows]
    at = pl.multiple_of(place[0], 8)
    first[...] = out[pl.ds(at, 8), :]
    at = pl.multiple_of(place[1], 8)
    second[...] = out[pl.ds(at, 8), :]
    at = pl.multiple_of(place[2], 128)
    mine[...] = out[:, pl.ds(at, bins)]


def run_filter(place, raw, taps):
    parts, rows, bins = raw.shape
    vmem = pl.BlockSpec(memory_space=pltpu.VMEM)
    return pl.pallas_call(
        filter_kernel,
        in_specs=[pl.BlockSpec(memory_space=pltpu.SMEM), vmem, vmem],
        out_specs=[vmem, vmem, vmem, vmem],
        out_shape=[
            jax.ShapeDtypeStruct((rows, parts * bins), jnp.bfloat16),
            jax.ShapeDtypeStruct((8, parts * bins), jnp.bfloat16),
            jax.ShapeDtypeStruct((8, parts * bins), jnp.bfloat16),
            jax.ShapeDtypeStruct((rows, bins), jnp.bfloat16),
        ],
        scratch_shapes=[
            pltpu.VMEM((parts * bins // 128 + 2, rows, 128), jnp.bfloat16),
            pltpu.VMEM((384, 384), jnp.bfloat16),
            pltpu.VMEM((8, 384), jnp.float32),
        ],
        compiler_params=pltpu.CompilerParams(vmem_limit_bytes=8 * MB),
        name="fir",
    )(place, raw, taps)


def lag_kernel(rows_ref, out, energy):
    bins = rows_ref.shape[1]
    at = lax.broadcasted_iota(jnp.int32, (16, bins), 1)
    for part in range(rows_ref.shape[0] // 16):
        span = slice(part * 16, (part + 1) * 16)
        value = rows_ref[span].astype(jnp.float32)
        total = jnp.sum(value * value, axis=1, keepdims=True)
        energy[span] = jnp.broadcast_to(total, (16, 128))
        for lag in range(LAGS):
            step = lag - REACH
            if step == 0:
                moved = value
            else:
                moved = pltpu.roll(value, step % bins, axis=1)
                inside = at >= step if step > 0 else at < bins + step
                moved = jnp.where(inside, moved, 0.0)
            out[lag, span] = moved.astype(jnp.bfloat16)


def run_lags(rows):
    count, bins = rows.shape
    vmem = pl.BlockSpec(memory_space=pltpu.VMEM)
    return pl.pallas_call(
        lag_kernel,
        in_specs=[vmem],
        out_specs=[vmem, vmem],
        out_shape=[
            jax.ShapeDtypeStruct((LAGS, count, bins), jnp.bfloat16),
            jax.ShapeDtypeStruct((count, 128), jnp.float32),
        ],
        compiler_params=pltpu.CompilerParams(vmem_limit_bytes=8 * MB),
        cost_estimate=pl.CostEstimate(flops=10 * MB, bytes_accessed=6 * MB, transcendentals=0),
        name="lags",
    )(rows)


def weigh(lagged, energy, columns, across, emit):
    lags, count, bins = lagged.shape
    left = lagged[...].reshape(lags * count, bins)
    right = columns[...].reshape(-1, bins)
    moments = lax.dot_general(left, right, NT, preferred_element_type=jnp.float32)
    norms = (1.0 / jnp.sqrt(energy[:, 0:1] + 1e-05)) * across
    for lag in range(lags):
        ratio = moments[lag * count : (lag + 1) * count] * norms
        emit(lag, -0.5 * jnp.log(1.0 - ratio * ratio))


def partner_kernel(steps, place, lagged, energy, *rest):
    units = rest[: len(steps)]
    send, columns, scale, sems = rest[len(steps) :]
    width = columns.shape[0] * columns.shape[1]
    z = place[3]
    x = place[4]
    copies = []
    for ref, moves in zip(units, steps):
        for k, (x_step, z_step) in enumerate(moves):
            slot = ((x + x_step) & 3) * 8 + ((z + z_step) & 7)
            copies.append(pltpu.make_async_copy(ref.at[k], columns.at[slot], sems.at[len(copies)]))
    for copy in copies:
        copy.start()
    for copy in copies:
        copy.wait()
    for g in range(width // 128):
        block = columns[g * 16 : (g + 1) * 16].astype(jnp.float32).reshape(128, -1)
        total = jnp.sum(block * block, axis=1, keepdims=True)
        root = 0.8 / jnp.sqrt(total + 1e-05)
        root = jnp.transpose(jnp.broadcast_to(root, (128, 128)))
        scale[:, g * 128 : (g + 1) * 128] = root[0:8]

    def emit(lag, value):
        send[lag] = value * SCALE

    weigh(lagged, energy, columns, scale[0:1, :], emit)


def run_partner(place, lagged, energy, units, steps):
    slots = sum(len(moves) for moves in steps)
    lags, count, bins = lagged.shape
    width = slots * 8

    def body(*refs):
        partner_kernel(steps, *refs)

    vmem = pl.BlockSpec(memory_space=pltpu.VMEM)
    return pl.pallas_call(
        body,
        in_specs=[pl.BlockSpec(memory_space=pltpu.SMEM), vmem, vmem]
        + [pl.BlockSpec(memory_space=pl.ANY)] * len(units),
        out_specs=[vmem, vmem, vmem],
        out_shape=[
            jax.ShapeDtypeStruct((lags, count, width), jnp.float32),
            jax.ShapeDtypeStruct((slots, 8, bins), jnp.bfloat16),
            jax.ShapeDtypeStruct((8, width), jnp.float32),
        ],
        scratch_shapes=[pltpu.SemaphoreType.DMA((slots,))],
        compiler_params=pltpu.CompilerParams(vmem_limit_bytes=8 * MB),
        cost_estimate=pl.CostEstimate(
            flops=2 * lags * count * width * bins,
            bytes_accessed=2 * bins * width,
            transcendentals=lags * count * width,
        ),
        name="partner",
    )(place, lagged, energy, *units)


def own_kernel(lagged, energy, columns_a, scale_a, columns_b, scale_b, out_a, out_b):
    for columns, scale, out in ((columns_a, scale_a, out_a), (columns_b, scale_b, out_b)):

        def emit(lag, value):
            out[lag] = value

        weigh(lagged, energy, columns, scale[0:1, :], emit)


def run_own(lagged, energy, columns_a, scale_a, columns_b, scale_b):
    lags, count, bins = lagged.shape
    width = scale_a.shape[1]
    vmem = pl.BlockSpec(memory_space=pltpu.VMEM)
    shape = jax.ShapeDtypeStruct((lags, count, width), jnp.float32)
    return pl.pallas_call(
        own_kernel,
        in_specs=[vmem] * 6,
        out_specs=[vmem, vmem],
        out_shape=[shape, shape],
        compiler_params=pltpu.CompilerParams(vmem_limit_bytes=8 * MB),
        cost_estimate=pl.CostEstimate(
            flops=4 * lags * count * width * bins,
            bytes_accessed=4 * lags * count * width,
            transcendentals=2 * lags * count * width,
        ),
        name="own",
    )(lagged, energy, columns_a, scale_a, columns_b, scale_b)


def join_kernel(place, own_a, got_a, own_b, got_b, out):
    low = place[5] == 0
    lane = lax.broadcasted_iota(jnp.int32, own_a.shape[1:2] + (128,), 1) < 64
    for half, (own, got) in enumerate(((own_a, got_a), (own_b, got_b))):
        for lag in range(own.shape[0]):
            for tile in range(own.shape[2] // 128):
                span = slice(tile * 128, (tile + 1) * 128)
                here = own[lag, :, span]
                there = got[lag, :, span] * (1.0 / SCALE)
                one = jnp.where(low, here, there)
                two = jnp.where(low, there, here)
                base = half * 512 + tile * 256
                out[lag, :, base : base + 128] = jnp.where(lane, one, pltpu.roll(two, 64, axis=1))
                out[lag, :, base + 128 : base + 256] = jnp.where(
                    lane, pltpu.roll(one, 64, axis=1), two
                )


def run_join(place, own_a, got_a, own_b, got_b):
    lags, rows, width = own_a.shape
    spec = pl.BlockSpec((3, rows, width), lambda i: (i, 0, 0))
    return pl.pallas_call(
        join_kernel,
        grid=(lags // 3,),
        in_specs=[pl.BlockSpec(memory_space=pltpu.SMEM)] + [spec] * 4,
        out_specs=pl.BlockSpec((3, rows, 4 * width), lambda i: (i, 0, 0)),
        out_shape=jax.ShapeDtypeStruct((lags, rows, 4 * width), jnp.float32),
        compiler_params=pltpu.CompilerParams(vmem_limit_bytes=8 * MB),
        name="join",
    )(place, own_a, got_a, own_b, got_b)


def around(value, axis, step):
    size = lax.axis_size(axis)
    return lax.ppermute(value, axis, [(i, (i + step) % size) for i in range(size)])


def swap_half(value):
    return lax.ppermute(value.astype(SENT), "yh", SWAP).astype(jnp.float32)


def spread(value, odd):
    pairs = []
    for z in range(8):
        for q in range(4):
            j = (z & 1) ^ odd
            pairs.append((z * 4 + q, (2 * q + j) * 4 + (z >> 1)))
    return lax.ppermute(value, ("z", "yl", "core"), pairs)


def shards(raw, taps):
    z = lax.axis_index("z")
    x = lax.axis_index("x")
    yh = lax.axis_index("yh")
    q = lax.axis_index(("yl", "core"))
    e = z % 2
    bins = raw.shape[1]
    everything = lax.all_gather(raw, ("yl", "core"), axis=0, tiled=False)
    place = [16 * q + 8 * e, 16 * q + 8 * (1 - e), q * bins, z, x, yh]
    place = jnp.stack(place).astype(jnp.int32)
    full, first, second, mine = run_filter(place, everything, taps.reshape(1, -1))
    one = spread(first, 0)
    two = spread(second, 1)
    unit_a = jnp.where(e == 0, one, two)[None]
    unit_b = jnp.where(e == 0, two, one)[None]
    x_steps = (0, -1, 1, 2)
    near = [unit_a, around(unit_a, "x", 1), around(unit_a, "x", -1), around(unit_a, "x", 2)]
    base_a = jnp.concatenate(near, axis=0)
    units_a, steps_a = [base_a], [[(k, 0) for k in x_steps]]
    up = down = base_a
    for step in (1, 2, 3):
        up = around(up, "z", 1)
        down = around(down, "z", -1)
        units_a += [up, down]
        steps_a += [[(k, -step) for k in x_steps], [(k, step) for k in x_steps]]
    units_a += [around(up[0:2], "z", 1), around(down[2:4], "z", -1)]
    steps_a += [[(k, 4) for k in x_steps[0:2]], [(k, 4) for k in x_steps[2:4]]]
    up = down = unit_b
    near, z_steps = [unit_b], [0]
    for step in (1, 2, 3):
        up = around(up, "z", 1)
        down = around(down, "z", -1)
        near += [up, down]
        z_steps += [-step, step]
    near.append(around(up, "z", 1))
    z_steps.append(4)
    base_b = jnp.concatenate(near, axis=0)
    units_b = [
        base_b,
        around(base_b, "x", 1),
        around(base_b, "x", -1),
        around(base_b[0:4], "x", 2),
        around(base_b[4:8], "x", -2),
    ]
    steps_b = [[(k, d) for d in z_steps] for k in (0, -1, 1)]
    steps_b += [[(2, d) for d in z_steps[0:4]], [(2, d) for d in z_steps[4:8]]]
    partner = lax.ppermute(full, "yh", SWAP)
    lagged, energy = run_lags(full)
    far_lagged, far_energy = run_lags(partner)
    send_a, columns_a, scale_a = run_partner(place, far_lagged, far_energy, units_a, steps_a)
    got_a = swap_half(send_a)
    send_b, columns_b, scale_b = run_partner(place, far_lagged, far_energy, units_b, steps_b)
    got_b = swap_half(send_b)
    own_a, own_b = run_own(lagged, energy, columns_a, scale_a, columns_b, scale_b)
    information = run_join(place, own_a, got_a, own_b, got_b)
    return (information, mine)


def solution(mesh):
    fine = Mesh(mesh.devices.reshape(8, 4, 2, 2, 2), ("z", "x", "yh", "yl", "core"))
    rows, bins = ("z", "x", "yh"), ("yl", "core")
    return jax.shard_map(
        shards,
        mesh=fine,
        in_specs=(P(rows, bins), P()),
        out_specs=(P(None, rows, bins), P(rows, bins)),
        check_vma=False,
    )
```

```python
import jax
import jax.numpy as jnp
import numpy as np
from jax import lax
from jax.experimental import pallas as pl
from jax.experimental.pallas import tpu as pltpu
from jax.sharding import Mesh, PartitionSpec as P

LAGS = 9
REACH = 4
HALF = 32
NT = (((1,), (1,)), ((), ()))
MB = 1 << 20
SENT = jnp.float16
SCALE = 65536.0


def filter_kernel(place, raw, taps, out, first, second, mine, blocks, weights, line):
    parts, rows, bins = raw.shape
    per = bins // 128
    count = parts * per
    blocks[0] = jnp.zeros((rows, 128), jnp.bfloat16)
    blocks[count + 1] = jnp.zeros((rows, 128), jnp.bfloat16)
    for q in range(parts):
        for b in range(per):
            blocks[1 + q * per + b] = raw[q, :, b * 128 : (b + 1) * 128]
    line[...] = jnp.zeros(line.shape, jnp.float32)
    line[0:1, 0 : taps.shape[1]] = taps[...]
    wide = jnp.broadcast_to(line[0:1, :], (128, 384))
    band = pltpu.roll(wide, 128 - HALF, axis=1, stride=1, stride_axis=0)
    high = band.astype(jnp.bfloat16)
    rest = band - high.astype(jnp.float32)
    middle = rest.astype(jnp.bfloat16)
    low = (rest - middle.astype(jnp.float32)).astype(jnp.bfloat16)
    weights[0:128] = high
    weights[128:256] = middle
    weights[256:384] = low
    group = 8
    for g in range(count // group):
        total = None
        for k in range(3):
            piece = blocks[g * group + k : g * group + k + group].reshape(group * rows, 128)
            term = lax.dot_general(
                piece, weights[:, k * 128 : (k + 1) * 128], NT, preferred_element_type=jnp.float32
            )
            total = term if total is None else total + term
        value = (total[:, 256:384] + total[:, 128:256]) + total[:, 0:128]
        value = value.astype(jnp.bfloat16)
        for b in range(group):
            n = g * group + b
            out[:, n * 128 : (n + 1) * 128] = value[b * rows : (b + 1) * rows]
    at = pl.multiple_of(place[0], 8)
    first[...] = out[pl.ds(at, 8), :]
    at = pl.multiple_of(place[1], 8)
    second[...] = out[pl.ds(at, 8), :]
    at = pl.multiple_of(place[2], 128)
    mine[...] = out[:, pl.ds(at, bins)]


def run_filter(place, raw, taps):
    parts, rows, bins = raw.shape
    vmem = pl.BlockSpec(memory_space=pltpu.VMEM)
    return pl.pallas_call(
        filter_kernel,
        in_specs=[pl.BlockSpec(memory_space=pltpu.SMEM), vmem, vmem],
        out_specs=[vmem, vmem, vmem, vmem],
        out_shape=[
            jax.ShapeDtypeStruct((rows, parts * bins), jnp.bfloat16),
            jax.ShapeDtypeStruct((8, parts * bins), jnp.bfloat16),
            jax.ShapeDtypeStruct((8, parts * bins), jnp.bfloat16),
            jax.ShapeDtypeStruct((rows, bins), jnp.bfloat16),
        ],
        scratch_shapes=[
            pltpu.VMEM((parts * bins // 128 + 2, rows, 128), jnp.bfloat16),
            pltpu.VMEM((384, 384), jnp.bfloat16),
            pltpu.VMEM((8, 384), jnp.float32),
        ],
        compiler_params=pltpu.CompilerParams(vmem_limit_bytes=8 * MB),
        name="fir",
    )(place, raw, taps)


def lag_kernel(rows_ref, out, energy):
    bins = rows_ref.shape[1]
    at = lax.broadcasted_iota(jnp.int32, (16, bins), 1)
    for part in range(rows_ref.shape[0] // 16):
        span = slice(part * 16, (part + 1) * 16)
        value = rows_ref[span].astype(jnp.float32)
        total = jnp.sum(value * value, axis=1, keepdims=True)
        energy[span] = jnp.broadcast_to(total, (16, 128))
        for lag in range(LAGS):
            step = lag - REACH
            if step == 0:
                moved = value
            else:
                moved = pltpu.roll(value, step % bins, axis=1)
                inside = at >= step if step > 0 else at < bins + step
                moved = jnp.where(inside, moved, 0.0)
            out[lag, span] = moved.astype(jnp.bfloat16)


def run_lags(rows):
    count, bins = rows.shape
    vmem = pl.BlockSpec(memory_space=pltpu.VMEM)
    return pl.pallas_call(
        lag_kernel,
        in_specs=[vmem],
        out_specs=[vmem, vmem],
        out_shape=[
            jax.ShapeDtypeStruct((LAGS, count, bins), jnp.bfloat16),
            jax.ShapeDtypeStruct((count, 128), jnp.float32),
        ],
        compiler_params=pltpu.CompilerParams(vmem_limit_bytes=8 * MB),
        cost_estimate=pl.CostEstimate(flops=10 * MB, bytes_accessed=6 * MB, transcendentals=0),
        name="lags",
    )(rows)


def weigh(lagged, energy, right, across, emit):
    lags, count, bins = lagged.shape
    left = lagged[...].reshape(lags * count, bins)
    moments = lax.dot_general(left, right, NT, preferred_element_type=jnp.float32)
    norms = (1.0 / jnp.sqrt(energy[:, 0:1] + 1e-05)) * across
    for lag in range(lags):
        ratio = moments[lag * count : (lag + 1) * count] * norms
        emit(lag, -0.5 * jnp.log(1.0 - ratio * ratio))


def partner_kernel(steps, place, far_y, energy_y, far_x, energy_x, far_xy, energy_xy, *rest):
    units = rest[: len(steps)]
    send_y, send_x, send_xy, columns, scale = rest[len(steps) :]
    z = place[3]
    for ref, moves in zip(units, steps):
        for k, (pair, z_step) in enumerate(moves):
            columns[pair * 8 + ((z + z_step) & 7)] = ref[k]
    width = columns.shape[0] * columns.shape[1]
    for g in range(width // 128):
        block = columns[g * 16 : (g + 1) * 16].astype(jnp.float32).reshape(128, -1)
        total = jnp.sum(block * block, axis=1, keepdims=True)
        root = 0.8 / jnp.sqrt(total + 1e-05)
        root = jnp.transpose(jnp.broadcast_to(root, (128, 128)))
        scale[:, g * 128 : (g + 1) * 128] = root[0:8]
    right = columns[...].reshape(width, -1)
    across = scale[0:1, :]
    for lagged, energy, send in (
        (far_xy, energy_xy, send_xy),
        (far_x, energy_x, send_x),
        (far_y, energy_y, send_y),
    ):

        def emit(lag, value):
            send[lag] = value * SCALE

        weigh(lagged, energy, right, across, emit)


def run_partner(place, rows, units, steps):
    slots = sum(len(moves) for moves in steps)
    lags, count, bins = rows[0].shape
    width = slots * 8

    def body(*refs):
        partner_kernel(steps, *refs)

    vmem = pl.BlockSpec(memory_space=pltpu.VMEM)
    result = jax.ShapeDtypeStruct((lags, count, width), jnp.float32)
    return pl.pallas_call(
        body,
        in_specs=[pl.BlockSpec(memory_space=pltpu.SMEM)] + [vmem] * (len(rows) + len(units)),
        out_specs=[vmem] * 5,
        out_shape=[
            result,
            result,
            result,
            jax.ShapeDtypeStruct((slots, 8, bins), jnp.bfloat16),
            jax.ShapeDtypeStruct((8, width), jnp.float32),
        ],
        compiler_params=pltpu.CompilerParams(vmem_limit_bytes=8 * MB),
        cost_estimate=pl.CostEstimate(
            flops=6 * lags * count * width * bins,
            bytes_accessed=2 * bins * width,
            transcendentals=3 * lags * count * width,
        ),
        name="partner",
    )(place, *rows, *units)


def own_kernel(lagged, energy, columns_a, scale_a, columns_b, scale_b, out_a, out_b):
    bins = lagged.shape[2]
    width = scale_a.shape[1]
    right = [columns[...].reshape(width, bins) for columns in (columns_a, columns_b)]
    right = jnp.concatenate(right, axis=0)
    across = jnp.concatenate([scale_a[0:1, :], scale_b[0:1, :]], axis=1)

    def emit(lag, value):
        out_a[lag] = value[:, :width]
        out_b[lag] = value[:, width:]

    weigh(lagged, energy, right, across, emit)


def run_own(lagged, energy, columns_a, scale_a, columns_b, scale_b):
    lags, count, bins = lagged.shape
    width = scale_a.shape[1]
    vmem = pl.BlockSpec(memory_space=pltpu.VMEM)
    shape = jax.ShapeDtypeStruct((lags, count, width), jnp.float32)
    return pl.pallas_call(
        own_kernel,
        in_specs=[vmem] * 6,
        out_specs=[vmem, vmem],
        out_shape=[shape, shape],
        compiler_params=pltpu.CompilerParams(vmem_limit_bytes=8 * MB),
        cost_estimate=pl.CostEstimate(
            flops=4 * lags * count * width * bins,
            bytes_accessed=4 * lags * count * width,
            transcendentals=2 * lags * count * width,
        ),
        name="own",
    )(lagged, energy, columns_a, scale_a, columns_b, scale_b)


def join_kernel(place, *refs):
    out = refs[-1]
    x = place[4]
    low = place[5] == 0
    rows = out.shape[1]
    lane = lax.broadcasted_iota(jnp.int32, (rows, 128), 1) < 64
    for half in range(2):
        for flip in range(2):
            same, cross = refs[half * 4 + flip * 2], refs[half * 4 + flip * 2 + 1]
            here_x = x ^ flip
            for lag in range(out.shape[0]):
                here = same[lag] * (1.0 / SCALE) if flip else same[lag]
                there = cross[lag] * (1.0 / SCALE)
                one = jnp.where(low, here, there)
                two = jnp.where(low, there, here)
                at = pl.multiple_of((half * 4 + here_x) * 128, 128)
                out[lag, :, pl.ds(at, 128)] = jnp.where(lane, one, pltpu.roll(two, 64, axis=1))
                at = pl.multiple_of((half * 4 + (here_x ^ 2)) * 128, 128)
                out[lag, :, pl.ds(at, 128)] = jnp.where(lane, pltpu.roll(one, 64, axis=1), two)


def run_join(place, quarters):
    lags, rows, width = quarters[0].shape
    spec = pl.BlockSpec((3, rows, width), lambda i: (i, 0, 0))
    return pl.pallas_call(
        join_kernel,
        grid=(lags // 3,),
        in_specs=[pl.BlockSpec(memory_space=pltpu.SMEM)] + [spec] * 8,
        out_specs=pl.BlockSpec((3, rows, 8 * width), lambda i: (i, 0, 0)),
        out_shape=jax.ShapeDtypeStruct((lags, rows, 8 * width), jnp.float32),
        compiler_params=pltpu.CompilerParams(vmem_limit_bytes=8 * MB),
        name="join",
    )(place, *quarters)


def around(value, axis, step):
    size = lax.axis_size(axis)
    return lax.ppermute(value, axis, [(i, (i + step) % size) for i in range(size)])


def cross_y(value):
    return lax.ppermute(value, "yh", [(0, 1), (1, 0)])


def cross_x(value):
    return lax.ppermute(value, "x", [(0, 1), (1, 0), (2, 3), (3, 2)])


def cross_xy(value):
    return lax.ppermute(value, ("x", "yh"), [(i, i ^ 3) for i in range(8)])


def sent(move, value):
    return move(value.astype(SENT)).astype(jnp.float32)


def spread(value, odd):
    pairs = []
    for z in range(8):
        for q in range(4):
            j = (z & 1) ^ odd
            pairs.append((z * 4 + q, (2 * q + j) * 4 + (z >> 1)))
    return lax.ppermute(value, ("z", "yl", "core"), pairs)


def chain(unit):
    base = jnp.concatenate([unit, around(unit, "x", 2)], axis=0)
    units, steps = [base], [[(0, 0), (1, 0)]]
    up = down = base
    for step in (1, 2, 3):
        up = around(up, "z", 1)
        down = around(down, "z", -1)
        units += [up, down]
        steps += [[(0, -step), (1, -step)], [(0, step), (1, step)]]
    units += [around(up[0:1], "z", 1), around(down[1:2], "z", -1)]
    steps += [[(0, 4)], [(1, 4)]]
    return units, steps


def shards(raw, taps):
    z = lax.axis_index("z")
    x = lax.axis_index("x")
    yh = lax.axis_index("yh")
    q = lax.axis_index(("yl", "core"))
    e = z % 2
    bins = raw.shape[1]
    everything = lax.all_gather(raw, ("yl", "core"), axis=0, tiled=False)
    place = [16 * q + 8 * e, 16 * q + 8 * (1 - e), q * bins, z, x, yh]
    place = jnp.stack(place).astype(jnp.int32)
    full, first, second, mine = run_filter(place, everything, taps.reshape(1, -1))
    one = spread(first, 0)
    two = spread(second, 1)
    unit_a = jnp.where(e == 0, one, two)[None]
    unit_b = jnp.where(e == 0, two, one)[None]
    units_a, steps_a = chain(unit_a)
    units_b, steps_b = chain(unit_b)
    row_y = cross_y(full)
    row_x = cross_x(full)
    row_xy = cross_x(row_y)
    lagged, energy = run_lags(full)
    rows = [*run_lags(row_y), *run_lags(row_x), *run_lags(row_xy)]
    quarters = []
    columns = []
    for units, steps in ((units_a, steps_a), (units_b, steps_b)):
        send_y, send_x, send_xy, *kept = run_partner(place, rows, units, steps)
        got_xy = sent(cross_xy, send_xy)
        quarters.append([sent(cross_y, send_y), sent(cross_x, send_x), got_xy])
        columns += kept
    own = run_own(lagged, energy, *columns)
    information = run_join(place, [part for k in range(2) for part in (own[k], *quarters[k])])
    return (information, mine)


def solution(mesh):
    fine = Mesh(mesh.devices.reshape(8, 4, 2, 2, 2), ("z", "x", "yh", "yl", "core"))
    rows, bins = ("z", "x", "yh"), ("yl", "core")
    return jax.shard_map(
        shards,
        mesh=fine,
        in_specs=(P(rows, bins), P()),
        out_specs=(P(None, rows, bins), P(rows, bins)),
        check_vma=False,
    )
```

```python
import jax
import jax.numpy as jnp
import numpy as np
from jax import lax
from jax.experimental import pallas as pl
from jax.experimental.pallas import tpu as pltpu
from jax.sharding import Mesh, PartitionSpec as P

LAGS = 9
REACH = 4
HALF = 32
NT = (((1,), (1,)), ((), ()))
MB = 1 << 20
SENT = jnp.float16
SCALE = 65536.0


def cut_kernel(place, raw, *outs):
    for k, out in enumerate(outs):
        at = pl.multiple_of(((place[0] + k) & 7) * 8, 8)
        out[...] = raw[pl.ds(at, 8), :]


def run_cut(place, raw):
    rows, bins = raw.shape
    vmem = pl.BlockSpec(memory_space=pltpu.VMEM)
    piece = jax.ShapeDtypeStruct((8, bins), raw.dtype)
    return pl.pallas_call(
        cut_kernel,
        in_specs=[pl.BlockSpec(memory_space=pltpu.SMEM), vmem],
        out_specs=[vmem] * (rows // 8),
        out_shape=[piece] * (rows // 8),
        compiler_params=pltpu.CompilerParams(vmem_limit_bytes=4 * MB),
        name="cut",
    )(place, raw)


def band(taps, line, weights):
    line[...] = jnp.zeros(line.shape, jnp.float32)
    line[0:1, 0 : taps.shape[1]] = taps[...]
    wide = jnp.broadcast_to(line[0:1, :], (128, 384))
    full = pltpu.roll(wide, 128 - HALF, axis=1, stride=1, stride_axis=0)
    high = full.astype(jnp.bfloat16)
    rest = full - high.astype(jnp.float32)
    middle = rest.astype(jnp.bfloat16)
    low = (rest - middle.astype(jnp.float32)).astype(jnp.bfloat16)
    weights[0:128] = high
    weights[128:256] = middle
    weights[256:384] = low


def filtered_blocks(window, weights):
    total = None
    for k in range(3):
        piece = window(k)
        piece = piece.reshape(piece.shape[0] * piece.shape[1], 128)
        term = lax.dot_general(
            piece, weights[:, k * 128 : (k + 1) * 128], NT, preferred_element_type=jnp.float32
        )
        total = term if total is None else total + term
    value = (total[:, 256:384] + total[:, 128:256]) + total[:, 0:128]
    return value.astype(jnp.bfloat16)


def piece_filter_kernel(place, taps, *refs):
    pieces = refs[:8]
    out, blocks, weights, line = refs[8:]
    per = pieces[0].shape[1] // 128
    count = 4 * per
    for e in range(2):
        blocks[e, 0] = jnp.zeros((8, 128), jnp.bfloat16)
        blocks[e, count + 1] = jnp.zeros((8, 128), jnp.bfloat16)
    for k, piece in enumerate(pieces):
        u = (place[1] - k) & 7
        for b in range(per):
            blocks[u >> 2, 1 + (u & 3) * per + b] = piece[:, b * 128 : (b + 1) * 128]
    band(taps, line, weights)
    for e in range(2):
        value = filtered_blocks(lambda k: blocks[e, k : k + count], weights)
        for n in range(count):
            out[e, :, n * 128 : (n + 1) * 128] = value[n * 8 : (n + 1) * 8]


def run_piece_filter(place, taps, pieces):
    bins = pieces[0].shape[1]
    vmem = pl.BlockSpec(memory_space=pltpu.VMEM)
    return pl.pallas_call(
        piece_filter_kernel,
        in_specs=[pl.BlockSpec(memory_space=pltpu.SMEM)] + [vmem] * 9,
        out_specs=vmem,
        out_shape=jax.ShapeDtypeStruct((2, 8, 4 * bins), jnp.bfloat16),
        scratch_shapes=[
            pltpu.VMEM((2, 4 * bins // 128 + 2, 8, 128), jnp.bfloat16),
            pltpu.VMEM((384, 384), jnp.bfloat16),
            pltpu.VMEM((8, 384), jnp.float32),
        ],
        compiler_params=pltpu.CompilerParams(vmem_limit_bytes=8 * MB),
        name="pieces",
    )(place, taps, *pieces)


def row_filter_kernel(place, taps, own, core, line_y, both, out, mine, blocks, weights, line):
    rows, bins = own.shape
    per = bins // 128
    count = 4 * per
    q = place[2]
    blocks[0] = jnp.zeros((rows, 128), jnp.bfloat16)
    blocks[count + 1] = jnp.zeros((rows, 128), jnp.bfloat16)
    for flip, part in enumerate((own, core, line_y, both)):
        for b in range(per):
            blocks[1 + (q ^ flip) * per + b] = part[:, b * 128 : (b + 1) * 128]
    band(taps, line, weights)
    group = 8
    for g in range(0, count, group):
        value = filtered_blocks(lambda k: blocks[g + k : g + k + group], weights)
        for b in range(group):
            n = g + b
            out[:, n * 128 : (n + 1) * 128] = value[b * rows : (b + 1) * rows]
    mine[...] = out[:, pl.ds(pl.multiple_of(q * bins, 128), bins)]


def run_row_filter(place, taps, parts):
    rows, bins = parts[0].shape
    vmem = pl.BlockSpec(memory_space=pltpu.VMEM)
    return pl.pallas_call(
        row_filter_kernel,
        in_specs=[pl.BlockSpec(memory_space=pltpu.SMEM)] + [vmem] * 5,
        out_specs=[vmem, vmem],
        out_shape=[
            jax.ShapeDtypeStruct((rows, 4 * bins), jnp.bfloat16),
            jax.ShapeDtypeStruct((rows, bins), jnp.bfloat16),
        ],
        scratch_shapes=[
            pltpu.VMEM((4 * bins // 128 + 2, rows, 128), jnp.bfloat16),
            pltpu.VMEM((384, 384), jnp.bfloat16),
            pltpu.VMEM((8, 384), jnp.float32),
        ],
        compiler_params=pltpu.CompilerParams(vmem_limit_bytes=8 * MB),
        cost_estimate=pl.CostEstimate(flops=1 << 30, bytes_accessed=4 * MB, transcendentals=0),
        name="rows",
    )(place, taps, *parts)


def lag_kernel(rows_ref, out, energy):
    bins = rows_ref.shape[1]
    at = lax.broadcasted_iota(jnp.int32, (16, bins), 1)
    for part in range(rows_ref.shape[0] // 16):
        span = slice(part * 16, (part + 1) * 16)
        value = rows_ref[span].astype(jnp.float32)
        total = jnp.sum(value * value, axis=1, keepdims=True)
        energy[span] = jnp.broadcast_to(total, (16, 128))
        for lag in range(LAGS):
            step = lag - REACH
            if step == 0:
                moved = value
            else:
                moved = pltpu.roll(value, step % bins, axis=1)
                inside = at >= step if step > 0 else at < bins + step
                moved = jnp.where(inside, moved, 0.0)
            out[lag, span] = moved.astype(jnp.bfloat16)


def run_lags(rows):
    count, bins = rows.shape
    vmem = pl.BlockSpec(memory_space=pltpu.VMEM)
    return pl.pallas_call(
        lag_kernel,
        in_specs=[vmem],
        out_specs=[vmem, vmem],
        out_shape=[
            jax.ShapeDtypeStruct((LAGS, count, bins), jnp.bfloat16),
            jax.ShapeDtypeStruct((count, 128), jnp.float32),
        ],
        compiler_params=pltpu.CompilerParams(vmem_limit_bytes=8 * MB),
        cost_estimate=pl.CostEstimate(flops=10 * MB, bytes_accessed=6 * MB, transcendentals=0),
        name="lags",
    )(rows)


def weigh(lagged, energy, right, across, emit):
    lags, count, bins = lagged.shape
    left = lagged[...].reshape(lags * count, bins)
    moments = lax.dot_general(left, right, NT, preferred_element_type=jnp.float32)
    norms = (1.0 / jnp.sqrt(energy[:, 0:1] + 1e-05)) * across
    for lag in range(lags):
        ratio = moments[lag * count : (lag + 1) * count] * norms
        emit(lag, -0.5 * jnp.log(1.0 - ratio * ratio))


def columns_kernel(steps, place, *refs):
    units = refs[: len(steps)]
    columns, scale = refs[len(steps) :]
    z = place[1]
    for ref, moves in zip(units, steps):
        for k, (part, z_step) in enumerate(moves):
            columns[part * 8 + ((z + z_step) & 7)] = ref[k]
    width = columns.shape[0] * columns.shape[1]
    for g in range(width // 128):
        block = columns[g * 16 : (g + 1) * 16].astype(jnp.float32).reshape(128, -1)
        total = jnp.sum(block * block, axis=1, keepdims=True)
        root = 0.8 / jnp.sqrt(total + 1e-05)
        root = jnp.transpose(jnp.broadcast_to(root, (128, 128)))
        scale[:, g * 128 : (g + 1) * 128] = root[0:8]


def run_columns(place, units, steps):
    slots = sum(len(moves) for moves in steps)
    bins = units[0].shape[2]

    def body(*refs):
        columns_kernel(steps, *refs)

    vmem = pl.BlockSpec(memory_space=pltpu.VMEM)
    return pl.pallas_call(
        body,
        in_specs=[pl.BlockSpec(memory_space=pltpu.SMEM)] + [vmem] * len(units),
        out_specs=[vmem, vmem],
        out_shape=[
            jax.ShapeDtypeStruct((slots, 8, bins), jnp.bfloat16),
            jax.ShapeDtypeStruct((8, slots * 8), jnp.float32),
        ],
        compiler_params=pltpu.CompilerParams(vmem_limit_bytes=8 * MB),
        cost_estimate=pl.CostEstimate(flops=8 * MB, bytes_accessed=4 * MB, transcendentals=0),
        name="columns",
    )(place, *units)


def weigh_kernel(factor, lagged, energy, columns, scale, out):
    lags, count, bins = lagged.shape
    left = lagged[...].reshape(lags * count, bins)
    right = columns[...].reshape(-1, bins)
    moments = lax.dot_general(left, right, NT, preferred_element_type=jnp.float32)
    norms = (1.0 / jnp.sqrt(energy[:, 0:1] + 1e-05)) * scale[0:1, :]
    for lag in range(lags):
        ratio = moments[lag * count : (lag + 1) * count] * norms
        value = -0.5 * jnp.log(1.0 - ratio * ratio)
        out[lag] = value if factor == 1 else value * factor


def run_weigh(rows, columns, scale, factor):
    lagged, energy = rows
    lags, count, bins = lagged.shape
    width = scale.shape[1]

    def body(*refs):
        weigh_kernel(factor, *refs)

    vmem = pl.BlockSpec(memory_space=pltpu.VMEM)
    return pl.pallas_call(
        body,
        in_specs=[vmem] * 4,
        out_specs=vmem,
        out_shape=jax.ShapeDtypeStruct((lags, count, width), jnp.float32),
        compiler_params=pltpu.CompilerParams(vmem_limit_bytes=8 * MB),
        cost_estimate=pl.CostEstimate(
            flops=2 * lags * count * width * bins,
            bytes_accessed=4 * lags * count * width,
            transcendentals=lags * count * width,
        ),
        name="weigh",
    )(lagged, energy, columns, scale)


def join_kernel(place, own, got_y, got_x, got_xy, out):
    low = place[4] == 0
    rows = out.shape[1]
    lane = lax.broadcasted_iota(jnp.int32, (rows, 128), 1) < 64
    for half in range(2):
        span = slice(half * 128, (half + 1) * 128)
        for flip, (same, cross) in enumerate(((own, got_y), (got_x, got_xy))):
            here_x = place[3] ^ flip
            for lag in range(out.shape[0]):
                here = same[lag, :, span] * (1.0 / SCALE) if flip else same[lag, :, span]
                there = cross[lag, :, span] * (1.0 / SCALE)
                one = jnp.where(low, here, there)
                two = jnp.where(low, there, here)
                at = pl.multiple_of((half * 4 + here_x) * 128, 128)
                out[lag, :, pl.ds(at, 128)] = jnp.where(lane, one, pltpu.roll(two, 64, axis=1))
                at = pl.multiple_of((half * 4 + (here_x ^ 2)) * 128, 128)
                out[lag, :, pl.ds(at, 128)] = jnp.where(lane, pltpu.roll(one, 64, axis=1), two)


def run_join(place, *quarters):
    lags, rows, width = quarters[0].shape
    spec = pl.BlockSpec((3, rows, width), lambda i: (i, 0, 0))
    return pl.pallas_call(
        join_kernel,
        grid=(lags // 3,),
        in_specs=[pl.BlockSpec(memory_space=pltpu.SMEM)] + [spec] * 4,
        out_specs=pl.BlockSpec((3, rows, 4 * width), lambda i: (i, 0, 0)),
        out_shape=jax.ShapeDtypeStruct((lags, rows, 4 * width), jnp.float32),
        compiler_params=pltpu.CompilerParams(vmem_limit_bytes=8 * MB),
        name="join",
    )(place, *quarters)


def around(value, axis, step):
    size = lax.axis_size(axis)
    return lax.ppermute(value, axis, [(i, (i + step) % size) for i in range(size)])


def cross_y(value):
    return lax.ppermute(value, "yh", [(0, 1), (1, 0)])


def cross_x(value):
    return lax.ppermute(value, "x", [(0, 1), (1, 0), (2, 3), (3, 2)])


def cross_xy(value):
    return lax.ppermute(value, ("x", "yh"), [(i, i ^ 3) for i in range(8)])


def sent(move, value):
    return move(value.astype(SENT)).astype(jnp.float32)


def spread(value, k):
    pairs = []
    for z in range(8):
        for q in range(4):
            pairs.append((z * 4 + q, ((4 * (z & 1) + q + k) & 7) * 4 + (z >> 1)))
    return lax.ppermute(value, ("z", "yl", "core"), pairs)


def flipped(value, flip):
    return lax.ppermute(value, ("yl", "core"), [(i, i ^ flip) for i in range(4)])


def after(value, *others):
    return lax.optimization_barrier((value, *others))[0]


def shards(raw, taps):
    z = lax.axis_index("z")
    x = lax.axis_index("x")
    yh = lax.axis_index("yh")
    q = lax.axis_index(("yl", "core"))
    place = jnp.stack([4 * (z % 2) + q, z, q, x, yh]).astype(jnp.int32)
    taps = taps.reshape(1, -1)
    pieces = [spread(piece, k) for k, piece in enumerate(run_cut(place, raw))]
    parts = [raw] + [flipped(raw, flip) for flip in (1, 2, 3)]
    unit = run_piece_filter(place, taps, pieces)
    base = jnp.concatenate([unit, around(unit, "x", 2)], axis=0)
    units, steps = [base], [[(0, 0), (2, 0), (1, 0), (3, 0)]]
    order = [part for part, _ in steps[0]]
    first = (around(base, "z", 1), around(base, "z", -1))
    second = (around(first[0], "z", 1), around(first[1], "z", -1))
    full, mine = run_row_filter(place, taps, [after(raw, unit)] + parts[1:])
    row_y = cross_y(full)
    row_x = cross_x(full)
    row_xy = cross_x(after(row_y, *first))
    own = run_lags(after(full, *first))
    ready = after(second, own)
    third = (around(ready[0], "z", 1), around(ready[1], "z", -1))
    far_y = run_lags(after(row_y, *second))
    ready = after(third, far_y)
    units += [*first, *second, *third, around(ready[0][0:2], "z", 1), around(ready[1][2:4], "z", -1)]
    for step in (1, 2, 3):
        steps += [[(part, -step) for part in order], [(part, step) for part in order]]
    steps += [[(part, 4) for part in order[0:2]], [(part, 4) for part in order[2:4]]]
    far_x = run_lags(after(row_x, *third))
    far_xy = run_lags(row_xy)
    columns, scale = run_columns(place, units, steps)
    got_xy = sent(cross_xy, run_weigh(far_xy, columns, scale, SCALE))
    got_x = sent(cross_x, run_weigh(far_x, columns, scale, SCALE))
    got_y = sent(cross_y, run_weigh(far_y, columns, scale, SCALE))
    information = run_join(place, run_weigh(own, columns, scale, 1), got_y, got_x, got_xy)
    return (information, mine)


def solution(mesh):
    fine = Mesh(mesh.devices.reshape(8, 4, 2, 2, 2), ("z", "x", "yh", "yl", "core"))
    rows, bins = ("z", "x", "yh"), ("yl", "core")
    return jax.shard_map(
        shards,
        mesh=fine,
        in_specs=(P(rows, bins), P()),
        out_specs=(P(None, rows, bins), P(rows, bins)),
        check_vma=False,
    )
```

```python
import jax
import jax.numpy as jnp
import numpy as np
from jax import lax
from jax.experimental import pallas as pl
from jax.experimental.pallas import tpu as pltpu
from jax.sharding import Mesh, PartitionSpec as P

LAGS = 9
REACH = 4
HALF = 32
NT = (((1,), (1,)), ((), ()))
MB = 1 << 20
SENT = jnp.float16
SCALE = 65536.0


def band(taps, line, weights):
    line[...] = jnp.zeros(line.shape, jnp.float32)
    line[0:1, 0 : taps.shape[1]] = taps[...]
    wide = jnp.broadcast_to(line[0:1, :], (128, 384))
    full = pltpu.roll(wide, 128 - HALF, axis=1, stride=1, stride_axis=0)
    high = full.astype(jnp.bfloat16)
    rest = full - high.astype(jnp.float32)
    middle = rest.astype(jnp.bfloat16)
    low = (rest - middle.astype(jnp.float32)).astype(jnp.bfloat16)
    weights[0:128] = high
    weights[128:256] = middle
    weights[256:384] = low


def filtered_blocks(window, weights):
    total = None
    for k in range(3):
        piece = window(k)
        piece = piece.reshape(piece.shape[0] * piece.shape[1], 128)
        term = lax.dot_general(
            piece, weights[:, k * 128 : (k + 1) * 128], NT, preferred_element_type=jnp.float32
        )
        total = term if total is None else total + term
    value = (total[:, 256:384] + total[:, 128:256]) + total[:, 0:128]
    return value.astype(jnp.bfloat16)


def piece_filter_kernel(place, taps, parts, out, blocks, weights, line):
    count, bins = parts.shape[0], parts.shape[2]
    per = bins // 128
    count = count * per
    at = pl.multiple_of(place[2] * 16, 16)
    blocks[0] = jnp.zeros((16, 128), jnp.bfloat16)
    blocks[count + 1] = jnp.zeros((16, 128), jnp.bfloat16)
    for n in range(count):
        b = n % per
        blocks[1 + n] = parts[n // per, pl.ds(at, 16), b * 128 : (b + 1) * 128]
    band(taps, line, weights)
    value = filtered_blocks(lambda k: blocks[k : k + count], weights)
    for n in range(count):
        for h in range(2):
            lo = n * 16 + h * 8
            out[h, :, n * 128 : (n + 1) * 128] = value[lo : lo + 8]


def run_piece_filter(place, taps, parts):
    count, _, bins = parts.shape
    vmem = pl.BlockSpec(memory_space=pltpu.VMEM)
    return pl.pallas_call(
        piece_filter_kernel,
        in_specs=[pl.BlockSpec(memory_space=pltpu.SMEM), vmem, vmem],
        out_specs=vmem,
        out_shape=jax.ShapeDtypeStruct((2, 8, count * bins), jnp.bfloat16),
        scratch_shapes=[
            pltpu.VMEM((count * bins // 128 + 2, 16, 128), jnp.bfloat16),
            pltpu.VMEM((384, 384), jnp.bfloat16),
            pltpu.VMEM((8, 384), jnp.float32),
        ],
        compiler_params=pltpu.CompilerParams(vmem_limit_bytes=8 * MB),
        name="pieces",
    )(place, taps, parts)


def row_filter_kernel(place, taps, parts, out, mine, blocks, weights, line):
    rows, bins = parts.shape[1:]
    per = bins // 128
    count = parts.shape[0] * per
    blocks[0] = jnp.zeros((rows, 128), jnp.bfloat16)
    blocks[count + 1] = jnp.zeros((rows, 128), jnp.bfloat16)
    for n in range(count):
        b = n % per
        blocks[1 + n] = parts[n // per, :, b * 128 : (b + 1) * 128]
    band(taps, line, weights)
    group = 8
    for g in range(0, count, group):
        value = filtered_blocks(lambda k: blocks[g + k : g + k + group], weights)
        for b in range(group):
            n = g + b
            out[:, n * 128 : (n + 1) * 128] = value[b * rows : (b + 1) * rows]
    mine[...] = out[:, pl.ds(pl.multiple_of(place[2] * bins, 128), bins)]


def run_row_filter(place, taps, parts):
    count, rows, bins = parts.shape
    vmem = pl.BlockSpec(memory_space=pltpu.VMEM)
    return pl.pallas_call(
        row_filter_kernel,
        in_specs=[pl.BlockSpec(memory_space=pltpu.SMEM), vmem, vmem],
        out_specs=[vmem, vmem],
        out_shape=[
            jax.ShapeDtypeStruct((rows, count * bins), jnp.bfloat16),
            jax.ShapeDtypeStruct((rows, bins), jnp.bfloat16),
        ],
        scratch_shapes=[
            pltpu.VMEM((count * bins // 128 + 2, rows, 128), jnp.bfloat16),
            pltpu.VMEM((384, 384), jnp.bfloat16),
            pltpu.VMEM((8, 384), jnp.float32),
        ],
        compiler_params=pltpu.CompilerParams(vmem_limit_bytes=8 * MB),
        cost_estimate=pl.CostEstimate(flops=1 << 30, bytes_accessed=4 * MB, transcendentals=0),
        name="rows",
    )(place, taps, parts)


def lag_kernel(rows_ref, out, energy):
    bins = rows_ref.shape[1]
    at = lax.broadcasted_iota(jnp.int32, (16, bins), 1)
    for part in range(rows_ref.shape[0] // 16):
        span = slice(part * 16, (part + 1) * 16)
        value = rows_ref[span].astype(jnp.float32)
        total = jnp.sum(value * value, axis=1, keepdims=True)
        energy[span] = jnp.broadcast_to(total, (16, 128))
        for lag in range(LAGS):
            step = lag - REACH
            if step == 0:
                moved = value
            else:
                moved = pltpu.roll(value, step % bins, axis=1)
                inside = at >= step if step > 0 else at < bins + step
                moved = jnp.where(inside, moved, 0.0)
            out[lag, span] = moved.astype(jnp.bfloat16)


def run_lags(rows):
    count, bins = rows.shape
    vmem = pl.BlockSpec(memory_space=pltpu.VMEM)
    return pl.pallas_call(
        lag_kernel,
        in_specs=[vmem],
        out_specs=[vmem, vmem],
        out_shape=[
            jax.ShapeDtypeStruct((LAGS, count, bins), jnp.bfloat16),
            jax.ShapeDtypeStruct((count, 128), jnp.float32),
        ],
        compiler_params=pltpu.CompilerParams(vmem_limit_bytes=8 * MB),
        cost_estimate=pl.CostEstimate(flops=10 * MB, bytes_accessed=6 * MB, transcendentals=0),
        name="lags",
    )(rows)


def weigh(lagged, energy, right, across, emit):
    lags, count, bins = lagged.shape
    left = lagged[...].reshape(lags * count, bins)
    moments = lax.dot_general(left, right, NT, preferred_element_type=jnp.float32)
    norms = (1.0 / jnp.sqrt(energy[:, 0:1] + 1e-05)) * across
    for lag in range(lags):
        ratio = moments[lag * count : (lag + 1) * count] * norms
        emit(lag, -0.5 * jnp.log(1.0 - ratio * ratio))


def columns_kernel(steps, place, *refs):
    units = refs[: len(steps)]
    columns, scale = refs[len(steps) :]
    z = place[1]
    for ref, moves in zip(units, steps):
        for k, (part, z_step) in enumerate(moves):
            far = (z + z_step) & 7
            columns[(far & 1) * 16 + (part >> 1) * 8 + (far >> 1) * 2 + (part & 1)] = ref[k]
    width = columns.shape[0] * columns.shape[1]
    for g in range(width // 128):
        block = columns[g * 16 : (g + 1) * 16].astype(jnp.float32).reshape(128, -1)
        total = jnp.sum(block * block, axis=1, keepdims=True)
        root = 0.8 / jnp.sqrt(total + 1e-05)
        root = jnp.transpose(jnp.broadcast_to(root, (128, 128)))
        scale[:, g * 128 : (g + 1) * 128] = root[0:8]


def run_columns(place, units, steps):
    slots = sum(len(moves) for moves in steps)
    bins = units[0].shape[2]

    def body(*refs):
        columns_kernel(steps, *refs)

    vmem = pl.BlockSpec(memory_space=pltpu.VMEM)
    return pl.pallas_call(
        body,
        in_specs=[pl.BlockSpec(memory_space=pltpu.SMEM)] + [vmem] * len(units),
        out_specs=[vmem, vmem],
        out_shape=[
            jax.ShapeDtypeStruct((slots, 8, bins), jnp.bfloat16),
            jax.ShapeDtypeStruct((8, slots * 8), jnp.float32),
        ],
        compiler_params=pltpu.CompilerParams(vmem_limit_bytes=8 * MB),
        cost_estimate=pl.CostEstimate(flops=8 * MB, bytes_accessed=4 * MB, transcendentals=0),
        name="columns",
    )(place, *units)


def weigh_kernel(factor, lagged, energy, columns, scale, out):
    lags, count, bins = lagged.shape
    left = lagged[...].reshape(lags * count, bins)
    right = columns[...].reshape(-1, bins)
    moments = lax.dot_general(left, right, NT, preferred_element_type=jnp.float32)
    norms = (1.0 / jnp.sqrt(energy[:, 0:1] + 1e-05)) * scale[0:1, :]
    for lag in range(lags):
        ratio = moments[lag * count : (lag + 1) * count] * norms
        value = -0.5 * jnp.log(1.0 - ratio * ratio)
        out[lag] = value if factor == 1 else value * factor


def run_weigh(rows, columns, scale, factor):
    lagged, energy = rows
    lags, count, bins = lagged.shape
    width = scale.shape[1]

    def body(*refs):
        weigh_kernel(factor, *refs)

    vmem = pl.BlockSpec(memory_space=pltpu.VMEM)
    return pl.pallas_call(
        body,
        in_specs=[vmem] * 4,
        out_specs=vmem,
        out_shape=jax.ShapeDtypeStruct((lags, count, width), jnp.float32),
        compiler_params=pltpu.CompilerParams(vmem_limit_bytes=8 * MB),
        cost_estimate=pl.CostEstimate(
            flops=2 * lags * count * width * bins,
            bytes_accessed=4 * lags * count * width,
            transcendentals=lags * count * width,
        ),
        name="weigh",
    )(lagged, energy, columns, scale)


def join_kernel(place, own, got_xy, got_x, got_y, out):
    low = place[4] == 0
    rows = out.shape[1]
    lag = pl.program_id(0)
    lane = lax.broadcasted_iota(jnp.int32, (rows, 128), 1) < 64
    for half in range(2):
        span = slice(half * 128, (half + 1) * 128)
        for flip, (same, cross) in enumerate(((own, got_y), (got_x, got_xy))):
            here_x = place[3] ^ flip
            here = same[lag, :, span] * (1.0 / SCALE) if flip else same[lag, :, span]
            there = cross[lag, :, span] * (1.0 / SCALE)
            one = jnp.where(low, here, there)
            two = jnp.where(low, there, here)
            at = pl.multiple_of((half * 4 + here_x) * 128, 128)
            out[0, :, pl.ds(at, 128)] = jnp.where(lane, one, pltpu.roll(two, 64, axis=1))
            at = pl.multiple_of((half * 4 + (here_x ^ 2)) * 128, 128)
            out[0, :, pl.ds(at, 128)] = jnp.where(lane, pltpu.roll(one, 64, axis=1), two)


def run_join(place, *quarters):
    lags, rows, width = quarters[0].shape
    vmem = pl.BlockSpec(memory_space=pltpu.VMEM)
    return pl.pallas_call(
        join_kernel,
        grid=(lags,),
        in_specs=[pl.BlockSpec(memory_space=pltpu.SMEM)] + [vmem] * 4,
        out_specs=pl.BlockSpec((1, rows, 4 * width), lambda i: (i, 0, 0)),
        out_shape=jax.ShapeDtypeStruct((lags, rows, 4 * width), jnp.float32),
        compiler_params=pltpu.CompilerParams(vmem_limit_bytes=8 * MB),
        name="join",
    )(place, *quarters)


def around(value, axis, step):
    size = lax.axis_size(axis)
    return lax.ppermute(value, axis, [(i, (i + step) % size) for i in range(size)])


def cross_y(value):
    return lax.ppermute(value, "yh", [(0, 1), (1, 0)])


def cross_x(value):
    return lax.ppermute(value, "x", [(0, 1), (1, 0), (2, 3), (3, 2)])


def cross_xy(value):
    return lax.ppermute(value, ("x", "yh"), [(i, i ^ 3) for i in range(8)])


def spread(value):
    pairs = []
    for z in range(8):
        for q in range(4):
            pairs.append((z * 4 + q, (2 * q + (z & 1)) * 4 + (z >> 1)))
    return lax.ppermute(value, ("z", "yl", "core"), pairs)


def after(value, *others):
    return lax.optimization_barrier((value, *others))[0]


def shards(raw, taps):
    z = lax.axis_index("z")
    x = lax.axis_index("x")
    yh = lax.axis_index("yh")
    q = lax.axis_index(("yl", "core"))
    place = jnp.stack([yh, z, q, x, yh]).astype(jnp.int32)
    taps = taps.reshape(1, -1)
    parts = lax.all_gather(raw, ("yl", "core"), axis=0, tiled=False)
    given = run_piece_filter(place, taps, parts)
    unit = spread(given)
    base = jnp.concatenate([unit, around(unit, "x", 2)], axis=0)
    order = (0, 1, 2, 3)
    units, steps = [base], [[(part, 0) for part in order]]
    first = (around(base, "z", 1), around(base, "z", -1))
    second = (around(first[0], "z", 1), around(first[1], "z", -1))
    full, mine = run_row_filter(place, taps, after(parts, given))
    row_y = cross_y(full)
    row_x = cross_x(full)
    row_xy = cross_x(after(row_y, *first))
    own = run_lags(after(full, *first))
    ready = after(second, own)
    third = (around(ready[0], "z", 1), around(ready[1], "z", -1))
    far_y = run_lags(after(row_y, *second))
    ready = after(third, far_y)
    units += [*first, *second, *third, around(ready[0][0:2], "z", 1), around(ready[1][2:4], "z", -1)]
    for step in (1, 2, 3):
        steps += [[(part, -step) for part in order], [(part, step) for part in order]]
    steps += [[(part, 4) for part in order[0:2]], [(part, 4) for part in order[2:4]]]
    far_x = run_lags(after(row_x, *third))
    far_xy = run_lags(row_xy)
    columns, scale = run_columns(place, units, steps)
    got = []
    for rows, move in ((far_xy, cross_xy), (far_x, cross_x), (far_y, cross_y)):
        send = run_weigh(rows, columns, scale, SCALE).astype(SENT)
        got.append(move(send).astype(jnp.float32))
    kept = run_weigh(own, columns, scale, 1)
    information = run_join(place, kept, *got)
    return (information, mine)


def solution(mesh):
    fine = Mesh(mesh.devices.reshape(8, 4, 2, 2, 2), ("z", "x", "yh", "yl", "core"))
    rows, bins = ("z", "x", "yh"), ("yl", "core")
    return jax.shard_map(
        shards,
        mesh=fine,
        in_specs=(P(rows, bins), P()),
        out_specs=(P(None, rows, bins), P(rows, bins)),
        check_vma=False,
    )
```

```python
import jax
import jax.numpy as jnp
import numpy as np
from jax import lax
from jax.experimental import pallas as pl
from jax.experimental.pallas import tpu as pltpu
from jax.sharding import Mesh, PartitionSpec as P

LAGS = 9
REACH = 4
HALF = 32
NT = (((1,), (1,)), ((), ()))
MB = 1 << 20
SENT = jnp.float16
SCALE = 65536.0


def band(taps, line, weights):
    line[...] = jnp.zeros(line.shape, jnp.float32)
    line[0:1, 0 : taps.shape[1]] = taps[...]
    wide = jnp.broadcast_to(line[0:1, :], (128, 384))
    full = pltpu.roll(wide, 128 - HALF, axis=1, stride=1, stride_axis=0)
    high = full.astype(jnp.bfloat16)
    rest = full - high.astype(jnp.float32)
    middle = rest.astype(jnp.bfloat16)
    low = (rest - middle.astype(jnp.float32)).astype(jnp.bfloat16)
    weights[0:128] = high
    weights[128:256] = middle
    weights[256:384] = low


def filtered_blocks(window, weights):
    total = None
    for k in range(3):
        piece = window(k)
        piece = piece.reshape(piece.shape[0] * piece.shape[1], 128)
        term = lax.dot_general(
            piece, weights[:, k * 128 : (k + 1) * 128], NT, preferred_element_type=jnp.float32
        )
        total = term if total is None else total + term
    value = (total[:, 256:384] + total[:, 128:256]) + total[:, 0:128]
    return value.astype(jnp.bfloat16)


def piece_filter_kernel(place, taps, parts, out, blocks, weights, line):
    count, bins = parts.shape[0], parts.shape[2]
    per = bins // 128
    count = count * per
    at = pl.multiple_of(place[2] * 16, 16)
    blocks[0] = jnp.zeros((16, 128), jnp.bfloat16)
    blocks[count + 1] = jnp.zeros((16, 128), jnp.bfloat16)
    for n in range(count):
        b = n % per
        blocks[1 + n] = parts[n // per, pl.ds(at, 16), b * 128 : (b + 1) * 128]
    band(taps, line, weights)
    value = filtered_blocks(lambda k: blocks[k : k + count], weights)
    for n in range(count):
        for h in range(2):
            lo = n * 16 + h * 8
            out[h, :, n * 128 : (n + 1) * 128] = value[lo : lo + 8]


def run_piece_filter(place, taps, parts):
    count, _, bins = parts.shape
    vmem = pl.BlockSpec(memory_space=pltpu.VMEM)
    return pl.pallas_call(
        piece_filter_kernel,
        in_specs=[pl.BlockSpec(memory_space=pltpu.SMEM), vmem, vmem],
        out_specs=vmem,
        out_shape=jax.ShapeDtypeStruct((2, 8, count * bins), jnp.bfloat16),
        scratch_shapes=[
            pltpu.VMEM((count * bins // 128 + 2, 16, 128), jnp.bfloat16),
            pltpu.VMEM((384, 384), jnp.bfloat16),
            pltpu.VMEM((8, 384), jnp.float32),
        ],
        compiler_params=pltpu.CompilerParams(vmem_limit_bytes=8 * MB),
        name="pieces",
    )(place, taps, parts)


def row_filter_kernel(place, taps, parts, out, mine, blocks, weights, line):
    rows, bins = parts.shape[1:]
    per = bins // 128
    count = parts.shape[0] * per
    blocks[0] = jnp.zeros((rows, 128), jnp.bfloat16)
    blocks[count + 1] = jnp.zeros((rows, 128), jnp.bfloat16)
    for n in range(count):
        b = n % per
        blocks[1 + n] = parts[n // per, :, b * 128 : (b + 1) * 128]
    band(taps, line, weights)
    group = 8
    for g in range(0, count, group):
        value = filtered_blocks(lambda k: blocks[g + k : g + k + group], weights)
        for b in range(group):
            n = g + b
            out[:, n * 128 : (n + 1) * 128] = value[b * rows : (b + 1) * rows]
    mine[...] = out[:, pl.ds(pl.multiple_of(place[2] * bins, 128), bins)]


def run_row_filter(place, taps, parts):
    count, rows, bins = parts.shape
    vmem = pl.BlockSpec(memory_space=pltpu.VMEM)
    return pl.pallas_call(
        row_filter_kernel,
        in_specs=[pl.BlockSpec(memory_space=pltpu.SMEM), vmem, vmem],
        out_specs=[vmem, vmem],
        out_shape=[
            jax.ShapeDtypeStruct((rows, count * bins), jnp.bfloat16),
            jax.ShapeDtypeStruct((rows, bins), jnp.bfloat16),
        ],
        scratch_shapes=[
            pltpu.VMEM((count * bins // 128 + 2, rows, 128), jnp.bfloat16),
            pltpu.VMEM((384, 384), jnp.bfloat16),
            pltpu.VMEM((8, 384), jnp.float32),
        ],
        compiler_params=pltpu.CompilerParams(vmem_limit_bytes=8 * MB),
        cost_estimate=pl.CostEstimate(flops=1 << 30, bytes_accessed=4 * MB, transcendentals=0),
        name="rows",
    )(place, taps, parts)


def lag_kernel(rows_ref, out, energy):
    bins = rows_ref.shape[1]
    at = lax.broadcasted_iota(jnp.int32, (16, bins), 1)
    for part in range(rows_ref.shape[0] // 16):
        span = slice(part * 16, (part + 1) * 16)
        value = rows_ref[span].astype(jnp.float32)
        total = jnp.sum(value * value, axis=1, keepdims=True)
        energy[span] = jnp.broadcast_to(total, (16, 128))
        for lag in range(LAGS):
            step = lag - REACH
            if step == 0:
                moved = value
            else:
                moved = pltpu.roll(value, step % bins, axis=1)
                inside = at >= step if step > 0 else at < bins + step
                moved = jnp.where(inside, moved, 0.0)
            out[lag, span] = moved.astype(jnp.bfloat16)


def run_lags(rows):
    count, bins = rows.shape
    vmem = pl.BlockSpec(memory_space=pltpu.VMEM)
    return pl.pallas_call(
        lag_kernel,
        in_specs=[vmem],
        out_specs=[vmem, vmem],
        out_shape=[
            jax.ShapeDtypeStruct((LAGS, count, bins), jnp.bfloat16),
            jax.ShapeDtypeStruct((count, 128), jnp.float32),
        ],
        compiler_params=pltpu.CompilerParams(vmem_limit_bytes=8 * MB),
        cost_estimate=pl.CostEstimate(flops=10 * MB, bytes_accessed=6 * MB, transcendentals=0),
        name="lags",
    )(rows)


def weigh(lagged, energy, right, across, emit):
    lags, count, bins = lagged.shape
    left = lagged[...].reshape(lags * count, bins)
    moments = lax.dot_general(left, right, NT, preferred_element_type=jnp.float32)
    norms = (1.0 / jnp.sqrt(energy[:, 0:1] + 1e-05)) * across
    for lag in range(lags):
        ratio = moments[lag * count : (lag + 1) * count] * norms
        emit(lag, -0.5 * jnp.log(1.0 - ratio * ratio))


def columns_kernel(steps, place, *refs):
    units = refs[: len(steps)]
    columns, scale = refs[len(steps) :]
    z = place[1]
    for ref, moves in zip(units, steps):
        for k, (part, z_step) in enumerate(moves):
            far = (z + z_step) & 7
            columns[(far & 1) * 16 + (part >> 1) * 8 + (far >> 1) * 2 + (part & 1)] = ref[k]
    width = columns.shape[0] * columns.shape[1]
    for g in range(width // 128):
        block = columns[g * 16 : (g + 1) * 16].astype(jnp.float32).reshape(128, -1)
        total = jnp.sum(block * block, axis=1, keepdims=True)
        root = 0.8 / jnp.sqrt(total + 1e-05)
        root = jnp.transpose(jnp.broadcast_to(root, (128, 128)))
        scale[:, g * 128 : (g + 1) * 128] = root[0:8]


def run_columns(place, units, steps):
    slots = sum(len(moves) for moves in steps)
    bins = units[0].shape[2]

    def body(*refs):
        columns_kernel(steps, *refs)

    vmem = pl.BlockSpec(memory_space=pltpu.VMEM)
    return pl.pallas_call(
        body,
        in_specs=[pl.BlockSpec(memory_space=pltpu.SMEM)] + [vmem] * len(units),
        out_specs=[vmem, vmem],
        out_shape=[
            jax.ShapeDtypeStruct((slots, 8, bins), jnp.bfloat16),
            jax.ShapeDtypeStruct((8, slots * 8), jnp.float32),
        ],
        compiler_params=pltpu.CompilerParams(vmem_limit_bytes=8 * MB),
        cost_estimate=pl.CostEstimate(flops=8 * MB, bytes_accessed=4 * MB, transcendentals=0),
        name="columns",
    )(place, *units)


def weigh_kernel(factor, lagged, energy, columns, scale, out):
    lags, count, bins = lagged.shape
    left = lagged[...].reshape(lags * count, bins)
    right = columns[...].reshape(-1, bins)
    moments = lax.dot_general(left, right, NT, preferred_element_type=jnp.float32)
    norms = (1.0 / jnp.sqrt(energy[:, 0:1] + 1e-05)) * scale[0:1, :]
    for lag in range(lags):
        ratio = moments[lag * count : (lag + 1) * count] * norms
        value = -0.5 * jnp.log(1.0 - ratio * ratio)
        out[lag] = value if factor == 1 else value * factor


def run_weigh(rows, columns, scale, factor):
    lagged, energy = rows
    lags, count, bins = lagged.shape
    width = scale.shape[1]

    def body(*refs):
        weigh_kernel(factor, *refs)

    vmem = pl.BlockSpec(memory_space=pltpu.VMEM)
    return pl.pallas_call(
        body,
        in_specs=[vmem] * 4,
        out_specs=vmem,
        out_shape=jax.ShapeDtypeStruct((lags, count, width), jnp.float32),
        compiler_params=pltpu.CompilerParams(vmem_limit_bytes=8 * MB),
        cost_estimate=pl.CostEstimate(
            flops=2 * lags * count * width * bins,
            bytes_accessed=4 * lags * count * width,
            transcendentals=lags * count * width,
        ),
        name="weigh",
    )(lagged, energy, columns, scale)


def join_kernel(place, own, got_xy, got_x, got_y, out, buffer, sems):
    low = place[4] == 0
    lags, rows = buffer.shape[:2]
    lane = lax.broadcasted_iota(jnp.int32, (rows, 128), 1) < 64
    copies = []
    for lag in range(lags):
        for half in range(2):
            span = slice(half * 128, (half + 1) * 128)
            for flip, (same, cross) in enumerate(((own, got_y), (got_x, got_xy))):
                here_x = place[3] ^ flip
                here = same[lag, :, span] * (1.0 / SCALE) if flip else same[lag, :, span]
                there = cross[lag, :, span] * (1.0 / SCALE)
                one = jnp.where(low, here, there)
                two = jnp.where(low, there, here)
                at = pl.multiple_of((half * 4 + here_x) * 128, 128)
                buffer[lag, :, pl.ds(at, 128)] = jnp.where(lane, one, pltpu.roll(two, 64, axis=1))
                at = pl.multiple_of((half * 4 + (here_x ^ 2)) * 128, 128)
                buffer[lag, :, pl.ds(at, 128)] = jnp.where(lane, pltpu.roll(one, 64, axis=1), two)
        copies.append(pltpu.make_async_copy(buffer.at[lag], out.at[lag], sems.at[lag]))
        copies[-1].start()
    for copy in copies:
        copy.wait()


def run_join(place, *quarters):
    lags, rows, width = quarters[0].shape
    vmem = pl.BlockSpec(memory_space=pltpu.VMEM)
    return pl.pallas_call(
        join_kernel,
        in_specs=[pl.BlockSpec(memory_space=pltpu.SMEM)] + [vmem] * 4,
        out_specs=pl.BlockSpec(memory_space=pltpu.HBM),
        out_shape=jax.ShapeDtypeStruct((lags, rows, 4 * width), jnp.float32),
        scratch_shapes=[
            pltpu.VMEM((lags, rows, 4 * width), jnp.float32),
            pltpu.SemaphoreType.DMA((lags,)),
        ],
        compiler_params=pltpu.CompilerParams(vmem_limit_bytes=8 * MB),
        name="join",
    )(place, *quarters)


def around(value, axis, step):
    size = lax.axis_size(axis)
    return lax.ppermute(value, axis, [(i, (i + step) % size) for i in range(size)])


def cross_y(value):
    return lax.ppermute(value, "yh", [(0, 1), (1, 0)])


def cross_x(value):
    return lax.ppermute(value, "x", [(0, 1), (1, 0), (2, 3), (3, 2)])


def cross_xy(value):
    return lax.ppermute(value, ("x", "yh"), [(i, i ^ 3) for i in range(8)])


def spread(value):
    pairs = []
    for z in range(8):
        for q in range(4):
            pairs.append((z * 4 + q, (2 * q + (z & 1)) * 4 + (z >> 1)))
    return lax.ppermute(value, ("z", "yl", "core"), pairs)


def after(value, *others):
    return lax.optimization_barrier((value, *others))[0]


def shards(raw, taps):
    z = lax.axis_index("z")
    x = lax.axis_index("x")
    yh = lax.axis_index("yh")
    q = lax.axis_index(("yl", "core"))
    place = jnp.stack([yh, z, q, x, yh]).astype(jnp.int32)
    taps = taps.reshape(1, -1)
    parts = lax.all_gather(raw, ("yl", "core"), axis=0, tiled=False)
    given = run_piece_filter(place, taps, parts)
    unit = spread(given)
    base = jnp.concatenate([unit, around(unit, "x", 2)], axis=0)
    order = (0, 1, 2, 3)
    units, steps = [base], [[(part, 0) for part in order]]
    first = (around(base, "z", 1), around(base, "z", -1))
    second = (around(first[0], "z", 1), around(first[1], "z", -1))
    full, mine = run_row_filter(place, taps, after(parts, given))
    row_y = cross_y(full)
    row_x = cross_x(full)
    row_xy = cross_x(after(row_y, *first))
    far_y = run_lags(after(row_y, *first))
    third = (around(after(second[0], far_y), "z", 1), around(after(second[1], far_y), "z", -1))
    far_x = run_lags(after(row_x, *second))
    ready = after(third[0], far_x), after(third[1], far_x)
    units += [*first, *second, *third, around(ready[0][0:2], "z", 1), around(ready[1][2:4], "z", -1)]
    for step in (1, 2, 3):
        steps += [[(part, -step) for part in order], [(part, step) for part in order]]
    steps += [[(part, 4) for part in order[0:2]], [(part, 4) for part in order[2:4]]]
    far_xy = run_lags(after(row_xy, *third))
    columns, scale = run_columns(place, units, steps)
    got = []
    for rows, move in ((far_xy, cross_xy), (far_x, cross_x), (far_y, cross_y)):
        came = move(run_weigh(rows, columns, scale, SCALE).astype(SENT))
        got.append(after(came, *got[-1:]).astype(jnp.float32))
    own = run_lags(after(full, scale))
    kept = run_weigh(own, columns, scale, 1)
    information = run_join(place, kept, *got)
    return (information, mine)


def solution(mesh):
    fine = Mesh(mesh.devices.reshape(8, 4, 2, 2, 2), ("z", "x", "yh", "yl", "core"))
    rows, bins = ("z", "x", "yh"), ("yl", "core")
    return jax.shard_map(
        shards,
        mesh=fine,
        in_specs=(P(rows, bins), P()),
        out_specs=(P(None, rows, bins), P(rows, bins)),
        check_vma=False,
    )
```

```python
import jax
import jax.numpy as jnp
import numpy as np
from jax import lax
from jax.experimental import pallas as pl
from jax.experimental.pallas import tpu as pltpu
from jax.sharding import Mesh, PartitionSpec as P

LAGS = 9
REACH = 4
HALF = 32
NT = (((1,), (1,)), ((), ()))
MB = 1 << 20
SENT = jnp.float16
SCALE = 65536.0


def band(taps, line, weights):
    line[...] = jnp.zeros(line.shape, jnp.float32)
    line[0:1, 0 : taps.shape[1]] = taps[...]
    wide = jnp.broadcast_to(line[0:1, :], (128, 384))
    full = pltpu.roll(wide, 128 - HALF, axis=1, stride=1, stride_axis=0)
    high = full.astype(jnp.bfloat16)
    rest = full - high.astype(jnp.float32)
    middle = rest.astype(jnp.bfloat16)
    low = (rest - middle.astype(jnp.float32)).astype(jnp.bfloat16)
    weights[0:128] = high
    weights[128:256] = middle
    weights[256:384] = low


def filtered_blocks(window, weights):
    total = None
    for k in range(3):
        piece = window(k)
        piece = piece.reshape(piece.shape[0] * piece.shape[1], 128)
        term = lax.dot_general(
            piece, weights[:, k * 128 : (k + 1) * 128], NT, preferred_element_type=jnp.float32
        )
        total = term if total is None else total + term
    value = (total[:, 256:384] + total[:, 128:256]) + total[:, 0:128]
    return value.astype(jnp.bfloat16)


def piece_filter_kernel(place, taps, parts, out, blocks, weights, line):
    count, bins = parts.shape[0], parts.shape[2]
    per = bins // 128
    count = count * per
    at = pl.multiple_of(place[2] * 16, 16)
    blocks[0] = jnp.zeros((16, 128), jnp.bfloat16)
    blocks[count + 1] = jnp.zeros((16, 128), jnp.bfloat16)
    for n in range(count):
        b = n % per
        blocks[1 + n] = parts[n // per, pl.ds(at, 16), b * 128 : (b + 1) * 128]
    band(taps, line, weights)
    value = filtered_blocks(lambda k: blocks[k : k + count], weights)
    for n in range(count):
        for h in range(2):
            lo = n * 16 + h * 8
            out[h, :, n * 128 : (n + 1) * 128] = value[lo : lo + 8]


def run_piece_filter(place, taps, parts):
    count, _, bins = parts.shape
    vmem = pl.BlockSpec(memory_space=pltpu.VMEM)
    return pl.pallas_call(
        piece_filter_kernel,
        in_specs=[pl.BlockSpec(memory_space=pltpu.SMEM), vmem, vmem],
        out_specs=vmem,
        out_shape=jax.ShapeDtypeStruct((2, 8, count * bins), jnp.bfloat16),
        scratch_shapes=[
            pltpu.VMEM((count * bins // 128 + 2, 16, 128), jnp.bfloat16),
            pltpu.VMEM((384, 384), jnp.bfloat16),
            pltpu.VMEM((8, 384), jnp.float32),
        ],
        compiler_params=pltpu.CompilerParams(vmem_limit_bytes=8 * MB),
        name="pieces",
    )(place, taps, parts)


def row_filter_kernel(place, taps, parts, out, mine, blocks, weights, line):
    rows, bins = parts.shape[1:]
    per = bins // 128
    count = parts.shape[0] * per
    blocks[0] = jnp.zeros((rows, 128), jnp.bfloat16)
    blocks[count + 1] = jnp.zeros((rows, 128), jnp.bfloat16)
    for n in range(count):
        b = n % per
        blocks[1 + n] = parts[n // per, :, b * 128 : (b + 1) * 128]
    band(taps, line, weights)
    group = 8
    for g in range(0, count, group):
        value = filtered_blocks(lambda k: blocks[g + k : g + k + group], weights)
        for b in range(group):
            n = g + b
            out[:, n * 128 : (n + 1) * 128] = value[b * rows : (b + 1) * rows]
    mine[...] = out[:, pl.ds(pl.multiple_of(place[2] * bins, 128), bins)]


def run_row_filter(place, taps, parts):
    count, rows, bins = parts.shape
    vmem = pl.BlockSpec(memory_space=pltpu.VMEM)
    return pl.pallas_call(
        row_filter_kernel,
        in_specs=[pl.BlockSpec(memory_space=pltpu.SMEM), vmem, vmem],
        out_specs=[vmem, vmem],
        out_shape=[
            jax.ShapeDtypeStruct((rows, count * bins), jnp.bfloat16),
            jax.ShapeDtypeStruct((rows, bins), jnp.bfloat16),
        ],
        scratch_shapes=[
            pltpu.VMEM((count * bins // 128 + 2, rows, 128), jnp.bfloat16),
            pltpu.VMEM((384, 384), jnp.bfloat16),
            pltpu.VMEM((8, 384), jnp.float32),
        ],
        compiler_params=pltpu.CompilerParams(vmem_limit_bytes=8 * MB),
        cost_estimate=pl.CostEstimate(flops=1 << 30, bytes_accessed=4 * MB, transcendentals=0),
        name="rows",
    )(place, taps, parts)


def lag_kernel(rows_ref, out, energy):
    bins = rows_ref.shape[1]
    at = lax.broadcasted_iota(jnp.int32, (16, bins), 1)
    for part in range(rows_ref.shape[0] // 16):
        span = slice(part * 16, (part + 1) * 16)
        value = rows_ref[span].astype(jnp.float32)
        total = jnp.sum(value * value, axis=1, keepdims=True)
        energy[span] = jnp.broadcast_to(total, (16, 128))
        for lag in range(LAGS):
            step = lag - REACH
            if step == 0:
                moved = value
            else:
                moved = pltpu.roll(value, step % bins, axis=1)
                inside = at >= step if step > 0 else at < bins + step
                moved = jnp.where(inside, moved, 0.0)
            out[lag, span] = moved.astype(jnp.bfloat16)


def run_lags(rows):
    count, bins = rows.shape
    vmem = pl.BlockSpec(memory_space=pltpu.VMEM)
    return pl.pallas_call(
        lag_kernel,
        in_specs=[vmem],
        out_specs=[vmem, vmem],
        out_shape=[
            jax.ShapeDtypeStruct((LAGS, count, bins), jnp.bfloat16),
            jax.ShapeDtypeStruct((count, 128), jnp.float32),
        ],
        compiler_params=pltpu.CompilerParams(vmem_limit_bytes=8 * MB),
        cost_estimate=pl.CostEstimate(flops=10 * MB, bytes_accessed=6 * MB, transcendentals=0),
        name="lags",
    )(rows)


def weigh(lagged, energy, right, across, emit):
    lags, count, bins = lagged.shape
    left = lagged[...].reshape(lags * count, bins)
    moments = lax.dot_general(left, right, NT, preferred_element_type=jnp.float32)
    norms = (1.0 / jnp.sqrt(energy[:, 0:1] + 1e-05)) * across
    for lag in range(lags):
        ratio = moments[lag * count : (lag + 1) * count] * norms
        emit(lag, -0.5 * jnp.log(1.0 - ratio * ratio))


def columns_kernel(steps, place, *refs):
    units = refs[: len(steps)]
    columns, scale = refs[len(steps) :]
    z = place[1]
    for ref, moves in zip(units, steps):
        for k, (part, z_step) in enumerate(moves):
            far = (z + z_step) & 7
            columns[(far & 1) * 16 + (part >> 1) * 8 + (far >> 1) * 2 + (part & 1)] = ref[k]
    width = columns.shape[0] * columns.shape[1]
    for g in range(width // 128):
        block = columns[g * 16 : (g + 1) * 16].astype(jnp.float32).reshape(128, -1)
        total = jnp.sum(block * block, axis=1, keepdims=True)
        root = 0.8 / jnp.sqrt(total + 1e-05)
        root = jnp.transpose(jnp.broadcast_to(root, (128, 128)))
        scale[:, g * 128 : (g + 1) * 128] = root[0:8]


def run_columns(place, units, steps):
    slots = sum(len(moves) for moves in steps)
    bins = units[0].shape[2]

    def body(*refs):
        columns_kernel(steps, *refs)

    vmem = pl.BlockSpec(memory_space=pltpu.VMEM)
    return pl.pallas_call(
        body,
        in_specs=[pl.BlockSpec(memory_space=pltpu.SMEM)] + [vmem] * len(units),
        out_specs=[vmem, vmem],
        out_shape=[
            jax.ShapeDtypeStruct((slots, 8, bins), jnp.bfloat16),
            jax.ShapeDtypeStruct((8, slots * 8), jnp.float32),
        ],
        compiler_params=pltpu.CompilerParams(vmem_limit_bytes=8 * MB),
        cost_estimate=pl.CostEstimate(flops=8 * MB, bytes_accessed=4 * MB, transcendentals=0),
        name="columns",
    )(place, *units)


def weigh_kernel(factor, lagged, energy, columns, scale, out):
    lags, count, bins = lagged.shape
    left = lagged[...].reshape(lags * count, bins)
    right = columns[...].reshape(-1, bins)
    moments = lax.dot_general(left, right, NT, preferred_element_type=jnp.float32)
    norms = (1.0 / jnp.sqrt(energy[:, 0:1] + 1e-05)) * scale[0:1, :]
    for lag in range(lags):
        ratio = moments[lag * count : (lag + 1) * count] * norms
        value = -0.5 * jnp.log(1.0 - ratio * ratio)
        out[lag] = value if factor == 1 else value * factor


def run_weigh(rows, columns, scale, factor):
    lagged, energy = rows
    lags, count, bins = lagged.shape
    width = scale.shape[1]

    def body(*refs):
        weigh_kernel(factor, *refs)

    vmem = pl.BlockSpec(memory_space=pltpu.VMEM)
    return pl.pallas_call(
        body,
        in_specs=[vmem] * 4,
        out_specs=vmem,
        out_shape=jax.ShapeDtypeStruct((lags, count, width), jnp.float32),
        compiler_params=pltpu.CompilerParams(vmem_limit_bytes=8 * MB),
        cost_estimate=pl.CostEstimate(
            flops=2 * lags * count * width * bins,
            bytes_accessed=4 * lags * count * width,
            transcendentals=lags * count * width,
        ),
        name="weigh",
    )(lagged, energy, columns, scale)


def join_kernel(place, own, got_x, got_xy, got_y, out, buffer, sems):
    low = place[4] == 0
    lags, rows = buffer.shape[:2]
    lane = lax.broadcasted_iota(jnp.int32, (rows, 128), 1) < 64
    copies = []
    for lag in range(lags):
        for half in range(2):
            span = slice(half * 128, (half + 1) * 128)
            for flip, (same, cross) in enumerate(((own, got_y), (got_x, got_xy))):
                here_x = place[3] ^ flip
                here = same[lag, :, span] * (1.0 / SCALE) if flip else same[lag, :, span]
                there = cross[lag, :, span] * (1.0 / SCALE)
                one = jnp.where(low, here, there)
                two = jnp.where(low, there, here)
                at = pl.multiple_of((half * 4 + here_x) * 128, 128)
                buffer[lag, :, pl.ds(at, 128)] = jnp.where(lane, one, pltpu.roll(two, 64, axis=1))
                at = pl.multiple_of((half * 4 + (here_x ^ 2)) * 128, 128)
                buffer[lag, :, pl.ds(at, 128)] = jnp.where(lane, pltpu.roll(one, 64, axis=1), two)
        copies.append(pltpu.make_async_copy(buffer.at[lag], out.at[lag], sems.at[lag]))
        copies[-1].start()
    for copy in copies:
        copy.wait()


def run_join(place, *quarters):
    lags, rows, width = quarters[0].shape
    vmem = pl.BlockSpec(memory_space=pltpu.VMEM)
    return pl.pallas_call(
        join_kernel,
        in_specs=[pl.BlockSpec(memory_space=pltpu.SMEM)] + [vmem] * 4,
        out_specs=pl.BlockSpec(memory_space=pltpu.HBM),
        out_shape=jax.ShapeDtypeStruct((lags, rows, 4 * width), jnp.float32),
        scratch_shapes=[
            pltpu.VMEM((lags, rows, 4 * width), jnp.float32),
            pltpu.SemaphoreType.DMA((lags,)),
        ],
        compiler_params=pltpu.CompilerParams(vmem_limit_bytes=8 * MB),
        name="join",
    )(place, *quarters)


def around(value, axis, step):
    size = lax.axis_size(axis)
    return lax.ppermute(value, axis, [(i, (i + step) % size) for i in range(size)])


def cross_y(value):
    return lax.ppermute(value, "yh", [(0, 1), (1, 0)])


def cross_x(value):
    return lax.ppermute(value, "x", [(0, 1), (1, 0), (2, 3), (3, 2)])


def cross_xy(value):
    return lax.ppermute(value, ("x", "yh"), [(i, i ^ 3) for i in range(8)])


def spread(value, across):
    pairs = []
    for z in range(8):
        for x in range(4):
            for q in range(4):
                source = (z * 4 + x) * 4 + q
                pairs.append((source, ((2 * q + (z & 1)) * 4 + (x ^ across)) * 4 + (z >> 1)))
    return lax.ppermute(value, ("z", "x", "yl", "core"), pairs)


def after(value, *others):
    return lax.optimization_barrier((value, *others))[0]


def shards(raw, taps):
    z = lax.axis_index("z")
    x = lax.axis_index("x")
    yh = lax.axis_index("yh")
    q = lax.axis_index(("yl", "core"))
    place = jnp.stack([yh, z, q, x, yh]).astype(jnp.int32)
    taps = taps.reshape(1, -1)
    parts = lax.all_gather(raw, ("yl", "core"), axis=0, tiled=False)
    given = run_piece_filter(place, taps, parts)
    base = jnp.concatenate([spread(given, 0), spread(given, 2)], axis=0)
    order = (0, 1, 2, 3)
    units, steps = [base], [[(part, 0) for part in order]]
    first = (around(base, "z", 1), around(base, "z", -1))
    second = (around(first[0], "z", 1), around(first[1], "z", -1))
    full, mine = run_row_filter(place, taps, after(parts, given))
    row_y = cross_y(full)
    row_x = cross_x(full)
    row_xy = cross_x(after(row_y, *first))
    far_y = run_lags(after(row_y, *first))
    third = (around(after(second[0], far_y), "z", 1), around(after(second[1], far_y), "z", -1))
    far_x = run_lags(after(row_x, *second))
    ready = after(third[0], far_x), after(third[1], far_x)
    units += [*first, *second, *third, around(ready[0][0:2], "z", 1), around(ready[1][2:4], "z", -1)]
    for step in (1, 2, 3):
        steps += [[(part, -step) for part in order], [(part, step) for part in order]]
    steps += [[(part, 4) for part in order[0:2]], [(part, 4) for part in order[2:4]]]
    far_xy = run_lags(after(row_xy, *third))
    columns, scale = run_columns(after(place, far_xy), units, steps)
    send_xy = run_weigh(far_xy, columns, scale, SCALE).astype(SENT)
    send_x = run_weigh(far_x, columns, after(scale, send_xy), SCALE).astype(SENT)
    send_y = run_weigh(far_y, columns, scale, SCALE).astype(SENT)
    came_xy = cross_xy(send_xy)
    came_x = cross_x(send_x)
    came_y = cross_y(send_y)
    got_xy = came_xy.astype(jnp.float32)
    got_x = after(came_x, got_xy).astype(jnp.float32)
    got_y = after(came_y, got_x).astype(jnp.float32)
    own = run_lags(after(full, scale))
    kept = run_weigh(own, columns, scale, 1)
    information = run_join(place, kept, got_x, got_xy, got_y)
    return (information, mine)


def solution(mesh):
    fine = Mesh(mesh.devices.reshape(8, 4, 2, 2, 2), ("z", "x", "yh", "yl", "core"))
    rows, bins = ("z", "x", "yh"), ("yl", "core")
    return jax.shard_map(
        shards,
        mesh=fine,
        in_specs=(P(rows, bins), P()),
        out_specs=(P(None, rows, bins), P(rows, bins)),
        check_vma=False,
    )
```

```python
import jax
import jax.numpy as jnp
import numpy as np
from jax import lax
from jax.experimental import pallas as pl
from jax.experimental.pallas import tpu as pltpu
from jax.sharding import Mesh, PartitionSpec as P

LAGS = 9
REACH = 4
HALF = 32
NT = (((1,), (1,)), ((), ()))
MB = 1 << 20
SENT = jnp.float16
SCALE = 65536.0


def band(taps, line, weights):
    line[...] = jnp.zeros(line.shape, jnp.float32)
    line[0:1, 0 : taps.shape[1]] = taps[...]
    wide = jnp.broadcast_to(line[0:1, :], (128, 384))
    full = pltpu.roll(wide, 128 - HALF, axis=1, stride=1, stride_axis=0)
    high = full.astype(jnp.bfloat16)
    rest = full - high.astype(jnp.float32)
    middle = rest.astype(jnp.bfloat16)
    low = (rest - middle.astype(jnp.float32)).astype(jnp.bfloat16)
    weights[0:128] = high
    weights[128:256] = middle
    weights[256:384] = low


def filtered_blocks(window, weights):
    total = None
    for k in range(3):
        piece = window(k)
        piece = piece.reshape(piece.shape[0] * piece.shape[1], 128)
        term = lax.dot_general(
            piece, weights[:, k * 128 : (k + 1) * 128], NT, preferred_element_type=jnp.float32
        )
        total = term if total is None else total + term
    value = (total[:, 256:384] + total[:, 128:256]) + total[:, 0:128]
    return value.astype(jnp.bfloat16)


def piece_filter_kernel(place, taps, parts, out, blocks, weights, line):
    count, bins = parts.shape[0], parts.shape[2]
    per = bins // 128
    count = count * per
    at = pl.multiple_of(place[2] * 16, 16)
    blocks[0] = jnp.zeros((16, 128), jnp.bfloat16)
    blocks[count + 1] = jnp.zeros((16, 128), jnp.bfloat16)
    for n in range(count):
        b = n % per
        blocks[1 + n] = parts[n // per, pl.ds(at, 16), b * 128 : (b + 1) * 128]
    band(taps, line, weights)
    value = filtered_blocks(lambda k: blocks[k : k + count], weights)
    for n in range(count):
        for h in range(2):
            lo = n * 16 + h * 8
            out[h, :, n * 128 : (n + 1) * 128] = value[lo : lo + 8]


def run_piece_filter(place, taps, parts):
    count, _, bins = parts.shape
    vmem = pl.BlockSpec(memory_space=pltpu.VMEM)
    return pl.pallas_call(
        piece_filter_kernel,
        in_specs=[pl.BlockSpec(memory_space=pltpu.SMEM), vmem, vmem],
        out_specs=vmem,
        out_shape=jax.ShapeDtypeStruct((2, 8, count * bins), jnp.bfloat16),
        scratch_shapes=[
            pltpu.VMEM((count * bins // 128 + 2, 16, 128), jnp.bfloat16),
            pltpu.VMEM((384, 384), jnp.bfloat16),
            pltpu.VMEM((8, 384), jnp.float32),
        ],
        compiler_params=pltpu.CompilerParams(vmem_limit_bytes=8 * MB),
        name="pieces",
    )(place, taps, parts)


def row_filter_kernel(place, taps, parts, out, mine, blocks, weights, line):
    rows, bins = parts.shape[1:]
    per = bins // 128
    count = parts.shape[0] * per
    blocks[0] = jnp.zeros((rows, 128), jnp.bfloat16)
    blocks[count + 1] = jnp.zeros((rows, 128), jnp.bfloat16)
    for n in range(count):
        b = n % per
        blocks[1 + n] = parts[n // per, :, b * 128 : (b + 1) * 128]
    band(taps, line, weights)
    group = 8
    for g in range(0, count, group):
        value = filtered_blocks(lambda k: blocks[g + k : g + k + group], weights)
        for b in range(group):
            n = g + b
            out[:, n * 128 : (n + 1) * 128] = value[b * rows : (b + 1) * rows]
    mine[...] = out[:, pl.ds(pl.multiple_of(place[2] * bins, 128), bins)]


def run_row_filter(place, taps, parts):
    count, rows, bins = parts.shape
    vmem = pl.BlockSpec(memory_space=pltpu.VMEM)
    return pl.pallas_call(
        row_filter_kernel,
        in_specs=[pl.BlockSpec(memory_space=pltpu.SMEM), vmem, vmem],
        out_specs=[vmem, vmem],
        out_shape=[
            jax.ShapeDtypeStruct((rows, count * bins), jnp.bfloat16),
            jax.ShapeDtypeStruct((rows, bins), jnp.bfloat16),
        ],
        scratch_shapes=[
            pltpu.VMEM((count * bins // 128 + 2, rows, 128), jnp.bfloat16),
            pltpu.VMEM((384, 384), jnp.bfloat16),
            pltpu.VMEM((8, 384), jnp.float32),
        ],
        compiler_params=pltpu.CompilerParams(vmem_limit_bytes=8 * MB),
        cost_estimate=pl.CostEstimate(flops=1 << 30, bytes_accessed=4 * MB, transcendentals=0),
        name="rows",
    )(place, taps, parts)


def lag_kernel(rows_ref, out, energy):
    bins = rows_ref.shape[1]
    at = lax.broadcasted_iota(jnp.int32, (16, bins), 1)
    for part in range(rows_ref.shape[0] // 16):
        span = slice(part * 16, (part + 1) * 16)
        value = rows_ref[span].astype(jnp.float32)
        total = jnp.sum(value * value, axis=1, keepdims=True)
        energy[span] = jnp.broadcast_to(total, (16, 128))
        for lag in range(LAGS):
            step = lag - REACH
            if step == 0:
                moved = value
            else:
                moved = pltpu.roll(value, step % bins, axis=1)
                inside = at >= step if step > 0 else at < bins + step
                moved = jnp.where(inside, moved, 0.0)
            out[lag, span] = moved.astype(jnp.bfloat16)


def run_lags(rows):
    count, bins = rows.shape
    vmem = pl.BlockSpec(memory_space=pltpu.VMEM)
    return pl.pallas_call(
        lag_kernel,
        in_specs=[vmem],
        out_specs=[vmem, vmem],
        out_shape=[
            jax.ShapeDtypeStruct((LAGS, count, bins), jnp.bfloat16),
            jax.ShapeDtypeStruct((count, 128), jnp.float32),
        ],
        compiler_params=pltpu.CompilerParams(vmem_limit_bytes=8 * MB),
        cost_estimate=pl.CostEstimate(flops=10 * MB, bytes_accessed=6 * MB, transcendentals=0),
        name="lags",
    )(rows)


def weigh(lagged, energy, right, across, emit):
    lags, count, bins = lagged.shape
    left = lagged[...].reshape(lags * count, bins)
    moments = lax.dot_general(left, right, NT, preferred_element_type=jnp.float32)
    norms = (1.0 / jnp.sqrt(energy[:, 0:1] + 1e-05)) * across
    for lag in range(lags):
        ratio = moments[lag * count : (lag + 1) * count] * norms
        emit(lag, -0.5 * jnp.log(1.0 - ratio * ratio))


def columns_kernel(steps, place, *refs):
    units = refs[: len(steps)]
    columns, scale = refs[len(steps) :]
    z = place[1]
    slab = place[2]
    for ref, moves in zip(units, steps):
        for k, (part, z_step) in enumerate(moves):
            up = (z + z_step - 2 * slab - 1) & 7
            e = (up < 4).astype(jnp.int32)
            giver = (3 - jnp.where(up < 4, up, 7 - up)) ^ slab
            columns[e * 16 + (part >> 1) * 8 + giver * 2 + (part & 1)] = ref[k]
    width = columns.shape[0] * columns.shape[1]
    for g in range(width // 128):
        block = columns[g * 16 : (g + 1) * 16].astype(jnp.float32).reshape(128, -1)
        total = jnp.sum(block * block, axis=1, keepdims=True)
        root = 0.8 / jnp.sqrt(total + 1e-05)
        root = jnp.transpose(jnp.broadcast_to(root, (128, 128)))
        scale[:, g * 128 : (g + 1) * 128] = root[0:8]


def run_columns(place, units, steps):
    slots = sum(len(moves) for moves in steps)
    bins = units[0].shape[2]

    def body(*refs):
        columns_kernel(steps, *refs)

    vmem = pl.BlockSpec(memory_space=pltpu.VMEM)
    return pl.pallas_call(
        body,
        in_specs=[pl.BlockSpec(memory_space=pltpu.SMEM)] + [vmem] * len(units),
        out_specs=[vmem, vmem],
        out_shape=[
            jax.ShapeDtypeStruct((slots, 8, bins), jnp.bfloat16),
            jax.ShapeDtypeStruct((8, slots * 8), jnp.float32),
        ],
        compiler_params=pltpu.CompilerParams(vmem_limit_bytes=8 * MB),
        cost_estimate=pl.CostEstimate(flops=8 * MB, bytes_accessed=4 * MB, transcendentals=0),
        name="columns",
    )(place, *units)


def weigh_kernel(factor, lagged, energy, columns, scale, out):
    lags, count, bins = lagged.shape
    left = lagged[...].reshape(lags * count, bins)
    right = columns[...].reshape(-1, bins)
    moments = lax.dot_general(left, right, NT, preferred_element_type=jnp.float32)
    norms = (1.0 / jnp.sqrt(energy[:, 0:1] + 1e-05)) * scale[0:1, :]
    for lag in range(lags):
        ratio = moments[lag * count : (lag + 1) * count] * norms
        value = -0.5 * jnp.log(1.0 - ratio * ratio)
        out[lag] = value if factor == 1 else value * factor


def run_weigh(rows, columns, scale, factor):
    lagged, energy = rows
    lags, count, bins = lagged.shape
    width = scale.shape[1]

    def body(*refs):
        weigh_kernel(factor, *refs)

    vmem = pl.BlockSpec(memory_space=pltpu.VMEM)
    return pl.pallas_call(
        body,
        in_specs=[vmem] * 4,
        out_specs=vmem,
        out_shape=jax.ShapeDtypeStruct((lags, count, width), jnp.float32),
        compiler_params=pltpu.CompilerParams(vmem_limit_bytes=8 * MB),
        cost_estimate=pl.CostEstimate(
            flops=2 * lags * count * width * bins,
            bytes_accessed=4 * lags * count * width,
            transcendentals=lags * count * width,
        ),
        name="weigh",
    )(lagged, energy, columns, scale)


def join_kernel(place, own, got_x, got_xy, got_y, out, buffer, sems):
    low = place[4] == 0
    lags, rows = buffer.shape[:2]
    lane = lax.broadcasted_iota(jnp.int32, (rows, 128), 1) < 64
    copies = []
    for lag in range(lags):
        for half in range(2):
            span = slice(half * 128, (half + 1) * 128)
            for flip, (same, cross) in enumerate(((own, got_y), (got_x, got_xy))):
                here_x = place[3] ^ flip
                here = same[lag, :, span] * (1.0 / SCALE) if flip else same[lag, :, span]
                there = cross[lag, :, span] * (1.0 / SCALE)
                one = jnp.where(low, here, there)
                two = jnp.where(low, there, here)
                at = pl.multiple_of((half * 4 + here_x) * 128, 128)
                buffer[lag, :, pl.ds(at, 128)] = jnp.where(lane, one, pltpu.roll(two, 64, axis=1))
                at = pl.multiple_of((half * 4 + (here_x ^ 2)) * 128, 128)
                buffer[lag, :, pl.ds(at, 128)] = jnp.where(lane, pltpu.roll(one, 64, axis=1), two)
        copies.append(pltpu.make_async_copy(buffer.at[lag], out.at[lag], sems.at[lag]))
        copies[-1].start()
    for copy in copies:
        copy.wait()


def run_join(place, *quarters):
    lags, rows, width = quarters[0].shape
    vmem = pl.BlockSpec(memory_space=pltpu.VMEM)
    return pl.pallas_call(
        join_kernel,
        in_specs=[pl.BlockSpec(memory_space=pltpu.SMEM)] + [vmem] * 4,
        out_specs=pl.BlockSpec(memory_space=pltpu.HBM),
        out_shape=jax.ShapeDtypeStruct((lags, rows, 4 * width), jnp.float32),
        scratch_shapes=[
            pltpu.VMEM((lags, rows, 4 * width), jnp.float32),
            pltpu.SemaphoreType.DMA((lags,)),
        ],
        compiler_params=pltpu.CompilerParams(vmem_limit_bytes=8 * MB),
        name="join",
    )(place, *quarters)


def around(value, axis, step):
    size = lax.axis_size(axis)
    return lax.ppermute(value, axis, [(i, (i + step) % size) for i in range(size)])


def cross_y(value):
    return lax.ppermute(value, "yh", [(0, 1), (1, 0)])


def cross_x(value):
    return lax.ppermute(value, "x", [(0, 1), (1, 0), (2, 3), (3, 2)])


def cross_xy(value):
    return lax.ppermute(value, ("x", "yh"), [(i, i ^ 3) for i in range(8)])


def spread(value, across):
    pairs = []
    for z in range(8):
        a, e = z >> 1, z & 1
        for x in range(4):
            for q in range(4):
                far = 3 - (q ^ a)
                to = (z + far if e else z - far) % 8
                pairs.append(((z * 4 + x) * 4 + q, (to * 4 + (x ^ across)) * 4 + a))
    return lax.ppermute(value, ("z", "x", "yl", "core"), pairs)


def after(value, *others):
    return lax.optimization_barrier((value, *others))[0]


def shards(raw, taps):
    z = lax.axis_index("z")
    x = lax.axis_index("x")
    yh = lax.axis_index("yh")
    q = lax.axis_index(("yl", "core"))
    place = jnp.stack([yh, z, q, x, yh]).astype(jnp.int32)
    taps = taps.reshape(1, -1)
    parts = lax.all_gather(raw, ("yl", "core"), axis=0, tiled=False)
    given = run_piece_filter(place, taps, parts)
    base = jnp.concatenate([spread(given, 0), spread(given, 2)], axis=0)
    order = (0, 1, 2, 3)
    units, steps = [base], [[(part, 0) for part in order]]
    first = (around(base, "z", 1), around(base, "z", -1))
    second = (around(first[0], "z", 1), around(first[1], "z", -1))
    full, mine = run_row_filter(place, taps, after(parts, given))
    row_y = cross_y(full)
    row_x = cross_x(full)
    row_xy = cross_x(after(row_y, *first))
    far_y = run_lags(after(row_y, *first))
    third = (around(after(second[0], far_y), "z", 1), around(after(second[1], far_y), "z", -1))
    far_x = run_lags(after(row_x, *second))
    ready = after(third[0], far_x), after(third[1], far_x)
    units += [*first, *second, *third, around(ready[0][0:2], "z", 1), around(ready[1][2:4], "z", -1)]
    for step in (1, 2, 3):
        steps += [[(part, -step) for part in order], [(part, step) for part in order]]
    steps += [[(part, 4) for part in order[0:2]], [(part, 4) for part in order[2:4]]]
    far_xy = run_lags(after(row_xy, *third))
    columns, scale = run_columns(after(place, far_xy), units, steps)
    send_xy = run_weigh(far_xy, columns, scale, SCALE).astype(SENT)
    send_x = run_weigh(far_x, columns, after(scale, send_xy), SCALE).astype(SENT)
    send_y = run_weigh(far_y, columns, scale, SCALE).astype(SENT)
    came_xy = cross_xy(send_xy)
    came_x = cross_x(send_x)
    came_y = cross_y(send_y)
    got_xy = came_xy.astype(jnp.float32)
    got_x = after(came_x, got_xy).astype(jnp.float32)
    got_y = after(came_y, got_x).astype(jnp.float32)
    own = run_lags(after(full, scale))
    kept = run_weigh(own, columns, scale, 1)
    information = run_join(place, kept, got_x, got_xy, got_y)
    return (information, mine)


def solution(mesh):
    fine = Mesh(mesh.devices.reshape(8, 4, 2, 2, 2), ("z", "x", "yh", "yl", "core"))
    rows, bins = ("z", "x", "yh"), ("yl", "core")
    return jax.shard_map(
        shards,
        mesh=fine,
        in_specs=(P(rows, bins), P()),
        out_specs=(P(None, rows, bins), P(rows, bins)),
        check_vma=False,
    )
```

```python
import jax
import jax.numpy as jnp
import numpy as np
from jax import lax
from jax.experimental import pallas as pl
from jax.experimental.pallas import tpu as pltpu
from jax.sharding import Mesh, PartitionSpec as P

LAGS = 9
REACH = 4
HALF = 32
NT = (((1,), (1,)), ((), ()))
MB = 1 << 20
SENT = jnp.float16
SCALE = 65536.0


def band(taps, line, weights):
    line[...] = jnp.zeros(line.shape, jnp.float32)
    line[0:1, 0 : taps.shape[1]] = taps[...]
    wide = jnp.broadcast_to(line[0:1, :], (128, 384))
    full = pltpu.roll(wide, 128 - HALF, axis=1, stride=1, stride_axis=0)
    high = full.astype(jnp.bfloat16)
    rest = full - high.astype(jnp.float32)
    middle = rest.astype(jnp.bfloat16)
    low = (rest - middle.astype(jnp.float32)).astype(jnp.bfloat16)
    weights[0:128] = high
    weights[128:256] = middle
    weights[256:384] = low


def filtered_blocks(window, weights):
    total = None
    for k in range(3):
        piece = window(k)
        piece = piece.reshape(piece.shape[0] * piece.shape[1], 128)
        term = lax.dot_general(
            piece, weights[:, k * 128 : (k + 1) * 128], NT, preferred_element_type=jnp.float32
        )
        total = term if total is None else total + term
    value = (total[:, 256:384] + total[:, 128:256]) + total[:, 0:128]
    return value.astype(jnp.bfloat16)


def edges_kernel(raw, low, high, held):
    low[...] = raw[:, :128]
    high[...] = raw[:, raw.shape[1] - 128 :]
    held[...] = raw[...]


def run_edges(raw):
    rows, bins = raw.shape
    vmem = pl.BlockSpec(memory_space=pltpu.VMEM)
    edge = jax.ShapeDtypeStruct((rows, 128), jnp.bfloat16)
    return pl.pallas_call(
        edges_kernel,
        in_specs=[vmem],
        out_specs=[vmem] * 3,
        out_shape=[edge, edge, jax.ShapeDtypeStruct((rows, bins), jnp.bfloat16)],
        compiler_params=pltpu.CompilerParams(vmem_limit_bytes=8 * MB),
        name="edges",
    )(raw)


def run_band(taps):
    vmem = pl.BlockSpec(memory_space=pltpu.VMEM)
    return pl.pallas_call(
        lambda taps, weights, line: band(taps, line, weights),
        in_specs=[vmem],
        out_specs=vmem,
        out_shape=jax.ShapeDtypeStruct((384, 384), jnp.bfloat16),
        scratch_shapes=[pltpu.VMEM((8, 384), jnp.float32)],
        compiler_params=pltpu.CompilerParams(vmem_limit_bytes=8 * MB),
        name="band",
    )(taps)


def filter_kernel(weights, left, raw, right, out, kept, blocks):
    rows, bins = raw.shape
    count = bins // 128
    blocks[0] = left[...]
    blocks[count + 1] = right[...]
    for n in range(count):
        blocks[1 + n] = raw[:, n * 128 : (n + 1) * 128]
    value = filtered_blocks(lambda k: blocks[k : k + count], weights)
    for n in range(count):
        out[:, n * 128 : (n + 1) * 128] = value[n * rows : (n + 1) * rows]
    kept[...] = out[...]


def run_filter(weights, left, raw, right):
    rows, bins = raw.shape
    vmem = pl.BlockSpec(memory_space=pltpu.VMEM)
    return pl.pallas_call(
        filter_kernel,
        in_specs=[vmem] * 4,
        out_specs=[vmem, vmem],
        out_shape=[jax.ShapeDtypeStruct((rows, bins), jnp.bfloat16)] * 2,
        scratch_shapes=[pltpu.VMEM((bins // 128 + 2, rows, 128), jnp.bfloat16)],
        compiler_params=pltpu.CompilerParams(vmem_limit_bytes=8 * MB),
        name="fir",
    )(weights, left, raw, right)


def slab_kernel(place, *refs):
    parts, out = refs[:-1], refs[-1]
    bins = parts[0].shape[1]
    for flip, part in enumerate(parts):
        out[:, pl.ds(pl.multiple_of((place[2] ^ flip) * bins, 128), bins)] = part[...]


def run_slab(place, parts):
    rows, bins = parts[0].shape
    vmem = pl.BlockSpec(memory_space=pltpu.VMEM)
    return pl.pallas_call(
        slab_kernel,
        in_specs=[pl.BlockSpec(memory_space=pltpu.SMEM)] + [vmem] * len(parts),
        out_specs=vmem,
        out_shape=jax.ShapeDtypeStruct((rows, len(parts) * bins), jnp.bfloat16),
        compiler_params=pltpu.CompilerParams(vmem_limit_bytes=8 * MB),
        name="slab",
    )(place, *parts)


def lag_kernel(rows_ref, out, energy):
    bins = rows_ref.shape[1]
    at = lax.broadcasted_iota(jnp.int32, (16, bins), 1)
    for part in range(rows_ref.shape[0] // 16):
        span = slice(part * 16, (part + 1) * 16)
        value = rows_ref[span].astype(jnp.float32)
        total = jnp.sum(value * value, axis=1, keepdims=True)
        energy[span] = jnp.broadcast_to(total, (16, 128))
        for lag in range(LAGS):
            step = lag - REACH
            if step == 0:
                moved = value
            else:
                moved = pltpu.roll(value, step % bins, axis=1)
                inside = at >= step if step > 0 else at < bins + step
                moved = jnp.where(inside, moved, 0.0)
            out[lag, span] = moved.astype(jnp.bfloat16)


def run_lags(rows):
    count, bins = rows.shape
    vmem = pl.BlockSpec(memory_space=pltpu.VMEM)
    return pl.pallas_call(
        lag_kernel,
        in_specs=[vmem],
        out_specs=[vmem, vmem],
        out_shape=[
            jax.ShapeDtypeStruct((LAGS, count, bins), jnp.bfloat16),
            jax.ShapeDtypeStruct((count, 128), jnp.float32),
        ],
        compiler_params=pltpu.CompilerParams(vmem_limit_bytes=8 * MB),
        cost_estimate=pl.CostEstimate(flops=10 * MB, bytes_accessed=6 * MB, transcendentals=0),
        name="lags",
    )(rows)


def weigh(lagged, energy, right, across, emit):
    lags, count, bins = lagged.shape
    left = lagged[...].reshape(lags * count, bins)
    moments = lax.dot_general(left, right, NT, preferred_element_type=jnp.float32)
    norms = (1.0 / jnp.sqrt(energy[:, 0:1] + 1e-05)) * across
    for lag in range(lags):
        ratio = moments[lag * count : (lag + 1) * count] * norms
        emit(lag, -0.5 * jnp.log(1.0 - ratio * ratio))


def columns_kernel(steps, place, *refs):
    units = refs[: len(steps)]
    columns, scale = refs[len(steps) :]
    z = place[1]
    slab = place[2]
    bins = units[0].shape[2]
    for ref, moves in zip(units, steps):
        for k, (pair, z_step) in enumerate(moves):
            up = (z + z_step - 2 * slab - 1) & 7
            e = (up < 4).astype(jnp.int32)
            giver = (3 - jnp.where(up < 4, up, 7 - up)) ^ slab
            columns[e * 2 + pair, :, pl.ds(pl.multiple_of(giver * bins, 128), bins)] = ref[k]
    for e in range(2):
        block = columns[2 * e : 2 * e + 2].astype(jnp.float32).reshape(128, -1)
        total = jnp.sum(block * block, axis=1, keepdims=True)
        root = 0.8 / jnp.sqrt(total + 1e-05)
        root = jnp.transpose(jnp.broadcast_to(root, (128, 128)))
        scale[:, e * 128 : (e + 1) * 128] = root[0:8]


def run_columns(place, units, steps):
    rows, bins = units[0].shape[1:]

    def body(*refs):
        columns_kernel(steps, *refs)

    vmem = pl.BlockSpec(memory_space=pltpu.VMEM)
    return pl.pallas_call(
        body,
        in_specs=[pl.BlockSpec(memory_space=pltpu.SMEM)] + [vmem] * len(units),
        out_specs=[vmem, vmem],
        out_shape=[
            jax.ShapeDtypeStruct((4, rows, 4 * bins), jnp.bfloat16),
            jax.ShapeDtypeStruct((8, 4 * rows), jnp.float32),
        ],
        compiler_params=pltpu.CompilerParams(vmem_limit_bytes=8 * MB),
        cost_estimate=pl.CostEstimate(flops=8 * MB, bytes_accessed=4 * MB, transcendentals=0),
        name="columns",
    )(place, *units)


def weigh_kernel(factor, lagged, energy, columns, scale, out):
    lags, count, bins = lagged.shape
    left = lagged[...].reshape(lags * count, bins)
    right = columns[...].reshape(-1, bins)
    moments = lax.dot_general(left, right, NT, preferred_element_type=jnp.float32)
    norms = (1.0 / jnp.sqrt(energy[:, 0:1] + 1e-05)) * scale[0:1, :]
    for lag in range(lags):
        ratio = moments[lag * count : (lag + 1) * count] * norms
        value = -0.5 * jnp.log(1.0 - ratio * ratio)
        out[lag] = value if factor == 1 else value * factor


def run_weigh(rows, columns, scale, factor):
    lagged, energy = rows
    lags, count, bins = lagged.shape
    width = scale.shape[1]

    def body(*refs):
        weigh_kernel(factor, *refs)

    vmem = pl.BlockSpec(memory_space=pltpu.VMEM)
    return pl.pallas_call(
        body,
        in_specs=[vmem] * 4,
        out_specs=vmem,
        out_shape=jax.ShapeDtypeStruct((lags, count, width), jnp.float32),
        compiler_params=pltpu.CompilerParams(vmem_limit_bytes=8 * MB),
        cost_estimate=pl.CostEstimate(
            flops=2 * lags * count * width * bins,
            bytes_accessed=4 * lags * count * width,
            transcendentals=lags * count * width,
        ),
        name="weigh",
    )(lagged, energy, columns, scale)


def join_kernel(place, own, got_x, got_xy, got_y, out, buffer, sems):
    low = place[4] == 0
    lags, rows = buffer.shape[:2]
    lane = lax.broadcasted_iota(jnp.int32, (rows, 128), 1) < 64
    copies = []
    for lag in range(lags):
        for half in range(2):
            span = slice(half * 128, (half + 1) * 128)
            for flip, (same, cross) in enumerate(((own, got_y), (got_x, got_xy))):
                here_x = place[3] ^ flip
                here = same[lag, :, span] * (1.0 / SCALE) if flip else same[lag, :, span]
                there = cross[lag, :, span] * (1.0 / SCALE)
                one = jnp.where(low, here, there)
                two = jnp.where(low, there, here)
                at = pl.multiple_of((half * 4 + here_x) * 128, 128)
                buffer[lag, :, pl.ds(at, 128)] = jnp.where(lane, one, pltpu.roll(two, 64, axis=1))
                at = pl.multiple_of((half * 4 + (here_x ^ 2)) * 128, 128)
                buffer[lag, :, pl.ds(at, 128)] = jnp.where(lane, pltpu.roll(one, 64, axis=1), two)
        copies.append(pltpu.make_async_copy(buffer.at[lag], out.at[lag], sems.at[lag]))
        copies[-1].start()
    for copy in copies:
        copy.wait()


def run_join(place, *quarters):
    lags, rows, width = quarters[0].shape
    vmem = pl.BlockSpec(memory_space=pltpu.VMEM)
    return pl.pallas_call(
        join_kernel,
        in_specs=[pl.BlockSpec(memory_space=pltpu.SMEM)] + [vmem] * 4,
        out_specs=pl.BlockSpec(memory_space=pltpu.HBM),
        out_shape=jax.ShapeDtypeStruct((lags, rows, 4 * width), jnp.float32),
        scratch_shapes=[
            pltpu.VMEM((lags, rows, 4 * width), jnp.float32),
            pltpu.SemaphoreType.DMA((lags,)),
        ],
        compiler_params=pltpu.CompilerParams(vmem_limit_bytes=8 * MB),
        name="join",
    )(place, *quarters)


def around(value, axis, step):
    size = lax.axis_size(axis)
    return lax.ppermute(value, axis, [(i, (i + step) % size) for i in range(size)])


def cross_y(value):
    return lax.ppermute(value, "yh", [(0, 1), (1, 0)])


def cross_x(value):
    return lax.ppermute(value, "x", [(0, 1), (1, 0), (2, 3), (3, 2)])


def cross_xy(value):
    return lax.ppermute(value, ("x", "yh"), [(i, i ^ 3) for i in range(8)])


def spread(value, across):
    pairs = []
    for z in range(8):
        a, e = z >> 1, z & 1
        for x in range(4):
            for q in range(4):
                far = 3 - (q ^ a)
                to = (z + far if e else z - far) % 8
                pairs.append(((z * 4 + x) * 4 + q, (to * 4 + (x ^ across)) * 4 + a))
    return lax.ppermute(value, ("z", "x", "yl", "core"), pairs)


def flipped(value, flip):
    return lax.ppermute(value, ("yl", "core"), [(i, i ^ flip) for i in range(4)])


def after(value, *others):
    return lax.optimization_barrier((value, *others))[0]


def shards(raw, taps):
    z = lax.axis_index("z")
    x = lax.axis_index("x")
    yh = lax.axis_index("yh")
    q = lax.axis_index(("yl", "core"))
    place = jnp.stack([yh, z, q, x, yh]).astype(jnp.int32)
    taps = taps.reshape(1, -1)
    low, high, held = run_edges(raw)
    left = lax.ppermute(high, ("yl", "core"), [(i, i + 1) for i in range(3)])
    right = lax.ppermute(low, ("yl", "core"), [(i + 1, i) for i in range(3)])
    mine, kept_mine = run_filter(run_band(after(taps, low)), left, held, right)
    base = jnp.stack([spread(mine, 0), spread(mine, 2)], axis=0)
    units, steps = [base], [[(0, 0), (1, 0)]]
    first = (around(base, "z", 1), around(base, "z", -1))
    second = (around(first[0], "z", 1), around(first[1], "z", -1))
    full = run_slab(after(place, base), [mine] + [flipped(mine, flip) for flip in (1, 2, 3)])
    row_y = cross_y(full)
    row_x = cross_x(full)
    row_xy = cross_x(after(row_y, *first))
    far_y = run_lags(after(row_y, *first))
    third = (around(after(second[0], far_y), "z", 1), around(after(second[1], far_y), "z", -1))
    far_x = run_lags(after(row_x, *second))
    ready = after(third[0], far_x), after(third[1], far_x)
    units += [*first, *second, *third, around(ready[0][0:1], "z", 1), around(ready[1][1:2], "z", -1)]
    for step in (-1, 1, -2, 2, -3, 3):
        steps.append([(0, step), (1, step)])
    steps += [[(0, 4)], [(1, 4)]]
    far_xy = run_lags(after(row_xy, *third))
    columns, scale = run_columns(after(place, far_xy), units, steps)
    send_xy = run_weigh(far_xy, columns, scale, SCALE).astype(SENT)
    send_x = run_weigh(far_x, columns, after(scale, send_xy), SCALE).astype(SENT)
    send_y = run_weigh(far_y, columns, scale, SCALE).astype(SENT)
    came_xy = cross_xy(send_xy)
    came_x = cross_x(send_x)
    came_y = cross_y(send_y)
    got_xy = came_xy.astype(jnp.float32)
    got_x = after(came_x, got_xy).astype(jnp.float32)
    got_y = after(came_y, got_x).astype(jnp.float32)
    own = run_lags(after(full, scale))
    kept = run_weigh(own, columns, scale, 1)
    information = run_join(place, kept, got_x, got_xy, got_y)
    return (information, kept_mine)


def solution(mesh):
    fine = Mesh(mesh.devices.reshape(8, 4, 2, 2, 2), ("z", "x", "yh", "yl", "core"))
    rows, bins = ("z", "x", "yh"), ("yl", "core")
    return jax.shard_map(
        shards,
        mesh=fine,
        in_specs=(P(rows, bins), P()),
        out_specs=(P(None, rows, bins), P(rows, bins)),
        check_vma=False,
    )
```

```python
import jax
import jax.numpy as jnp
import numpy as np
from jax import lax
from jax.experimental import pallas as pl
from jax.experimental.pallas import tpu as pltpu
from jax.sharding import Mesh, PartitionSpec as P

LAGS = 9
REACH = 4
HALF = 32
NT = (((1,), (1,)), ((), ()))
MB = 1 << 20
SENT = jnp.float16
SCALE = 65536.0


def band(taps, line, weights):
    line[...] = jnp.zeros(line.shape, jnp.float32)
    line[0:1, 0 : taps.shape[1]] = taps[...]
    wide = jnp.broadcast_to(line[0:1, :], (128, 384))
    full = pltpu.roll(wide, 128 - HALF, axis=1, stride=1, stride_axis=0)
    high = full.astype(jnp.bfloat16)
    rest = full - high.astype(jnp.float32)
    middle = rest.astype(jnp.bfloat16)
    low = (rest - middle.astype(jnp.float32)).astype(jnp.bfloat16)
    weights[0:128] = high
    weights[128:256] = middle
    weights[256:384] = low


def filtered_blocks(window, weights):
    total = None
    for k in range(3):
        piece = window(k)
        piece = piece.reshape(piece.shape[0] * piece.shape[1], 128)
        term = lax.dot_general(
            piece, weights[:, k * 128 : (k + 1) * 128], NT, preferred_element_type=jnp.float32
        )
        total = term if total is None else total + term
    value = (total[:, 256:384] + total[:, 128:256]) + total[:, 0:128]
    return value.astype(jnp.bfloat16)


def piece_filter_kernel(place, taps, parts, out, blocks, weights, line):
    count, bins = parts.shape[0], parts.shape[2]
    per = bins // 128
    count = count * per
    at = pl.multiple_of(place[2] * 16, 16)
    blocks[0] = jnp.zeros((16, 128), jnp.bfloat16)
    blocks[count + 1] = jnp.zeros((16, 128), jnp.bfloat16)
    for n in range(count):
        b = n % per
        blocks[1 + n] = parts[n // per, pl.ds(at, 16), b * 128 : (b + 1) * 128]
    band(taps, line, weights)
    value = filtered_blocks(lambda k: blocks[k : k + count], weights)
    for n in range(count):
        for h in range(2):
            lo = n * 16 + h * 8
            out[h, :, n * 128 : (n + 1) * 128] = value[lo : lo + 8]


def run_piece_filter(place, taps, parts):
    count, _, bins = parts.shape
    vmem = pl.BlockSpec(memory_space=pltpu.VMEM)
    return pl.pallas_call(
        piece_filter_kernel,
        in_specs=[pl.BlockSpec(memory_space=pltpu.SMEM), vmem, vmem],
        out_specs=vmem,
        out_shape=jax.ShapeDtypeStruct((2, 8, count * bins), jnp.bfloat16),
        scratch_shapes=[
            pltpu.VMEM((count * bins // 128 + 2, 16, 128), jnp.bfloat16),
            pltpu.VMEM((384, 384), jnp.bfloat16),
            pltpu.VMEM((8, 384), jnp.float32),
        ],
        compiler_params=pltpu.CompilerParams(vmem_limit_bytes=8 * MB),
        name="pieces",
    )(place, taps, parts)


def row_filter_kernel(place, taps, parts, out, mine, blocks, weights, line):
    rows, bins = parts.shape[1:]
    per = bins // 128
    count = parts.shape[0] * per
    blocks[0] = jnp.zeros((rows, 128), jnp.bfloat16)
    blocks[count + 1] = jnp.zeros((rows, 128), jnp.bfloat16)
    for n in range(count):
        b = n % per
        blocks[1 + n] = parts[n // per, :, b * 128 : (b + 1) * 128]
    band(taps, line, weights)
    group = 8
    for g in range(0, count, group):
        value = filtered_blocks(lambda k: blocks[g + k : g + k + group], weights)
        for b in range(group):
            n = g + b
            out[:, n * 128 : (n + 1) * 128] = value[b * rows : (b + 1) * rows]
    mine[...] = out[:, pl.ds(pl.multiple_of(place[2] * bins, 128), bins)]


def run_row_filter(place, taps, parts):
    count, rows, bins = parts.shape
    vmem = pl.BlockSpec(memory_space=pltpu.VMEM)
    return pl.pallas_call(
        row_filter_kernel,
        in_specs=[pl.BlockSpec(memory_space=pltpu.SMEM), vmem, vmem],
        out_specs=[vmem, vmem],
        out_shape=[
            jax.ShapeDtypeStruct((rows, count * bins), jnp.bfloat16),
            jax.ShapeDtypeStruct((rows, bins), jnp.bfloat16),
        ],
        scratch_shapes=[
            pltpu.VMEM((count * bins // 128 + 2, rows, 128), jnp.bfloat16),
            pltpu.VMEM((384, 384), jnp.bfloat16),
            pltpu.VMEM((8, 384), jnp.float32),
        ],
        compiler_params=pltpu.CompilerParams(vmem_limit_bytes=8 * MB),
        cost_estimate=pl.CostEstimate(flops=1 << 30, bytes_accessed=4 * MB, transcendentals=0),
        name="rows",
    )(place, taps, parts)


def lag_kernel(rows_ref, out, energy):
    bins = rows_ref.shape[1]
    at = lax.broadcasted_iota(jnp.int32, (16, bins), 1)
    for part in range(rows_ref.shape[0] // 16):
        span = slice(part * 16, (part + 1) * 16)
        value = rows_ref[span].astype(jnp.float32)
        total = jnp.sum(value * value, axis=1, keepdims=True)
        energy[span] = jnp.broadcast_to(total, (16, 128))
        for lag in range(LAGS):
            step = lag - REACH
            if step == 0:
                moved = value
            else:
                moved = pltpu.roll(value, step % bins, axis=1)
                inside = at >= step if step > 0 else at < bins + step
                moved = jnp.where(inside, moved, 0.0)
            out[lag, span] = moved.astype(jnp.bfloat16)


def run_lags(rows):
    count, bins = rows.shape
    vmem = pl.BlockSpec(memory_space=pltpu.VMEM)
    return pl.pallas_call(
        lag_kernel,
        in_specs=[vmem],
        out_specs=[vmem, vmem],
        out_shape=[
            jax.ShapeDtypeStruct((LAGS, count, bins), jnp.bfloat16),
            jax.ShapeDtypeStruct((count, 128), jnp.float32),
        ],
        compiler_params=pltpu.CompilerParams(vmem_limit_bytes=8 * MB),
        cost_estimate=pl.CostEstimate(flops=10 * MB, bytes_accessed=6 * MB, transcendentals=0),
        name="lags",
    )(rows)


def weigh(lagged, energy, right, across, emit):
    lags, count, bins = lagged.shape
    left = lagged[...].reshape(lags * count, bins)
    moments = lax.dot_general(left, right, NT, preferred_element_type=jnp.float32)
    norms = (1.0 / jnp.sqrt(energy[:, 0:1] + 1e-05)) * across
    for lag in range(lags):
        ratio = moments[lag * count : (lag + 1) * count] * norms
        emit(lag, -0.5 * jnp.log(1.0 - ratio * ratio))


def columns_kernel(steps, place, *refs):
    units = refs[: len(steps)]
    columns, scale = refs[len(steps) :]
    z = place[1]
    slab = place[2]
    for ref, moves in zip(units, steps):
        for k, (part, z_step) in enumerate(moves):
            up = (z + z_step - 2 * slab - 1) & 7
            e = (up < 4).astype(jnp.int32)
            giver = (3 - jnp.where(up < 4, up, 7 - up)) ^ slab
            columns[e * 16 + (part >> 1) * 8 + giver * 2 + (part & 1)] = ref[k]
    width = columns.shape[0] * columns.shape[1]
    for g in range(width // 128):
        block = columns[g * 16 : (g + 1) * 16].astype(jnp.float32).reshape(128, -1)
        total = jnp.sum(block * block, axis=1, keepdims=True)
        root = 0.8 / jnp.sqrt(total + 1e-05)
        root = jnp.transpose(jnp.broadcast_to(root, (128, 128)))
        scale[:, g * 128 : (g + 1) * 128] = root[0:8]


def run_columns(place, units, steps):
    slots = sum(len(moves) for moves in steps)
    bins = units[0].shape[2]

    def body(*refs):
        columns_kernel(steps, *refs)

    vmem = pl.BlockSpec(memory_space=pltpu.VMEM)
    return pl.pallas_call(
        body,
        in_specs=[pl.BlockSpec(memory_space=pltpu.SMEM)] + [vmem] * len(units),
        out_specs=[vmem, vmem],
        out_shape=[
            jax.ShapeDtypeStruct((slots, 8, bins), jnp.bfloat16),
            jax.ShapeDtypeStruct((8, slots * 8), jnp.float32),
        ],
        compiler_params=pltpu.CompilerParams(vmem_limit_bytes=8 * MB),
        cost_estimate=pl.CostEstimate(flops=8 * MB, bytes_accessed=4 * MB, transcendentals=0),
        name="columns",
    )(place, *units)


def weigh_kernel(factor, lagged, energy, columns, scale, out):
    lags, count, bins = lagged.shape
    left = lagged[...].reshape(lags * count, bins)
    right = columns[...].reshape(-1, bins)
    moments = lax.dot_general(left, right, NT, preferred_element_type=jnp.float32)
    norms = (1.0 / jnp.sqrt(energy[:, 0:1] + 1e-05)) * scale[0:1, :]
    for lag in range(lags):
        ratio = moments[lag * count : (lag + 1) * count] * norms
        value = -0.5 * jnp.log(1.0 - ratio * ratio)
        out[lag] = value if factor == 1 else value * factor


def run_weigh(rows, columns, scale, factor):
    lagged, energy = rows
    lags, count, bins = lagged.shape
    width = scale.shape[1]

    def body(*refs):
        weigh_kernel(factor, *refs)

    vmem = pl.BlockSpec(memory_space=pltpu.VMEM)
    return pl.pallas_call(
        body,
        in_specs=[vmem] * 4,
        out_specs=vmem,
        out_shape=jax.ShapeDtypeStruct((lags, count, width), jnp.float32),
        compiler_params=pltpu.CompilerParams(vmem_limit_bytes=8 * MB),
        cost_estimate=pl.CostEstimate(
            flops=2 * lags * count * width * bins,
            bytes_accessed=4 * lags * count * width,
            transcendentals=lags * count * width,
        ),
        name="weigh",
    )(lagged, energy, columns, scale)


def join_kernel(flip, place, same, cross, *refs):
    out, tiles, sems = refs[-3:]
    low = place[4] == 0
    here_x = place[3] ^ flip
    lags, rows, width = same.shape
    lane = lax.broadcasted_iota(jnp.int32, (rows, 128), 1) < 64
    copies = []
    for half in range(width // 128):
        span = slice(half * 128, (half + 1) * 128)
        for lag in range(lags):
            here = same[lag, :, span] * (1.0 / SCALE) if flip else same[lag, :, span]
            there = cross[lag, :, span] * (1.0 / SCALE)
            one = jnp.where(low, here, there)
            two = jnp.where(low, there, here)
            tiles[half * 2, lag] = jnp.where(lane, one, pltpu.roll(two, 64, axis=1))
            tiles[half * 2 + 1, lag] = jnp.where(lane, pltpu.roll(one, 64, axis=1), two)
        for k, to_x in enumerate((here_x, here_x ^ 2)):
            at = pl.multiple_of((half * 4 + to_x) * 128, 128)
            tile = half * 2 + k
            copies.append(
                pltpu.make_async_copy(tiles.at[tile], out.at[:, :, pl.ds(at, 128)], sems.at[tile])
            )
            copies[-1].start()
    for copy in copies:
        copy.wait()


def run_join(place, flip, same, cross, *base):
    lags, rows, width = same.shape
    vmem = pl.BlockSpec(memory_space=pltpu.VMEM)
    hbm = pl.BlockSpec(memory_space=pltpu.HBM)

    def body(*refs):
        join_kernel(flip, *refs)

    return pl.pallas_call(
        body,
        in_specs=[pl.BlockSpec(memory_space=pltpu.SMEM), vmem, vmem] + [hbm] * len(base),
        out_specs=hbm,
        out_shape=jax.ShapeDtypeStruct((lags, rows, 4 * width), jnp.float32),
        input_output_aliases={3: 0} if base else {},
        scratch_shapes=[
            pltpu.VMEM((width // 64, lags, rows, 128), jnp.float32),
            pltpu.SemaphoreType.DMA((width // 64,)),
        ],
        compiler_params=pltpu.CompilerParams(vmem_limit_bytes=8 * MB),
        name="join",
    )(place, same, cross, *base)


def around(value, axis, step):
    size = lax.axis_size(axis)
    return lax.ppermute(value, axis, [(i, (i + step) % size) for i in range(size)])


def cross_y(value):
    return lax.ppermute(value, "yh", [(0, 1), (1, 0)])


def cross_x(value):
    return lax.ppermute(value, "x", [(0, 1), (1, 0), (2, 3), (3, 2)])


def cross_xy(value):
    return lax.ppermute(value, ("x", "yh"), [(i, i ^ 3) for i in range(8)])


def spread(value, across):
    pairs = []
    for z in range(8):
        a, e = z >> 1, z & 1
        for x in range(4):
            for q in range(4):
                far = 3 - (q ^ a)
                to = (z + far if e else z - far) % 8
                pairs.append(((z * 4 + x) * 4 + q, (to * 4 + (x ^ across)) * 4 + a))
    return lax.ppermute(value, ("z", "x", "yl", "core"), pairs)


def after(value, *others):
    return lax.optimization_barrier((value, *others))[0]


def shards(raw, taps):
    z = lax.axis_index("z")
    x = lax.axis_index("x")
    yh = lax.axis_index("yh")
    q = lax.axis_index(("yl", "core"))
    place = jnp.stack([yh, z, q, x, yh]).astype(jnp.int32)
    taps = taps.reshape(1, -1)
    parts = lax.all_gather(raw, ("yl", "core"), axis=0, tiled=False)
    given = run_piece_filter(place, taps, parts)
    base = jnp.concatenate([spread(given, 0), spread(given, 2)], axis=0)
    order = (0, 1, 2, 3)
    units, steps = [base], [[(part, 0) for part in order]]
    first = (around(base, "z", 1), around(base, "z", -1))
    second = (around(first[0], "z", 1), around(first[1], "z", -1))
    full, mine = run_row_filter(place, taps, after(parts, given))
    row_y = cross_y(full)
    row_x = cross_x(full)
    row_xy = cross_x(after(row_y, *first))
    far_y = run_lags(after(row_y, *first))
    third = (around(after(second[0], far_y), "z", 1), around(after(second[1], far_y), "z", -1))
    far_x = run_lags(after(row_x, *second))
    ready = after(third[0], far_x), after(third[1], far_x)
    units += [*first, *second, *third, around(ready[0][0:2], "z", 1), around(ready[1][2:4], "z", -1)]
    for step in (1, 2, 3):
        steps += [[(part, -step) for part in order], [(part, step) for part in order]]
    steps += [[(part, 4) for part in order[0:2]], [(part, 4) for part in order[2:4]]]
    far_xy = run_lags(after(row_xy, *third))
    columns, scale = run_columns(after(place, far_xy), units, steps)
    send_xy = run_weigh(far_xy, columns, scale, SCALE).astype(SENT)
    send_x = run_weigh(far_x, columns, after(scale, send_xy), SCALE).astype(SENT)
    send_y = run_weigh(far_y, columns, scale, SCALE).astype(SENT)
    came_xy = cross_xy(send_xy)
    came_x = cross_x(send_x)
    came_y = cross_y(send_y)
    got_xy = came_xy.astype(jnp.float32)
    got_x = after(came_x, got_xy).astype(jnp.float32)
    base = run_join(place, 1, got_x, got_xy)
    got_y = after(came_y, base).astype(jnp.float32)
    own = run_lags(after(full, scale))
    kept = run_weigh(own, columns, scale, 1)
    information = run_join(place, 0, kept, got_y, base)
    return (information, mine)


def solution(mesh):
    fine = Mesh(mesh.devices.reshape(8, 4, 2, 2, 2), ("z", "x", "yh", "yl", "core"))
    rows, bins = ("z", "x", "yh"), ("yl", "core")
    return jax.shard_map(
        shards,
        mesh=fine,
        in_specs=(P(rows, bins), P()),
        out_specs=(P(None, rows, bins), P(rows, bins)),
        check_vma=False,
    )
```

```python
import jax
import jax.numpy as jnp
import numpy as np
from jax import lax
from jax.experimental import pallas as pl
from jax.experimental.pallas import tpu as pltpu
from jax.sharding import Mesh, PartitionSpec as P

LAGS = 9
REACH = 4
HALF = 32
NT = (((1,), (1,)), ((), ()))
MB = 1 << 20
SENT = jnp.float16
SCALE = 65536.0


def band(taps, line, weights):
    line[...] = jnp.zeros(line.shape, jnp.float32)
    line[0:1, 0 : taps.shape[1]] = taps[...]
    wide = jnp.broadcast_to(line[0:1, :], (128, 384))
    full = pltpu.roll(wide, 128 - HALF, axis=1, stride=1, stride_axis=0)
    high = full.astype(jnp.bfloat16)
    rest = full - high.astype(jnp.float32)
    middle = rest.astype(jnp.bfloat16)
    low = (rest - middle.astype(jnp.float32)).astype(jnp.bfloat16)
    weights[0:128] = high
    weights[128:256] = middle
    weights[256:384] = low


def filtered_blocks(window, weights):
    total = None
    for k in range(3):
        piece = window(k)
        piece = piece.reshape(piece.shape[0] * piece.shape[1], 128)
        term = lax.dot_general(
            piece, weights[:, k * 128 : (k + 1) * 128], NT, preferred_element_type=jnp.float32
        )
        total = term if total is None else total + term
    value = (total[:, 256:384] + total[:, 128:256]) + total[:, 0:128]
    return value.astype(jnp.bfloat16)


def piece_filter_kernel(place, taps, parts, out, blocks, weights, line):
    count, bins = parts.shape[0], parts.shape[2]
    per = bins // 128
    count = count * per
    at = pl.multiple_of(place[2] * 16, 16)
    blocks[0] = jnp.zeros((16, 128), jnp.bfloat16)
    blocks[count + 1] = jnp.zeros((16, 128), jnp.bfloat16)
    for n in range(count):
        b = n % per
        blocks[1 + n] = parts[n // per, pl.ds(at, 16), b * 128 : (b + 1) * 128]
    band(taps, line, weights)
    value = filtered_blocks(lambda k: blocks[k : k + count], weights)
    for n in range(count):
        for h in range(2):
            lo = n * 16 + h * 8
            out[h, :, n * 128 : (n + 1) * 128] = value[lo : lo + 8]


def run_piece_filter(place, taps, parts):
    count, _, bins = parts.shape
    vmem = pl.BlockSpec(memory_space=pltpu.VMEM)
    return pl.pallas_call(
        piece_filter_kernel,
        in_specs=[pl.BlockSpec(memory_space=pltpu.SMEM), vmem, vmem],
        out_specs=vmem,
        out_shape=jax.ShapeDtypeStruct((2, 8, count * bins), jnp.bfloat16),
        scratch_shapes=[
            pltpu.VMEM((count * bins // 128 + 2, 16, 128), jnp.bfloat16),
            pltpu.VMEM((384, 384), jnp.bfloat16),
            pltpu.VMEM((8, 384), jnp.float32),
        ],
        compiler_params=pltpu.CompilerParams(vmem_limit_bytes=8 * MB),
        name="pieces",
    )(place, taps, parts)


def row_filter_kernel(place, taps, parts, out, mine, blocks, weights, line):
    rows, bins = parts.shape[1:]
    per = bins // 128
    count = parts.shape[0] * per
    blocks[0] = jnp.zeros((rows, 128), jnp.bfloat16)
    blocks[count + 1] = jnp.zeros((rows, 128), jnp.bfloat16)
    for n in range(count):
        b = n % per
        blocks[1 + n] = parts[n // per, :, b * 128 : (b + 1) * 128]
    band(taps, line, weights)
    group = 8
    for g in range(0, count, group):
        value = filtered_blocks(lambda k: blocks[g + k : g + k + group], weights)
        for b in range(group):
            n = g + b
            out[:, n * 128 : (n + 1) * 128] = value[b * rows : (b + 1) * rows]
    mine[...] = out[:, pl.ds(pl.multiple_of(place[2] * bins, 128), bins)]


def run_row_filter(place, taps, parts):
    count, rows, bins = parts.shape
    vmem = pl.BlockSpec(memory_space=pltpu.VMEM)
    return pl.pallas_call(
        row_filter_kernel,
        in_specs=[pl.BlockSpec(memory_space=pltpu.SMEM), vmem, vmem],
        out_specs=[vmem, vmem],
        out_shape=[
            jax.ShapeDtypeStruct((rows, count * bins), jnp.bfloat16),
            jax.ShapeDtypeStruct((rows, bins), jnp.bfloat16),
        ],
        scratch_shapes=[
            pltpu.VMEM((count * bins // 128 + 2, rows, 128), jnp.bfloat16),
            pltpu.VMEM((384, 384), jnp.bfloat16),
            pltpu.VMEM((8, 384), jnp.float32),
        ],
        compiler_params=pltpu.CompilerParams(vmem_limit_bytes=8 * MB),
        cost_estimate=pl.CostEstimate(flops=1 << 30, bytes_accessed=4 * MB, transcendentals=0),
        name="rows",
    )(place, taps, parts)


def lag_kernel(rows_ref, out, energy):
    bins = rows_ref.shape[1]
    at = lax.broadcasted_iota(jnp.int32, (16, bins), 1)
    for part in range(rows_ref.shape[0] // 16):
        span = slice(part * 16, (part + 1) * 16)
        value = rows_ref[span].astype(jnp.float32)
        total = jnp.sum(value * value, axis=1, keepdims=True)
        energy[span] = jnp.broadcast_to(total, (16, 128))
        for lag in range(LAGS):
            step = lag - REACH
            if step == 0:
                moved = value
            else:
                moved = pltpu.roll(value, step % bins, axis=1)
                inside = at >= step if step > 0 else at < bins + step
                moved = jnp.where(inside, moved, 0.0)
            out[lag, span] = moved.astype(jnp.bfloat16)


def run_lags(rows):
    count, bins = rows.shape
    vmem = pl.BlockSpec(memory_space=pltpu.VMEM)
    return pl.pallas_call(
        lag_kernel,
        in_specs=[vmem],
        out_specs=[vmem, vmem],
        out_shape=[
            jax.ShapeDtypeStruct((LAGS, count, bins), jnp.bfloat16),
            jax.ShapeDtypeStruct((count, 128), jnp.float32),
        ],
        compiler_params=pltpu.CompilerParams(vmem_limit_bytes=8 * MB),
        cost_estimate=pl.CostEstimate(flops=10 * MB, bytes_accessed=6 * MB, transcendentals=0),
        name="lags",
    )(rows)


def weigh(lagged, energy, right, across, emit):
    lags, count, bins = lagged.shape
    left = lagged[...].reshape(lags * count, bins)
    moments = lax.dot_general(left, right, NT, preferred_element_type=jnp.float32)
    norms = (1.0 / jnp.sqrt(energy[:, 0:1] + 1e-05)) * across
    for lag in range(lags):
        ratio = moments[lag * count : (lag + 1) * count] * norms
        emit(lag, -0.5 * jnp.log(1.0 - ratio * ratio))


def columns_kernel(steps, last, place, *refs):
    units = refs[: len(steps)]
    columns = refs[-2] if last else refs[-1]
    z = place[1]
    slab = place[2]
    for ref, moves in zip(units, steps):
        for k, (part, z_step) in enumerate(moves):
            up = (z + z_step - 2 * slab - 1) & 7
            e = (up < 4).astype(jnp.int32)
            giver = (3 - jnp.where(up < 4, up, 7 - up)) ^ slab
            columns[e * 16 + (part >> 1) * 8 + giver * 2 + (part & 1)] = ref[k]
    if last:
        scale = refs[-1]
        for g in range(columns.shape[0] * columns.shape[1] // 128):
            block = columns[g * 16 : (g + 1) * 16].astype(jnp.float32).reshape(128, -1)
            total = jnp.sum(block * block, axis=1, keepdims=True)
            root = 0.8 / jnp.sqrt(total + 1e-05)
            root = jnp.transpose(jnp.broadcast_to(root, (128, 128)))
            scale[:, g * 128 : (g + 1) * 128] = root[0:8]


def run_columns(place, slots, units, steps, *begun):
    bins = units[0].shape[2]
    last = bool(begun)

    def body(*refs):
        columns_kernel(steps, last, *refs)

    vmem = pl.BlockSpec(memory_space=pltpu.VMEM)
    columns = jax.ShapeDtypeStruct((slots, 8, bins), jnp.bfloat16)
    scale = jax.ShapeDtypeStruct((8, slots * 8), jnp.float32)
    return pl.pallas_call(
        body,
        in_specs=[pl.BlockSpec(memory_space=pltpu.SMEM)] + [vmem] * (len(units) + len(begun)),
        out_specs=[vmem, vmem] if last else vmem,
        out_shape=[columns, scale] if last else columns,
        input_output_aliases={1 + len(units): 0} if last else {},
        compiler_params=pltpu.CompilerParams(vmem_limit_bytes=8 * MB),
        cost_estimate=pl.CostEstimate(flops=8 * MB, bytes_accessed=4 * MB, transcendentals=0),
        name="columns",
    )(place, *units, *begun)


def weigh_kernel(factor, lagged, energy, columns, scale, out):
    lags, count, bins = lagged.shape
    left = lagged[...].reshape(lags * count, bins)
    right = columns[...].reshape(-1, bins)
    moments = lax.dot_general(left, right, NT, preferred_element_type=jnp.float32)
    norms = (1.0 / jnp.sqrt(energy[:, 0:1] + 1e-05)) * scale[0:1, :]
    for lag in range(lags):
        ratio = moments[lag * count : (lag + 1) * count] * norms
        value = -0.5 * jnp.log(1.0 - ratio * ratio)
        out[lag] = value if factor == 1 else value * factor


def run_weigh(rows, columns, scale, factor):
    lagged, energy = rows
    lags, count, bins = lagged.shape
    width = scale.shape[1]

    def body(*refs):
        weigh_kernel(factor, *refs)

    vmem = pl.BlockSpec(memory_space=pltpu.VMEM)
    return pl.pallas_call(
        body,
        in_specs=[vmem] * 4,
        out_specs=vmem,
        out_shape=jax.ShapeDtypeStruct((lags, count, width), jnp.float32),
        compiler_params=pltpu.CompilerParams(vmem_limit_bytes=8 * MB),
        cost_estimate=pl.CostEstimate(
            flops=2 * lags * count * width * bins,
            bytes_accessed=4 * lags * count * width,
            transcendentals=lags * count * width,
        ),
        name="weigh",
    )(lagged, energy, columns, scale)


def join_kernel(flip, place, same, cross, *refs):
    out, tiles, sems = refs[-3:]
    low = place[4] == 0
    here_x = place[3] ^ flip
    lags, rows, width = same.shape
    lane = lax.broadcasted_iota(jnp.int32, (rows, 128), 1) < 64
    copies = []
    for half in range(width // 128):
        span = slice(half * 128, (half + 1) * 128)
        for lag in range(lags):
            here = same[lag, :, span] * (1.0 / SCALE) if flip else same[lag, :, span]
            there = cross[lag, :, span] * (1.0 / SCALE)
            one = jnp.where(low, here, there)
            two = jnp.where(low, there, here)
            tiles[half * 2, lag] = jnp.where(lane, one, pltpu.roll(two, 64, axis=1))
            tiles[half * 2 + 1, lag] = jnp.where(lane, pltpu.roll(one, 64, axis=1), two)
        for k, to_x in enumerate((here_x, here_x ^ 2)):
            at = pl.multiple_of((half * 4 + to_x) * 128, 128)
            tile = half * 2 + k
            copies.append(
                pltpu.make_async_copy(tiles.at[tile], out.at[:, :, pl.ds(at, 128)], sems.at[tile])
            )
            copies[-1].start()
    for copy in copies:
        copy.wait()


def run_join(place, flip, same, cross, *base):
    lags, rows, width = same.shape
    vmem = pl.BlockSpec(memory_space=pltpu.VMEM)
    hbm = pl.BlockSpec(memory_space=pltpu.HBM)

    def body(*refs):
        join_kernel(flip, *refs)

    return pl.pallas_call(
        body,
        in_specs=[pl.BlockSpec(memory_space=pltpu.SMEM), vmem, vmem] + [hbm] * len(base),
        out_specs=hbm,
        out_shape=jax.ShapeDtypeStruct((lags, rows, 4 * width), jnp.float32),
        input_output_aliases={3: 0} if base else {},
        scratch_shapes=[
            pltpu.VMEM((width // 64, lags, rows, 128), jnp.float32),
            pltpu.SemaphoreType.DMA((width // 64,)),
        ],
        compiler_params=pltpu.CompilerParams(vmem_limit_bytes=8 * MB),
        name="join",
    )(place, same, cross, *base)


def around(value, axis, step):
    size = lax.axis_size(axis)
    return lax.ppermute(value, axis, [(i, (i + step) % size) for i in range(size)])


def cross_y(value):
    return lax.ppermute(value, "yh", [(0, 1), (1, 0)])


def cross_x(value):
    return lax.ppermute(value, "x", [(0, 1), (1, 0), (2, 3), (3, 2)])


def cross_xy(value):
    return lax.ppermute(value, ("x", "yh"), [(i, i ^ 3) for i in range(8)])


def spread(value, across):
    pairs = []
    for z in range(8):
        a, e = z >> 1, z & 1
        for x in range(4):
            for q in range(4):
                far = 3 - (q ^ a)
                to = (z + far if e else z - far) % 8
                pairs.append(((z * 4 + x) * 4 + q, (to * 4 + (x ^ across)) * 4 + a))
    return lax.ppermute(value, ("z", "x", "yl", "core"), pairs)


def after(value, *others):
    return lax.optimization_barrier((value, *others))[0]


def shards(raw, taps):
    z = lax.axis_index("z")
    x = lax.axis_index("x")
    yh = lax.axis_index("yh")
    q = lax.axis_index(("yl", "core"))
    place = jnp.stack([yh, z, q, x, yh]).astype(jnp.int32)
    taps = taps.reshape(1, -1)
    parts = lax.all_gather(raw, ("yl", "core"), axis=0, tiled=False)
    given = run_piece_filter(place, taps, parts)
    base = jnp.concatenate([spread(given, 0), spread(given, 2)], axis=0)
    order = (0, 1, 2, 3)
    units, steps = [base], [[(part, 0) for part in order]]
    first = (around(base, "z", 1), around(base, "z", -1))
    second = (around(first[0], "z", 1), around(first[1], "z", -1))
    full, mine = run_row_filter(place, taps, after(parts, given))
    row_y = cross_y(full)
    row_x = cross_x(full)
    row_xy = cross_x(after(row_y, *first))
    far_y = run_lags(after(row_y, *first))
    third = (around(after(second[0], far_y), "z", 1), around(after(second[1], far_y), "z", -1))
    far_x = run_lags(after(row_x, *second))
    ready = after(third[0], far_x), after(third[1], far_x)
    units += [*first, *second, *third, around(ready[0][0:2], "z", 1), around(ready[1][2:4], "z", -1)]
    for step in (1, 2, 3):
        steps += [[(part, -step) for part in order], [(part, step) for part in order]]
    steps += [[(part, 4) for part in order[0:2]], [(part, 4) for part in order[2:4]]]
    far_xy = run_lags(after(row_xy, *third))
    slots = sum(len(moves) for moves in steps)
    begun = run_columns(place, slots, units[:-2], steps[:-2])
    ends = after(place, far_xy)
    columns, scale = run_columns(ends, slots, units[-2:], steps[-2:], begun)
    send_xy = run_weigh(far_xy, columns, scale, SCALE).astype(SENT)
    later = after(scale, send_xy)
    send_y = run_weigh(far_y, columns, later, SCALE).astype(SENT)
    send_x = run_weigh(far_x, columns, later, SCALE).astype(SENT)
    came_xy = cross_xy(send_xy)
    came_y = cross_y(send_y)
    came_x = cross_x(send_x)
    got_xy = came_xy.astype(jnp.float32)
    got_y = after(came_y, got_xy).astype(jnp.float32)
    own = run_lags(after(full, scale))
    kept = run_weigh(own, columns, scale, 1)
    base = run_join(place, 0, kept, got_y)
    got_x = after(came_x, base).astype(jnp.float32)
    information = run_join(place, 1, got_x, got_xy, base)
    return (information, mine)


def solution(mesh):
    fine = Mesh(mesh.devices.reshape(8, 4, 2, 2, 2), ("z", "x", "yh", "yl", "core"))
    rows, bins = ("z", "x", "yh"), ("yl", "core")
    return jax.shard_map(
        shards,
        mesh=fine,
        in_specs=(P(rows, bins), P()),
        out_specs=(P(None, rows, bins), P(rows, bins)),
        check_vma=False,
    )
```

```python
import jax
import jax.numpy as jnp
import numpy as np
from jax import lax
from jax.experimental import pallas as pl
from jax.experimental.pallas import tpu as pltpu
from jax.sharding import Mesh, PartitionSpec as P

LAGS = 9
REACH = 4
HALF = 32
NT = (((1,), (1,)), ((), ()))
MB = 1 << 20
SENT = jnp.float16
SCALE = 65536.0


def band(taps, line, weights):
    line[...] = jnp.zeros(line.shape, jnp.float32)
    line[0:1, 0 : taps.shape[1]] = taps[...]
    wide = jnp.broadcast_to(line[0:1, :], (128, 384))
    full = pltpu.roll(wide, 128 - HALF, axis=1, stride=1, stride_axis=0)
    high = full.astype(jnp.bfloat16)
    rest = full - high.astype(jnp.float32)
    middle = rest.astype(jnp.bfloat16)
    low = (rest - middle.astype(jnp.float32)).astype(jnp.bfloat16)
    weights[0:128] = high
    weights[128:256] = middle
    weights[256:384] = low


def filtered_blocks(window, weights):
    total = None
    for k in range(3):
        piece = window(k)
        piece = piece.reshape(piece.shape[0] * piece.shape[1], 128)
        term = lax.dot_general(
            piece, weights[:, k * 128 : (k + 1) * 128], NT, preferred_element_type=jnp.float32
        )
        total = term if total is None else total + term
    value = (total[:, 256:384] + total[:, 128:256]) + total[:, 0:128]
    return value.astype(jnp.bfloat16)


def piece_filter_kernel(place, taps, parts, out, blocks, weights, line):
    count, bins = parts.shape[0], parts.shape[2]
    per = bins // 128
    count = count * per
    at = pl.multiple_of(place[2] * 16, 16)
    blocks[0] = jnp.zeros((16, 128), jnp.bfloat16)
    blocks[count + 1] = jnp.zeros((16, 128), jnp.bfloat16)
    for n in range(count):
        b = n % per
        blocks[1 + n] = parts[n // per, pl.ds(at, 16), b * 128 : (b + 1) * 128]
    band(taps, line, weights)
    value = filtered_blocks(lambda k: blocks[k : k + count], weights)
    for n in range(count):
        for h in range(2):
            lo = n * 16 + h * 8
            out[h, :, n * 128 : (n + 1) * 128] = value[lo : lo + 8]


def run_piece_filter(place, taps, parts):
    count, _, bins = parts.shape
    vmem = pl.BlockSpec(memory_space=pltpu.VMEM)
    return pl.pallas_call(
        piece_filter_kernel,
        in_specs=[pl.BlockSpec(memory_space=pltpu.SMEM), vmem, vmem],
        out_specs=vmem,
        out_shape=jax.ShapeDtypeStruct((2, 8, count * bins), jnp.bfloat16),
        scratch_shapes=[
            pltpu.VMEM((count * bins // 128 + 2, 16, 128), jnp.bfloat16),
            pltpu.VMEM((384, 384), jnp.bfloat16),
            pltpu.VMEM((8, 384), jnp.float32),
        ],
        compiler_params=pltpu.CompilerParams(vmem_limit_bytes=8 * MB),
        name="pieces",
    )(place, taps, parts)


def row_filter_kernel(place, taps, parts, out, mine, blocks, weights, line):
    rows, bins = parts.shape[1:]
    per = bins // 128
    count = parts.shape[0] * per
    blocks[0] = jnp.zeros((rows, 128), jnp.bfloat16)
    blocks[count + 1] = jnp.zeros((rows, 128), jnp.bfloat16)
    for n in range(count):
        b = n % per
        blocks[1 + n] = parts[n // per, :, b * 128 : (b + 1) * 128]
    band(taps, line, weights)
    group = 8
    for g in range(0, count, group):
        value = filtered_blocks(lambda k: blocks[g + k : g + k + group], weights)
        for b in range(group):
            n = g + b
            out[:, n * 128 : (n + 1) * 128] = value[b * rows : (b + 1) * rows]
    mine[...] = out[:, pl.ds(pl.multiple_of(place[2] * bins, 128), bins)]


def run_row_filter(place, taps, parts):
    count, rows, bins = parts.shape
    vmem = pl.BlockSpec(memory_space=pltpu.VMEM)
    return pl.pallas_call(
        row_filter_kernel,
        in_specs=[pl.BlockSpec(memory_space=pltpu.SMEM), vmem, vmem],
        out_specs=[vmem, vmem],
        out_shape=[
            jax.ShapeDtypeStruct((rows, count * bins), jnp.bfloat16),
            jax.ShapeDtypeStruct((rows, bins), jnp.bfloat16),
        ],
        scratch_shapes=[
            pltpu.VMEM((count * bins // 128 + 2, rows, 128), jnp.bfloat16),
            pltpu.VMEM((384, 384), jnp.bfloat16),
            pltpu.VMEM((8, 384), jnp.float32),
        ],
        compiler_params=pltpu.CompilerParams(vmem_limit_bytes=8 * MB),
        cost_estimate=pl.CostEstimate(flops=1 << 30, bytes_accessed=4 * MB, transcendentals=0),
        name="rows",
    )(place, taps, parts)


def lag_kernel(rows_ref, out, energy):
    bins = rows_ref.shape[1]
    at = lax.broadcasted_iota(jnp.int32, (16, bins), 1)
    for part in range(rows_ref.shape[0] // 16):
        span = slice(part * 16, (part + 1) * 16)
        value = rows_ref[span].astype(jnp.float32)
        total = jnp.sum(value * value, axis=1, keepdims=True)
        energy[span] = jnp.broadcast_to(total, (16, 128))
        for lag in range(LAGS):
            step = lag - REACH
            if step == 0:
                moved = value
            else:
                moved = pltpu.roll(value, step % bins, axis=1)
                inside = at >= step if step > 0 else at < bins + step
                moved = jnp.where(inside, moved, 0.0)
            out[lag, span] = moved.astype(jnp.bfloat16)


def run_lags(rows):
    count, bins = rows.shape
    vmem = pl.BlockSpec(memory_space=pltpu.VMEM)
    return pl.pallas_call(
        lag_kernel,
        in_specs=[vmem],
        out_specs=[vmem, vmem],
        out_shape=[
            jax.ShapeDtypeStruct((LAGS, count, bins), jnp.bfloat16),
            jax.ShapeDtypeStruct((count, 128), jnp.float32),
        ],
        compiler_params=pltpu.CompilerParams(vmem_limit_bytes=8 * MB),
        cost_estimate=pl.CostEstimate(flops=10 * MB, bytes_accessed=6 * MB, transcendentals=0),
        name="lags",
    )(rows)


def weigh(lagged, energy, right, across, emit):
    lags, count, bins = lagged.shape
    left = lagged[...].reshape(lags * count, bins)
    moments = lax.dot_general(left, right, NT, preferred_element_type=jnp.float32)
    norms = (1.0 / jnp.sqrt(energy[:, 0:1] + 1e-05)) * across
    for lag in range(lags):
        ratio = moments[lag * count : (lag + 1) * count] * norms
        emit(lag, -0.5 * jnp.log(1.0 - ratio * ratio))


def columns_kernel(steps, place, *refs):
    units = refs[: len(steps)]
    columns, scale = refs[len(steps) :]
    z = place[1]
    slab = place[2]
    for ref, moves in zip(units, steps):
        for k, (part, z_step) in enumerate(moves):
            up = (z + z_step - 2 * slab - 1) & 7
            e = (up < 4).astype(jnp.int32)
            giver = (3 - jnp.where(up < 4, up, 7 - up)) ^ slab
            columns[e * 16 + (part >> 1) * 8 + giver * 2 + (part & 1)] = ref[k]
    width = columns.shape[0] * columns.shape[1]
    for g in range(width // 128):
        block = columns[g * 16 : (g + 1) * 16].astype(jnp.float32).reshape(128, -1)
        total = jnp.sum(block * block, axis=1, keepdims=True)
        root = 0.8 / jnp.sqrt(total + 1e-05)
        root = jnp.transpose(jnp.broadcast_to(root, (128, 128)))
        scale[:, g * 128 : (g + 1) * 128] = root[0:8]


def run_columns(place, units, steps):
    slots = sum(len(moves) for moves in steps)
    bins = units[0].shape[2]

    def body(*refs):
        columns_kernel(steps, *refs)

    vmem = pl.BlockSpec(memory_space=pltpu.VMEM)
    return pl.pallas_call(
        body,
        in_specs=[pl.BlockSpec(memory_space=pltpu.SMEM)] + [vmem] * len(units),
        out_specs=[vmem, vmem],
        out_shape=[
            jax.ShapeDtypeStruct((slots, 8, bins), jnp.bfloat16),
            jax.ShapeDtypeStruct((8, slots * 8), jnp.float32),
        ],
        compiler_params=pltpu.CompilerParams(vmem_limit_bytes=8 * MB),
        cost_estimate=pl.CostEstimate(flops=8 * MB, bytes_accessed=4 * MB, transcendentals=0),
        name="columns",
    )(place, *units)


def weigh_kernel(factor, lagged, energy, columns, scale, out):
    lags, count, bins = lagged.shape
    left = lagged[...].reshape(lags * count, bins)
    right = columns[...].reshape(-1, bins)
    moments = lax.dot_general(left, right, NT, preferred_element_type=jnp.float32)
    norms = (1.0 / jnp.sqrt(energy[:, 0:1] + 1e-05)) * scale[0:1, :]
    for lag in range(lags):
        ratio = moments[lag * count : (lag + 1) * count] * norms
        value = -0.5 * jnp.log(1.0 - ratio * ratio)
        out[lag] = value if factor == 1 else value * factor


def run_weigh(rows, columns, scale, factor):
    lagged, energy = rows
    lags, count, bins = lagged.shape
    width = scale.shape[1]

    def body(*refs):
        weigh_kernel(factor, *refs)

    vmem = pl.BlockSpec(memory_space=pltpu.VMEM)
    return pl.pallas_call(
        body,
        in_specs=[vmem] * 4,
        out_specs=vmem,
        out_shape=jax.ShapeDtypeStruct((lags, count, width), jnp.float32),
        compiler_params=pltpu.CompilerParams(vmem_limit_bytes=8 * MB),
        cost_estimate=pl.CostEstimate(
            flops=2 * lags * count * width * bins,
            bytes_accessed=4 * lags * count * width,
            transcendentals=lags * count * width,
        ),
        name="weigh",
    )(lagged, energy, columns, scale)


def join_kernel(flip, place, same, cross, *refs):
    out, tiles, sems = refs[-3:]
    low = place[4] == 0
    here_x = place[3] ^ flip
    lags, rows, width = same.shape
    lane = lax.broadcasted_iota(jnp.int32, (rows, 128), 1) < 64
    copies = []
    for group in range(0, lags, 3):
        for half in range(width // 128):
            span = slice(half * 128, (half + 1) * 128)
            for lag in range(group, group + 3):
                here = same[lag, :, span] * (1.0 / SCALE) if flip else same[lag, :, span]
                there = cross[lag, :, span] * (1.0 / SCALE)
                one = jnp.where(low, here, there)
                two = jnp.where(low, there, here)
                tiles[half * 2, lag] = jnp.where(lane, one, pltpu.roll(two, 64, axis=1))
                tiles[half * 2 + 1, lag] = jnp.where(lane, pltpu.roll(one, 64, axis=1), two)
            for k, to_x in enumerate((here_x, here_x ^ 2)):
                at = pl.multiple_of((half * 4 + to_x) * 128, 128)
                source = tiles.at[half * 2 + k, pl.ds(group, 3)]
                target = out.at[pl.ds(group, 3), :, pl.ds(at, 128)]
                copies.append(pltpu.make_async_copy(source, target, sems.at[len(copies)]))
                copies[-1].start()
    for copy in copies:
        copy.wait()


def run_join(place, flip, same, cross, *base):
    lags, rows, width = same.shape
    vmem = pl.BlockSpec(memory_space=pltpu.VMEM)
    hbm = pl.BlockSpec(memory_space=pltpu.HBM)

    def body(*refs):
        join_kernel(flip, *refs)

    return pl.pallas_call(
        body,
        in_specs=[pl.BlockSpec(memory_space=pltpu.SMEM), vmem, vmem] + [hbm] * len(base),
        out_specs=hbm,
        out_shape=jax.ShapeDtypeStruct((lags, rows, 4 * width), jnp.float32),
        input_output_aliases={3: 0} if base else {},
        scratch_shapes=[
            pltpu.VMEM((width // 64, lags, rows, 128), jnp.float32),
            pltpu.SemaphoreType.DMA((width // 64 * (lags // 3),)),
        ],
        compiler_params=pltpu.CompilerParams(vmem_limit_bytes=8 * MB),
        name="join",
    )(place, same, cross, *base)


def around(value, axis, step):
    size = lax.axis_size(axis)
    return lax.ppermute(value, axis, [(i, (i + step) % size) for i in range(size)])


def cross_y(value):
    return lax.ppermute(value, "yh", [(0, 1), (1, 0)])


def cross_x(value):
    return lax.ppermute(value, "x", [(0, 1), (1, 0), (2, 3), (3, 2)])


def cross_xy(value):
    return lax.ppermute(value, ("x", "yh"), [(i, i ^ 3) for i in range(8)])


def spread(value, across):
    pairs = []
    for z in range(8):
        a, e = z >> 1, z & 1
        for x in range(4):
            for q in range(4):
                far = 3 - (q ^ a)
                to = (z + far if e else z - far) % 8
                pairs.append(((z * 4 + x) * 4 + q, (to * 4 + (x ^ across)) * 4 + a))
    return lax.ppermute(value, ("z", "x", "yl", "core"), pairs)


def after(value, *others):
    return lax.optimization_barrier((value, *others))[0]


def shards(raw, taps):
    z = lax.axis_index("z")
    x = lax.axis_index("x")
    yh = lax.axis_index("yh")
    q = lax.axis_index(("yl", "core"))
    place = jnp.stack([yh, z, q, x, yh]).astype(jnp.int32)
    taps = taps.reshape(1, -1)
    parts = lax.all_gather(raw, ("yl", "core"), axis=0, tiled=False)
    given = run_piece_filter(place, taps, parts)
    base = jnp.concatenate([spread(given, 2), spread(given, 0)], axis=0)
    order = (2, 3, 0, 1)
    units, steps = [base], [[(part, 0) for part in order]]
    first = (around(base, "z", 1), around(base, "z", -1))
    second = (around(first[0], "z", 1), around(first[1], "z", -1))
    full, mine = run_row_filter(place, taps, after(parts, given))
    row_y = cross_y(full)
    row_x = cross_x(full)
    row_xy = cross_x(after(row_y, *first))
    far_y = run_lags(after(row_y, *first))
    third = (around(after(second[0], far_y), "z", 1), around(after(second[1], far_y), "z", -1))
    far_x = run_lags(after(row_x, *second))
    ready = after(third[0], far_x), after(third[1], far_x)
    units += [*first, *second, *third, around(ready[0][0:2], "z", 1), around(ready[1][2:4], "z", -1)]
    for step in (1, 2, 3):
        steps += [[(part, -step) for part in order], [(part, step) for part in order]]
    steps += [[(part, 4) for part in order[0:2]], [(part, 4) for part in order[2:4]]]
    far_xy = run_lags(after(row_xy, *third))
    columns, scale = run_columns(after(place, far_xy), units, steps)
    send_xy = run_weigh(far_xy, columns, scale, SCALE).astype(SENT)
    send_x = run_weigh(far_x, columns, after(scale, send_xy), SCALE).astype(SENT)
    send_y = run_weigh(far_y, columns, scale, SCALE).astype(SENT)
    came_xy = cross_xy(send_xy)
    came_x = cross_x(send_x)
    came_y = cross_y(send_y)
    got_xy = came_xy.astype(jnp.float32)
    got_x = after(came_x, got_xy).astype(jnp.float32)
    base = run_join(place, 1, got_x, got_xy)
    got_y = after(came_y, base).astype(jnp.float32)
    own = run_lags(after(full, scale))
    kept = run_weigh(own, columns, scale, 1)
    information = run_join(place, 0, kept, got_y, base)
    return (information, mine)


def solution(mesh):
    fine = Mesh(mesh.devices.reshape(8, 4, 2, 2, 2), ("z", "x", "yh", "yl", "core"))
    rows, bins = ("z", "x", "yh"), ("yl", "core")
    return jax.shard_map(
        shards,
        mesh=fine,
        in_specs=(P(rows, bins), P()),
        out_specs=(P(None, rows, bins), P(rows, bins)),
        check_vma=False,
    )
```

```python
import jax
import jax.numpy as jnp
import numpy as np
from jax import lax
from jax.experimental import pallas as pl
from jax.experimental.pallas import tpu as pltpu
from jax.sharding import Mesh, PartitionSpec as P

LAGS = 9
REACH = 4
HALF = 32
NT = (((1,), (1,)), ((), ()))
MB = 1 << 20
SENT = jnp.float16
SCALE = 65536.0


def band(taps, line, weights):
    line[...] = jnp.zeros(line.shape, jnp.float32)
    line[0:1, 0 : taps.shape[1]] = taps[...]
    wide = jnp.broadcast_to(line[0:1, :], (128, 384))
    full = pltpu.roll(wide, 128 - HALF, axis=1, stride=1, stride_axis=0)
    high = full.astype(jnp.bfloat16)
    rest = full - high.astype(jnp.float32)
    middle = rest.astype(jnp.bfloat16)
    low = (rest - middle.astype(jnp.float32)).astype(jnp.bfloat16)
    weights[0:128] = high
    weights[128:256] = middle
    weights[256:384] = low


def filtered_blocks(window, weights):
    total = None
    for k in range(3):
        piece = window(k)
        piece = piece.reshape(piece.shape[0] * piece.shape[1], 128)
        term = lax.dot_general(
            piece, weights[:, k * 128 : (k + 1) * 128], NT, preferred_element_type=jnp.float32
        )
        total = term if total is None else total + term
    value = (total[:, 256:384] + total[:, 128:256]) + total[:, 0:128]
    return value.astype(jnp.bfloat16)


def piece_filter_kernel(place, taps, parts, out, blocks, weights, line):
    count, bins = parts.shape[0], parts.shape[2]
    per = bins // 128
    count = count * per
    at = pl.multiple_of(place[2] * 16, 16)
    blocks[0] = jnp.zeros((16, 128), jnp.bfloat16)
    blocks[count + 1] = jnp.zeros((16, 128), jnp.bfloat16)
    for n in range(count):
        b = n % per
        blocks[1 + n] = parts[n // per, pl.ds(at, 16), b * 128 : (b + 1) * 128]
    band(taps, line, weights)
    value = filtered_blocks(lambda k: blocks[k : k + count], weights)
    for n in range(count):
        for h in range(2):
            lo = n * 16 + h * 8
            out[h, :, n * 128 : (n + 1) * 128] = value[lo : lo + 8]


def run_piece_filter(place, taps, parts):
    count, _, bins = parts.shape
    vmem = pl.BlockSpec(memory_space=pltpu.VMEM)
    return pl.pallas_call(
        piece_filter_kernel,
        in_specs=[pl.BlockSpec(memory_space=pltpu.SMEM), vmem, vmem],
        out_specs=vmem,
        out_shape=jax.ShapeDtypeStruct((2, 8, count * bins), jnp.bfloat16),
        scratch_shapes=[
            pltpu.VMEM((count * bins // 128 + 2, 16, 128), jnp.bfloat16),
            pltpu.VMEM((384, 384), jnp.bfloat16),
            pltpu.VMEM((8, 384), jnp.float32),
        ],
        compiler_params=pltpu.CompilerParams(vmem_limit_bytes=8 * MB),
        name="pieces",
    )(place, taps, parts)


def row_filter_kernel(place, taps, parts, out, mine, blocks, weights, line):
    rows, bins = parts.shape[1:]
    per = bins // 128
    count = parts.shape[0] * per
    blocks[0] = jnp.zeros((rows, 128), jnp.bfloat16)
    blocks[count + 1] = jnp.zeros((rows, 128), jnp.bfloat16)
    for n in range(count):
        b = n % per
        blocks[1 + n] = parts[n // per, :, b * 128 : (b + 1) * 128]
    band(taps, line, weights)
    group = 8
    for g in range(0, count, group):
        value = filtered_blocks(lambda k: blocks[g + k : g + k + group], weights)
        for b in range(group):
            n = g + b
            out[:, n * 128 : (n + 1) * 128] = value[b * rows : (b + 1) * rows]
    mine[...] = out[:, pl.ds(pl.multiple_of(place[2] * bins, 128), bins)]


def run_row_filter(place, taps, parts):
    count, rows, bins = parts.shape
    vmem = pl.BlockSpec(memory_space=pltpu.VMEM)
    return pl.pallas_call(
        row_filter_kernel,
        in_specs=[pl.BlockSpec(memory_space=pltpu.SMEM), vmem, vmem],
        out_specs=[vmem, vmem],
        out_shape=[
            jax.ShapeDtypeStruct((rows, count * bins), jnp.bfloat16),
            jax.ShapeDtypeStruct((rows, bins), jnp.bfloat16),
        ],
        scratch_shapes=[
            pltpu.VMEM((count * bins // 128 + 2, rows, 128), jnp.bfloat16),
            pltpu.VMEM((384, 384), jnp.bfloat16),
            pltpu.VMEM((8, 384), jnp.float32),
        ],
        compiler_params=pltpu.CompilerParams(vmem_limit_bytes=8 * MB),
        cost_estimate=pl.CostEstimate(flops=1 << 30, bytes_accessed=4 * MB, transcendentals=0),
        name="rows",
    )(place, taps, parts)


def lag_kernel(rows_ref, out, energy):
    bins = rows_ref.shape[1]
    at = lax.broadcasted_iota(jnp.int32, (16, bins), 1)
    for part in range(rows_ref.shape[0] // 16):
        span = slice(part * 16, (part + 1) * 16)
        value = rows_ref[span].astype(jnp.float32)
        total = jnp.sum(value * value, axis=1, keepdims=True)
        energy[span] = jnp.broadcast_to(total, (16, 128))
        for lag in range(LAGS):
            step = lag - REACH
            if step == 0:
                moved = value
            else:
                moved = pltpu.roll(value, step % bins, axis=1)
                inside = at >= step if step > 0 else at < bins + step
                moved = jnp.where(inside, moved, 0.0)
            out[lag, span] = moved.astype(jnp.bfloat16)


def run_lags(rows):
    count, bins = rows.shape
    vmem = pl.BlockSpec(memory_space=pltpu.VMEM)
    return pl.pallas_call(
        lag_kernel,
        in_specs=[vmem],
        out_specs=[vmem, vmem],
        out_shape=[
            jax.ShapeDtypeStruct((LAGS, count, bins), jnp.bfloat16),
            jax.ShapeDtypeStruct((count, 128), jnp.float32),
        ],
        compiler_params=pltpu.CompilerParams(vmem_limit_bytes=8 * MB),
        cost_estimate=pl.CostEstimate(flops=10 * MB, bytes_accessed=6 * MB, transcendentals=0),
        name="lags",
    )(rows)


def weigh(lagged, energy, right, across, emit):
    lags, count, bins = lagged.shape
    left = lagged[...].reshape(lags * count, bins)
    moments = lax.dot_general(left, right, NT, preferred_element_type=jnp.float32)
    norms = (1.0 / jnp.sqrt(energy[:, 0:1] + 1e-05)) * across
    for lag in range(lags):
        ratio = moments[lag * count : (lag + 1) * count] * norms
        emit(lag, -0.5 * jnp.log(1.0 - ratio * ratio))


def columns_kernel(steps, place, lagged, energy, *refs):
    units = refs[: len(steps)]
    columns, scale, out = refs[len(steps) :]
    z = place[1]
    slab = place[2]
    for ref, moves in zip(units, steps):
        for k, (part, z_step) in enumerate(moves):
            up = (z + z_step - 2 * slab - 1) & 7
            e = (up < 4).astype(jnp.int32)
            giver = (3 - jnp.where(up < 4, up, 7 - up)) ^ slab
            columns[e * 16 + (part >> 1) * 8 + giver * 2 + (part & 1)] = ref[k]
    lags, count, bins = lagged.shape
    left = lagged[...].reshape(lags * count, bins)
    right = columns[...].reshape(-1, bins)
    moments = lax.dot_general(left, right, NT, preferred_element_type=jnp.float32)
    for g in range(right.shape[0] // 128):
        block = right[g * 128 : (g + 1) * 128].astype(jnp.float32)
        total = jnp.sum(block * block, axis=1, keepdims=True)
        root = 0.8 / jnp.sqrt(total + 1e-05)
        root = jnp.transpose(jnp.broadcast_to(root, (128, 128)))
        scale[:, g * 128 : (g + 1) * 128] = root[0:8]
    emit(moments, energy, scale, SCALE, out)


def run_columns(place, rows, units, steps):
    slots = sum(len(moves) for moves in steps)
    lags, count, bins = rows[0].shape

    def body(*refs):
        columns_kernel(steps, *refs)

    vmem = pl.BlockSpec(memory_space=pltpu.VMEM)
    return pl.pallas_call(
        body,
        in_specs=[pl.BlockSpec(memory_space=pltpu.SMEM)] + [vmem] * (2 + len(units)),
        out_specs=[vmem] * 3,
        out_shape=[
            jax.ShapeDtypeStruct((slots, 8, bins), jnp.bfloat16),
            jax.ShapeDtypeStruct((8, slots * 8), jnp.float32),
            jax.ShapeDtypeStruct((lags, count, slots * 8), jnp.float32),
        ],
        compiler_params=pltpu.CompilerParams(vmem_limit_bytes=8 * MB),
        cost_estimate=pl.CostEstimate(flops=1 << 30, bytes_accessed=4 * MB, transcendentals=0),
        name="columns",
    )(place, *rows, *units)


def emit(moments, energy, scale, factor, out):
    lags, count = out.shape[:2]
    norms = (1.0 / jnp.sqrt(energy[:, 0:1] + 1e-05)) * scale[0:1, :]
    for lag in range(lags):
        ratio = moments[lag * count : (lag + 1) * count] * norms
        value = -0.5 * jnp.log(1.0 - ratio * ratio)
        out[lag] = value if factor == 1 else value * factor


def weigh_kernel(factor, lagged, energy, columns, scale, out):
    lags, count, bins = lagged.shape
    left = lagged[...].reshape(lags * count, bins)
    right = columns[...].reshape(-1, bins)
    moments = lax.dot_general(left, right, NT, preferred_element_type=jnp.float32)
    emit(moments, energy, scale, factor, out)


def run_weigh(rows, columns, scale, factor):
    lagged, energy = rows
    lags, count, bins = lagged.shape
    width = scale.shape[1]

    def body(*refs):
        weigh_kernel(factor, *refs)

    vmem = pl.BlockSpec(memory_space=pltpu.VMEM)
    return pl.pallas_call(
        body,
        in_specs=[vmem] * 4,
        out_specs=vmem,
        out_shape=jax.ShapeDtypeStruct((lags, count, width), jnp.float32),
        compiler_params=pltpu.CompilerParams(vmem_limit_bytes=8 * MB),
        cost_estimate=pl.CostEstimate(
            flops=2 * lags * count * width * bins,
            bytes_accessed=4 * lags * count * width,
            transcendentals=lags * count * width,
        ),
        name="weigh",
    )(lagged, energy, columns, scale)


def join_kernel(flip, place, same, cross, *refs):
    out, tiles, sems = refs[-3:]
    low = place[4] == 0
    here_x = place[3] ^ flip
    lags, rows, width = same.shape
    lane = lax.broadcasted_iota(jnp.int32, (rows, 128), 1) < 64
    copies = []
    for group in range(0, lags, 3):
        for half in range(width // 128):
            span = slice(half * 128, (half + 1) * 128)
            for lag in range(group, group + 3):
                here = same[lag, :, span] * (1.0 / SCALE) if flip else same[lag, :, span]
                there = cross[lag, :, span] * (1.0 / SCALE)
                one = jnp.where(low, here, there)
                two = jnp.where(low, there, here)
                tiles[half * 2, lag] = jnp.where(lane, one, pltpu.roll(two, 64, axis=1))
                tiles[half * 2 + 1, lag] = jnp.where(lane, pltpu.roll(one, 64, axis=1), two)
            for k, to_x in enumerate((here_x, here_x ^ 2)):
                at = pl.multiple_of((half * 4 + to_x) * 128, 128)
                source = tiles.at[half * 2 + k, pl.ds(group, 3)]
                target = out.at[pl.ds(group, 3), :, pl.ds(at, 128)]
                copies.append(pltpu.make_async_copy(source, target, sems.at[len(copies)]))
                copies[-1].start()
    for copy in copies:
        copy.wait()


def run_join(place, flip, same, cross, *base):
    lags, rows, width = same.shape
    vmem = pl.BlockSpec(memory_space=pltpu.VMEM)
    hbm = pl.BlockSpec(memory_space=pltpu.HBM)

    def body(*refs):
        join_kernel(flip, *refs)

    return pl.pallas_call(
        body,
        in_specs=[pl.BlockSpec(memory_space=pltpu.SMEM), vmem, vmem] + [hbm] * len(base),
        out_specs=hbm,
        out_shape=jax.ShapeDtypeStruct((lags, rows, 4 * width), jnp.float32),
        input_output_aliases={3: 0} if base else {},
        scratch_shapes=[
            pltpu.VMEM((width // 64, lags, rows, 128), jnp.float32),
            pltpu.SemaphoreType.DMA((width // 64 * (lags // 3),)),
        ],
        compiler_params=pltpu.CompilerParams(vmem_limit_bytes=8 * MB),
        name="join",
    )(place, same, cross, *base)


def around(value, axis, step):
    size = lax.axis_size(axis)
    return lax.ppermute(value, axis, [(i, (i + step) % size) for i in range(size)])


def cross_y(value):
    return lax.ppermute(value, "yh", [(0, 1), (1, 0)])


def cross_x(value):
    return lax.ppermute(value, "x", [(0, 1), (1, 0), (2, 3), (3, 2)])


def cross_xy(value):
    return lax.ppermute(value, ("x", "yh"), [(i, i ^ 3) for i in range(8)])


def spread(value, across):
    pairs = []
    for z in range(8):
        a, e = z >> 1, z & 1
        for x in range(4):
            for q in range(4):
                far = 3 - (q ^ a)
                to = (z + far if e else z - far) % 8
                pairs.append(((z * 4 + x) * 4 + q, (to * 4 + (x ^ across)) * 4 + a))
    return lax.ppermute(value, ("z", "x", "yl", "core"), pairs)


def after(value, *others):
    return lax.optimization_barrier((value, *others))[0]


def shards(raw, taps):
    z = lax.axis_index("z")
    x = lax.axis_index("x")
    yh = lax.axis_index("yh")
    q = lax.axis_index(("yl", "core"))
    place = jnp.stack([yh, z, q, x, yh]).astype(jnp.int32)
    taps = taps.reshape(1, -1)
    parts = lax.all_gather(raw, ("yl", "core"), axis=0, tiled=False)
    given = run_piece_filter(place, taps, parts)
    base = jnp.concatenate([spread(given, 2), spread(given, 0)], axis=0)
    order = (2, 3, 0, 1)
    units, steps = [base], [[(part, 0) for part in order]]
    first = (around(base, "z", 1), around(base, "z", -1))
    second = (around(first[0], "z", 1), around(first[1], "z", -1))
    full, mine = run_row_filter(place, taps, after(parts, given))
    row_y = cross_y(full)
    row_x = cross_x(full)
    row_xy = cross_x(after(row_y, *first))
    far_y = run_lags(after(row_y, *first))
    third = (around(after(second[0], far_y), "z", 1), around(after(second[1], far_y), "z", -1))
    far_x = run_lags(after(row_x, *second))
    ready = after(third[0], far_x), after(third[1], far_x)
    units += [*first, *second, *third, around(ready[0][0:2], "z", 1), around(ready[1][2:4], "z", -1)]
    for step in (1, 2, 3):
        steps += [[(part, -step) for part in order], [(part, step) for part in order]]
    steps += [[(part, 4) for part in order[0:2]], [(part, 4) for part in order[2:4]]]
    far_xy = run_lags(after(row_xy, *third))
    columns, scale, send_xy = run_columns(place, far_xy, units, steps)
    send_xy = send_xy.astype(SENT)
    send_x = run_weigh(far_x, columns, after(scale, send_xy), SCALE).astype(SENT)
    send_y = run_weigh(far_y, columns, scale, SCALE).astype(SENT)
    came_xy = cross_xy(send_xy)
    came_x = cross_x(send_x)
    came_y = cross_y(send_y)
    got_xy = came_xy.astype(jnp.float32)
    got_x = after(came_x, got_xy).astype(jnp.float32)
    base = run_join(place, 1, got_x, got_xy)
    got_y = after(came_y, base).astype(jnp.float32)
    own = run_lags(after(full, scale))
    kept = run_weigh(own, columns, scale, 1)
    information = run_join(place, 0, kept, got_y, base)
    return (information, mine)


def solution(mesh):
    fine = Mesh(mesh.devices.reshape(8, 4, 2, 2, 2), ("z", "x", "yh", "yl", "core"))
    rows, bins = ("z", "x", "yh"), ("yl", "core")
    return jax.shard_map(
        shards,
        mesh=fine,
        in_specs=(P(rows, bins), P()),
        out_specs=(P(None, rows, bins), P(rows, bins)),
        check_vma=False,
    )
```

```python
import jax
import jax.numpy as jnp
import numpy as np
from jax import lax
from jax.experimental import pallas as pl
from jax.experimental.pallas import tpu as pltpu
from jax.sharding import Mesh, PartitionSpec as P

LAGS = 9
REACH = 4
HALF = 32
NT = (((1,), (1,)), ((), ()))
MB = 1 << 20
SENT = jnp.float16
SCALE = 65536.0


def band(taps, line, weights):
    line[...] = jnp.zeros(line.shape, jnp.float32)
    line[0:1, 0 : taps.shape[1]] = taps[...]
    wide = jnp.broadcast_to(line[0:1, :], (128, 384))
    full = pltpu.roll(wide, 128 - HALF, axis=1, stride=1, stride_axis=0)
    high = full.astype(jnp.bfloat16)
    rest = full - high.astype(jnp.float32)
    middle = rest.astype(jnp.bfloat16)
    low = (rest - middle.astype(jnp.float32)).astype(jnp.bfloat16)
    weights[0:128] = high
    weights[128:256] = middle
    weights[256:384] = low


def filtered_blocks(window, weights):
    total = None
    for k in range(3):
        piece = window(k)
        piece = piece.reshape(piece.shape[0] * piece.shape[1], 128)
        term = lax.dot_general(
            piece, weights[:, k * 128 : (k + 1) * 128], NT, preferred_element_type=jnp.float32
        )
        total = term if total is None else total + term
    value = (total[:, 256:384] + total[:, 128:256]) + total[:, 0:128]
    return value.astype(jnp.bfloat16)


def piece_filter_kernel(place, taps, parts, out, blocks, weights, line):
    count, bins = parts.shape[0], parts.shape[2]
    per = bins // 128
    count = count * per
    at = pl.multiple_of(place[2] * 16, 16)
    blocks[0] = jnp.zeros((16, 128), jnp.bfloat16)
    blocks[count + 1] = jnp.zeros((16, 128), jnp.bfloat16)
    for n in range(count):
        b = n % per
        blocks[1 + n] = parts[n // per, pl.ds(at, 16), b * 128 : (b + 1) * 128]
    band(taps, line, weights)
    value = filtered_blocks(lambda k: blocks[k : k + count], weights)
    for n in range(count):
        for h in range(2):
            lo = n * 16 + h * 8
            out[h, :, n * 128 : (n + 1) * 128] = value[lo : lo + 8]


def run_piece_filter(place, taps, parts):
    count, _, bins = parts.shape
    vmem = pl.BlockSpec(memory_space=pltpu.VMEM)
    return pl.pallas_call(
        piece_filter_kernel,
        in_specs=[pl.BlockSpec(memory_space=pltpu.SMEM), vmem, vmem],
        out_specs=vmem,
        out_shape=jax.ShapeDtypeStruct((2, 8, count * bins), jnp.bfloat16),
        scratch_shapes=[
            pltpu.VMEM((count * bins // 128 + 2, 16, 128), jnp.bfloat16),
            pltpu.VMEM((384, 384), jnp.bfloat16),
            pltpu.VMEM((8, 384), jnp.float32),
        ],
        compiler_params=pltpu.CompilerParams(vmem_limit_bytes=8 * MB),
        name="pieces",
    )(place, taps, parts)


def row_filter_kernel(place, taps, parts, out, mine, blocks, weights, line):
    rows, bins = parts.shape[1:]
    per = bins // 128
    count = parts.shape[0] * per
    blocks[0] = jnp.zeros((rows, 128), jnp.bfloat16)
    blocks[count + 1] = jnp.zeros((rows, 128), jnp.bfloat16)
    for n in range(count):
        b = n % per
        blocks[1 + n] = parts[n // per, :, b * 128 : (b + 1) * 128]
    band(taps, line, weights)
    group = 8
    for g in range(0, count, group):
        value = filtered_blocks(lambda k: blocks[g + k : g + k + group], weights)
        for b in range(group):
            n = g + b
            out[:, n * 128 : (n + 1) * 128] = value[b * rows : (b + 1) * rows]
    mine[...] = out[:, pl.ds(pl.multiple_of(place[2] * bins, 128), bins)]


def run_row_filter(place, taps, parts):
    count, rows, bins = parts.shape
    vmem = pl.BlockSpec(memory_space=pltpu.VMEM)
    return pl.pallas_call(
        row_filter_kernel,
        in_specs=[pl.BlockSpec(memory_space=pltpu.SMEM), vmem, vmem],
        out_specs=[vmem, vmem],
        out_shape=[
            jax.ShapeDtypeStruct((rows, count * bins), jnp.bfloat16),
            jax.ShapeDtypeStruct((rows, bins), jnp.bfloat16),
        ],
        scratch_shapes=[
            pltpu.VMEM((count * bins // 128 + 2, rows, 128), jnp.bfloat16),
            pltpu.VMEM((384, 384), jnp.bfloat16),
            pltpu.VMEM((8, 384), jnp.float32),
        ],
        compiler_params=pltpu.CompilerParams(vmem_limit_bytes=8 * MB),
        cost_estimate=pl.CostEstimate(flops=1 << 30, bytes_accessed=4 * MB, transcendentals=0),
        name="rows",
    )(place, taps, parts)


def lag_kernel(rows_ref, out, energy):
    bins = rows_ref.shape[1]
    at = lax.broadcasted_iota(jnp.int32, (16, bins), 1)
    for part in range(rows_ref.shape[0] // 16):
        span = slice(part * 16, (part + 1) * 16)
        value = rows_ref[span].astype(jnp.float32)
        total = jnp.sum(value * value, axis=1, keepdims=True)
        energy[span] = jnp.broadcast_to(total, (16, 128))
        for lag in range(LAGS):
            step = lag - REACH
            if step == 0:
                moved = value
            else:
                moved = pltpu.roll(value, step % bins, axis=1)
                inside = at >= step if step > 0 else at < bins + step
                moved = jnp.where(inside, moved, 0.0)
            out[lag, span] = moved.astype(jnp.bfloat16)


def run_lags(rows):
    count, bins = rows.shape
    vmem = pl.BlockSpec(memory_space=pltpu.VMEM)
    return pl.pallas_call(
        lag_kernel,
        in_specs=[vmem],
        out_specs=[vmem, vmem],
        out_shape=[
            jax.ShapeDtypeStruct((LAGS, count, bins), jnp.bfloat16),
            jax.ShapeDtypeStruct((count, 128), jnp.float32),
        ],
        compiler_params=pltpu.CompilerParams(vmem_limit_bytes=8 * MB),
        cost_estimate=pl.CostEstimate(flops=10 * MB, bytes_accessed=6 * MB, transcendentals=0),
        name="lags",
    )(rows)


def weigh(lagged, energy, right, across, emit):
    lags, count, bins = lagged.shape
    left = lagged[...].reshape(lags * count, bins)
    moments = lax.dot_general(left, right, NT, preferred_element_type=jnp.float32)
    norms = (1.0 / jnp.sqrt(energy[:, 0:1] + 1e-05)) * across
    for lag in range(lags):
        ratio = moments[lag * count : (lag + 1) * count] * norms
        emit(lag, -0.5 * jnp.log(1.0 - ratio * ratio))


def columns_kernel(steps, place, lagged, energy, *refs):
    units = refs[: len(steps)]
    columns, scale, out = refs[len(steps) :]
    z = place[1]
    slab = place[2]
    for ref, moves in zip(units, steps):
        for k, (part, z_step) in enumerate(moves):
            up = (z + z_step - 2 * slab - 1) & 7
            e = (up < 4).astype(jnp.int32)
            giver = (3 - jnp.where(up < 4, up, 7 - up)) ^ slab
            columns[e * 16 + (part >> 1) * 8 + giver * 2 + (part & 1)] = ref[k]
    lags, count, bins = lagged.shape
    left = lagged[...].reshape(lags * count, bins)
    right = columns[...].reshape(-1, bins)
    moments = lax.dot_general(left, right, NT, preferred_element_type=jnp.float32)
    for g in range(right.shape[0] // 128):
        block = right[g * 128 : (g + 1) * 128].astype(jnp.float32)
        total = jnp.sum(block * block, axis=1, keepdims=True)
        root = 0.8 / jnp.sqrt(total + 1e-05)
        root = jnp.transpose(jnp.broadcast_to(root, (128, 128)))
        scale[:, g * 128 : (g + 1) * 128] = root[0:8]
    emit(moments, energy, scale, SCALE, out)


def run_columns(place, rows, units, steps):
    slots = sum(len(moves) for moves in steps)
    lags, count, bins = rows[0].shape

    def body(*refs):
        columns_kernel(steps, *refs)

    vmem = pl.BlockSpec(memory_space=pltpu.VMEM)
    return pl.pallas_call(
        body,
        in_specs=[pl.BlockSpec(memory_space=pltpu.SMEM)] + [vmem] * (2 + len(units)),
        out_specs=[vmem] * 3,
        out_shape=[
            jax.ShapeDtypeStruct((slots, 8, bins), jnp.bfloat16),
            jax.ShapeDtypeStruct((8, slots * 8), jnp.float32),
            jax.ShapeDtypeStruct((lags, count, slots * 8), jnp.float32),
        ],
        compiler_params=pltpu.CompilerParams(vmem_limit_bytes=8 * MB),
        cost_estimate=pl.CostEstimate(flops=1 << 30, bytes_accessed=4 * MB, transcendentals=0),
        name="columns",
    )(place, *rows, *units)


def emit(moments, energy, scale, factor, out):
    lags, count = out.shape[:2]
    norms = (1.0 / jnp.sqrt(energy[:, 0:1] + 1e-05)) * scale[0:1, :]
    for lag in range(lags):
        ratio = moments[lag * count : (lag + 1) * count] * norms
        value = -0.5 * jnp.log(1.0 - ratio * ratio)
        out[lag] = value if factor == 1 else value * factor


def weigh_kernel(factor, lagged, energy, columns, scale, out):
    lags, count, bins = lagged.shape
    left = lagged[...].reshape(lags * count, bins)
    right = columns[...].reshape(-1, bins)
    moments = lax.dot_general(left, right, NT, preferred_element_type=jnp.float32)
    emit(moments, energy, scale, factor, out)


def run_weigh(rows, columns, scale, factor):
    lagged, energy = rows
    lags, count, bins = lagged.shape
    width = scale.shape[1]

    def body(*refs):
        weigh_kernel(factor, *refs)

    vmem = pl.BlockSpec(memory_space=pltpu.VMEM)
    return pl.pallas_call(
        body,
        in_specs=[vmem] * 4,
        out_specs=vmem,
        out_shape=jax.ShapeDtypeStruct((lags, count, width), jnp.float32),
        compiler_params=pltpu.CompilerParams(vmem_limit_bytes=8 * MB),
        cost_estimate=pl.CostEstimate(
            flops=2 * lags * count * width * bins,
            bytes_accessed=4 * lags * count * width,
            transcendentals=lags * count * width,
        ),
        name="weigh",
    )(lagged, energy, columns, scale)


def join_kernel(flip, place, same, cross, *refs):
    out, tiles, sems = refs[-3:]
    low = place[4] == 0
    here_x = place[3] ^ flip
    lags, rows, width = same.shape
    lane = lax.broadcasted_iota(jnp.int32, (rows, 128), 1) < 64
    copies = []
    for group in range(0, lags, 3):
        for half in range(width // 128):
            span = slice(half * 128, (half + 1) * 128)
            for lag in range(group, group + 3):
                here = same[lag, :, span] * (1.0 / SCALE) if flip else same[lag, :, span]
                there = cross[lag, :, span] * (1.0 / SCALE)
                one = jnp.where(low, here, there)
                two = jnp.where(low, there, here)
                tiles[half * 2, lag] = jnp.where(lane, one, pltpu.roll(two, 64, axis=1))
                tiles[half * 2 + 1, lag] = jnp.where(lane, pltpu.roll(one, 64, axis=1), two)
            for k, to_x in enumerate((here_x, here_x ^ 2)):
                at = pl.multiple_of((half * 4 + to_x) * 128, 128)
                source = tiles.at[half * 2 + k, pl.ds(group, 3)]
                target = out.at[pl.ds(group, 3), :, pl.ds(at, 128)]
                copies.append(pltpu.make_async_copy(source, target, sems.at[len(copies)]))
                copies[-1].start()
    for copy in copies:
        copy.wait()


def run_join(place, flip, same, cross, *base):
    lags, rows, width = same.shape
    vmem = pl.BlockSpec(memory_space=pltpu.VMEM)
    hbm = pl.BlockSpec(memory_space=pltpu.HBM)

    def body(*refs):
        join_kernel(flip, *refs)

    return pl.pallas_call(
        body,
        in_specs=[pl.BlockSpec(memory_space=pltpu.SMEM), vmem, vmem] + [hbm] * len(base),
        out_specs=hbm,
        out_shape=jax.ShapeDtypeStruct((lags, rows, 4 * width), jnp.float32),
        input_output_aliases={3: 0} if base else {},
        scratch_shapes=[
            pltpu.VMEM((width // 64, lags, rows, 128), jnp.float32),
            pltpu.SemaphoreType.DMA((width // 64 * (lags // 3),)),
        ],
        compiler_params=pltpu.CompilerParams(vmem_limit_bytes=8 * MB),
        name="join",
    )(place, same, cross, *base)


def around(value, axis, step):
    size = lax.axis_size(axis)
    return lax.ppermute(value, axis, [(i, (i + step) % size) for i in range(size)])


def cross_y(value):
    return lax.ppermute(value, "yh", [(0, 1), (1, 0)])


def cross_x(value):
    return lax.ppermute(value, "x", [(0, 1), (1, 0), (2, 3), (3, 2)])


def cross_xy(value):
    return lax.ppermute(value, ("x", "yh"), [(i, i ^ 3) for i in range(8)])


def spread(value, across):
    pairs = []
    for z in range(8):
        a, e = z >> 1, z & 1
        for x in range(4):
            for q in range(4):
                far = 3 - (q ^ a)
                to = (z + far if e else z - far) % 8
                pairs.append(((z * 4 + x) * 4 + q, (to * 4 + (x ^ across)) * 4 + a))
    return lax.ppermute(value, ("z", "x", "yl", "core"), pairs)


def after(value, *others):
    return lax.optimization_barrier((value, *others))[0]


def shards(raw, taps):
    z = lax.axis_index("z")
    x = lax.axis_index("x")
    yh = lax.axis_index("yh")
    q = lax.axis_index(("yl", "core"))
    place = jnp.stack([yh, z, q, x, yh]).astype(jnp.int32)
    taps = taps.reshape(1, -1)
    parts = lax.all_gather(raw, ("yl", "core"), axis=0, tiled=False)
    given = run_piece_filter(place, taps, parts)
    base = jnp.concatenate([spread(given, 2), spread(given, 0)], axis=0)
    order = (2, 3, 0, 1)
    units, steps = [base], [[(part, 0) for part in order]]
    first = (around(base, "z", 1), around(base, "z", -1))
    second = (around(first[0], "z", 1), around(first[1], "z", -1))
    full, mine = run_row_filter(place, taps, after(parts, given))
    row_x = cross_x(full)
    row_y = cross_y(full)
    row_xy = cross_y(after(row_x, *first))
    far_x = run_lags(after(row_x, *first))
    third = (around(after(second[0], far_x), "z", 1), around(after(second[1], far_x), "z", -1))
    far_y = run_lags(after(row_y, *second))
    ready = after(third[0], far_y), after(third[1], far_y)
    units += [*first, *second, *third, around(ready[0][0:2], "z", 1), around(ready[1][2:4], "z", -1)]
    for step in (1, 2, 3):
        steps += [[(part, -step) for part in order], [(part, step) for part in order]]
    steps += [[(part, 4) for part in order[0:2]], [(part, 4) for part in order[2:4]]]
    far_xy = run_lags(after(row_xy, *third))
    columns, scale, send_xy = run_columns(place, far_xy, units, steps)
    send_xy = send_xy.astype(SENT)
    send_x = run_weigh(far_x, columns, after(scale, send_xy), SCALE).astype(SENT)
    send_y = run_weigh(far_y, columns, scale, SCALE).astype(SENT)
    came_xy = cross_xy(send_xy)
    came_x = cross_x(send_x)
    came_y = cross_y(send_y)
    got_xy = came_xy.astype(jnp.float32)
    got_x = after(came_x, got_xy).astype(jnp.float32)
    base = run_join(place, 1, got_x, got_xy)
    got_y = after(came_y, base).astype(jnp.float32)
    own = run_lags(after(full, scale))
    kept = run_weigh(own, columns, scale, 1)
    information = run_join(place, 0, kept, got_y, base)
    return (information, mine)


def solution(mesh):
    fine = Mesh(mesh.devices.reshape(8, 4, 2, 2, 2), ("z", "x", "yh", "yl", "core"))
    rows, bins = ("z", "x", "yh"), ("yl", "core")
    return jax.shard_map(
        shards,
        mesh=fine,
        in_specs=(P(rows, bins), P()),
        out_specs=(P(None, rows, bins), P(rows, bins)),
        check_vma=False,
    )
```

```python
import jax
import jax.numpy as jnp
import numpy as np
from jax import lax
from jax.experimental import pallas as pl
from jax.experimental.pallas import tpu as pltpu
from jax.sharding import Mesh, PartitionSpec as P

LAGS = 9
REACH = 4
HALF = 32
NT = (((1,), (1,)), ((), ()))
MB = 1 << 20
SENT = jnp.float16
SCALE = 65536.0


def band(taps, line, weights):
    line[...] = jnp.zeros(line.shape, jnp.float32)
    line[0:1, 0 : taps.shape[1]] = taps[...]
    wide = jnp.broadcast_to(line[0:1, :], (128, 384))
    full = pltpu.roll(wide, 128 - HALF, axis=1, stride=1, stride_axis=0)
    high = full.astype(jnp.bfloat16)
    rest = full - high.astype(jnp.float32)
    middle = rest.astype(jnp.bfloat16)
    low = (rest - middle.astype(jnp.float32)).astype(jnp.bfloat16)
    weights[0:128] = high
    weights[128:256] = middle
    weights[256:384] = low


def filtered_blocks(window, weights):
    total = None
    for k in range(3):
        piece = window(k)
        piece = piece.reshape(piece.shape[0] * piece.shape[1], 128)
        term = lax.dot_general(
            piece, weights[:, k * 128 : (k + 1) * 128], NT, preferred_element_type=jnp.float32
        )
        total = term if total is None else total + term
    value = (total[:, 256:384] + total[:, 128:256]) + total[:, 0:128]
    return value.astype(jnp.bfloat16)


def piece_filter_kernel(place, taps, parts, out, blocks, weights, line):
    count, bins = parts.shape[0], parts.shape[2]
    per = bins // 128
    count = count * per
    at = pl.multiple_of(place[2] * 16, 16)
    blocks[0] = jnp.zeros((16, 128), jnp.bfloat16)
    blocks[count + 1] = jnp.zeros((16, 128), jnp.bfloat16)
    for n in range(count):
        b = n % per
        blocks[1 + n] = parts[n // per, pl.ds(at, 16), b * 128 : (b + 1) * 128]
    band(taps, line, weights)
    value = filtered_blocks(lambda k: blocks[k : k + count], weights)
    for n in range(count):
        for h in range(2):
            lo = n * 16 + h * 8
            out[h, :, n * 128 : (n + 1) * 128] = value[lo : lo + 8]


def run_piece_filter(place, taps, parts):
    count, _, bins = parts.shape
    vmem = pl.BlockSpec(memory_space=pltpu.VMEM)
    return pl.pallas_call(
        piece_filter_kernel,
        in_specs=[pl.BlockSpec(memory_space=pltpu.SMEM), vmem, vmem],
        out_specs=vmem,
        out_shape=jax.ShapeDtypeStruct((2, 8, count * bins), jnp.bfloat16),
        scratch_shapes=[
            pltpu.VMEM((count * bins // 128 + 2, 16, 128), jnp.bfloat16),
            pltpu.VMEM((384, 384), jnp.bfloat16),
            pltpu.VMEM((8, 384), jnp.float32),
        ],
        compiler_params=pltpu.CompilerParams(vmem_limit_bytes=8 * MB),
        name="pieces",
    )(place, taps, parts)


def row_filter_kernel(place, taps, parts, out, mine, blocks, weights, line):
    rows, bins = parts.shape[1:]
    per = bins // 128
    count = parts.shape[0] * per
    blocks[0] = jnp.zeros((rows, 128), jnp.bfloat16)
    blocks[count + 1] = jnp.zeros((rows, 128), jnp.bfloat16)
    for n in range(count):
        b = n % per
        blocks[1 + n] = parts[n // per, :, b * 128 : (b + 1) * 128]
    band(taps, line, weights)
    group = 8
    for g in range(0, count, group):
        value = filtered_blocks(lambda k: blocks[g + k : g + k + group], weights)
        for b in range(group):
            n = g + b
            out[:, n * 128 : (n + 1) * 128] = value[b * rows : (b + 1) * rows]
    mine[...] = out[:, pl.ds(pl.multiple_of(place[2] * bins, 128), bins)]


def run_row_filter(place, taps, parts):
    count, rows, bins = parts.shape
    vmem = pl.BlockSpec(memory_space=pltpu.VMEM)
    return pl.pallas_call(
        row_filter_kernel,
        in_specs=[pl.BlockSpec(memory_space=pltpu.SMEM), vmem, vmem],
        out_specs=[vmem, vmem],
        out_shape=[
            jax.ShapeDtypeStruct((rows, count * bins), jnp.bfloat16),
            jax.ShapeDtypeStruct((rows, bins), jnp.bfloat16),
        ],
        scratch_shapes=[
            pltpu.VMEM((count * bins // 128 + 2, rows, 128), jnp.bfloat16),
            pltpu.VMEM((384, 384), jnp.bfloat16),
            pltpu.VMEM((8, 384), jnp.float32),
        ],
        compiler_params=pltpu.CompilerParams(vmem_limit_bytes=8 * MB),
        cost_estimate=pl.CostEstimate(flops=1 << 30, bytes_accessed=4 * MB, transcendentals=0),
        name="rows",
    )(place, taps, parts)


def lag_kernel(rows_ref, out, energy):
    bins = rows_ref.shape[1]
    at = lax.broadcasted_iota(jnp.int32, (16, bins), 1)
    for part in range(rows_ref.shape[0] // 16):
        span = slice(part * 16, (part + 1) * 16)
        value = rows_ref[span].astype(jnp.float32)
        total = jnp.sum(value * value, axis=1, keepdims=True)
        energy[span] = jnp.broadcast_to(total, (16, 128))
        for lag in range(LAGS):
            step = lag - REACH
            if step == 0:
                moved = value
            else:
                moved = pltpu.roll(value, step % bins, axis=1)
                inside = at >= step if step > 0 else at < bins + step
                moved = jnp.where(inside, moved, 0.0)
            out[lag, span] = moved.astype(jnp.bfloat16)


def run_lags(rows):
    count, bins = rows.shape
    vmem = pl.BlockSpec(memory_space=pltpu.VMEM)
    return pl.pallas_call(
        lag_kernel,
        in_specs=[vmem],
        out_specs=[vmem, vmem],
        out_shape=[
            jax.ShapeDtypeStruct((LAGS, count, bins), jnp.bfloat16),
            jax.ShapeDtypeStruct((count, 128), jnp.float32),
        ],
        compiler_params=pltpu.CompilerParams(vmem_limit_bytes=8 * MB),
        cost_estimate=pl.CostEstimate(flops=10 * MB, bytes_accessed=6 * MB, transcendentals=0),
        name="lags",
    )(rows)


def weigh(lagged, energy, right, across, emit):
    lags, count, bins = lagged.shape
    left = lagged[...].reshape(lags * count, bins)
    moments = lax.dot_general(left, right, NT, preferred_element_type=jnp.float32)
    norms = (1.0 / jnp.sqrt(energy[:, 0:1] + 1e-05)) * across
    for lag in range(lags):
        ratio = moments[lag * count : (lag + 1) * count] * norms
        emit(lag, -0.5 * jnp.log(1.0 - ratio * ratio))


def columns_kernel(steps, place, lagged, energy, *refs):
    units = refs[: len(steps)]
    columns, scale, out = refs[len(steps) :]
    z = place[1]
    slab = place[2]
    for ref, moves in zip(units, steps):
        for k, (part, z_step) in enumerate(moves):
            up = (z + z_step - 2 * slab - 1) & 7
            e = (up < 4).astype(jnp.int32)
            giver = (3 - jnp.where(up < 4, up, 7 - up)) ^ slab
            columns[e * 16 + (part >> 1) * 8 + giver * 2 + (part & 1)] = ref[k]
    lags, count, bins = lagged.shape
    left = lagged[...].reshape(lags * count, bins)
    right = columns[...].reshape(-1, bins)
    moments = lax.dot_general(left, right, NT, preferred_element_type=jnp.float32)
    for g in range(right.shape[0] // 128):
        block = right[g * 128 : (g + 1) * 128].astype(jnp.float32)
        total = jnp.sum(block * block, axis=1, keepdims=True)
        root = 0.8 / jnp.sqrt(total + 1e-05)
        root = jnp.transpose(jnp.broadcast_to(root, (128, 128)))
        scale[:, g * 128 : (g + 1) * 128] = root[0:8]
    emit(moments, energy, scale, SCALE, out)


def run_columns(place, rows, units, steps):
    slots = sum(len(moves) for moves in steps)
    lags, count, bins = rows[0].shape

    def body(*refs):
        columns_kernel(steps, *refs)

    vmem = pl.BlockSpec(memory_space=pltpu.VMEM)
    return pl.pallas_call(
        body,
        in_specs=[pl.BlockSpec(memory_space=pltpu.SMEM)] + [vmem] * (2 + len(units)),
        out_specs=[vmem] * 3,
        out_shape=[
            jax.ShapeDtypeStruct((slots, 8, bins), jnp.bfloat16),
            jax.ShapeDtypeStruct((8, slots * 8), jnp.float32),
            jax.ShapeDtypeStruct((lags, count, slots * 8), jnp.float32),
        ],
        compiler_params=pltpu.CompilerParams(vmem_limit_bytes=8 * MB),
        cost_estimate=pl.CostEstimate(flops=1 << 30, bytes_accessed=4 * MB, transcendentals=0),
        name="columns",
    )(place, *rows, *units)


def emit(moments, energy, scale, factor, out):
    lags, count = out.shape[:2]
    norms = (1.0 / jnp.sqrt(energy[:, 0:1] + 1e-05)) * scale[0:1, :]
    for lag in range(lags):
        ratio = moments[lag * count : (lag + 1) * count] * norms
        value = -0.5 * jnp.log(1.0 - ratio * ratio)
        out[lag] = value if factor == 1 else value * factor


def weigh_kernel(factor, lagged, energy, columns, scale, out):
    lags, count, bins = lagged.shape
    left = lagged[...].reshape(lags * count, bins)
    right = columns[...].reshape(-1, bins)
    moments = lax.dot_general(left, right, NT, preferred_element_type=jnp.float32)
    emit(moments, energy, scale, factor, out)


def run_weigh(rows, columns, scale, factor):
    lagged, energy = rows
    lags, count, bins = lagged.shape
    width = scale.shape[1]

    def body(*refs):
        weigh_kernel(factor, *refs)

    vmem = pl.BlockSpec(memory_space=pltpu.VMEM)
    return pl.pallas_call(
        body,
        in_specs=[vmem] * 4,
        out_specs=vmem,
        out_shape=jax.ShapeDtypeStruct((lags, count, width), jnp.float32),
        compiler_params=pltpu.CompilerParams(vmem_limit_bytes=8 * MB),
        cost_estimate=pl.CostEstimate(
            flops=2 * lags * count * width * bins,
            bytes_accessed=4 * lags * count * width,
            transcendentals=lags * count * width,
        ),
        name="weigh",
    )(lagged, energy, columns, scale)


def join_kernel(flip, place, same, cross, *refs):
    out, tiles, sems = refs[-3:]
    low = place[4] == 0
    here_x = place[3] ^ flip
    lags, rows, width = same.shape
    lane = lax.broadcasted_iota(jnp.int32, (rows, 128), 1) < 64
    copies = []
    for lag in range(lags):
        for half in range(width // 128):
            span = slice(half * 128, (half + 1) * 128)
            here = same[lag, :, span] * (1.0 / SCALE) if flip else same[lag, :, span]
            there = cross[lag, :, span] * (1.0 / SCALE)
            one = jnp.where(low, here, there)
            two = jnp.where(low, there, here)
            tiles[half * 2, lag] = jnp.where(lane, one, pltpu.roll(two, 64, axis=1))
            tiles[half * 2 + 1, lag] = jnp.where(lane, pltpu.roll(one, 64, axis=1), two)
            for k, to_x in enumerate((here_x, here_x ^ 2)):
                at = pl.multiple_of((half * 4 + to_x) * 128, 128)
                source = tiles.at[half * 2 + k, lag]
                target = out.at[lag, :, pl.ds(at, 128)]
                copies.append(pltpu.make_async_copy(source, target, sems.at[len(copies)]))
                copies[-1].start()
    for copy in copies:
        copy.wait()


def run_join(place, flip, same, cross, *base):
    lags, rows, width = same.shape
    vmem = pl.BlockSpec(memory_space=pltpu.VMEM)
    hbm = pl.BlockSpec(memory_space=pltpu.HBM)

    def body(*refs):
        join_kernel(flip, *refs)

    return pl.pallas_call(
        body,
        in_specs=[pl.BlockSpec(memory_space=pltpu.SMEM), vmem, vmem] + [hbm] * len(base),
        out_specs=hbm,
        out_shape=jax.ShapeDtypeStruct((lags, rows, 4 * width), jnp.float32),
        input_output_aliases={3: 0} if base else {},
        scratch_shapes=[
            pltpu.VMEM((width // 64, lags, rows, 128), jnp.float32),
            pltpu.SemaphoreType.DMA((width // 64 * lags,)),
        ],
        compiler_params=pltpu.CompilerParams(vmem_limit_bytes=8 * MB),
        name="join",
    )(place, same, cross, *base)


def around(value, axis, step):
    size = lax.axis_size(axis)
    return lax.ppermute(value, axis, [(i, (i + step) % size) for i in range(size)])


def cross_y(value):
    return lax.ppermute(value, "yh", [(0, 1), (1, 0)])


def cross_x(value):
    return lax.ppermute(value, "x", [(0, 1), (1, 0), (2, 3), (3, 2)])


def cross_xy(value):
    return lax.ppermute(value, ("x", "yh"), [(i, i ^ 3) for i in range(8)])


def spread(value, across):
    pairs = []
    for z in range(8):
        a, e = z >> 1, z & 1
        for x in range(4):
            for q in range(4):
                far = 3 - (q ^ a)
                to = (z + far if e else z - far) % 8
                pairs.append(((z * 4 + x) * 4 + q, (to * 4 + (x ^ across)) * 4 + a))
    return lax.ppermute(value, ("z", "x", "yl", "core"), pairs)


def after(value, *others):
    return lax.optimization_barrier((value, *others))[0]


def shards(raw, taps):
    z = lax.axis_index("z")
    x = lax.axis_index("x")
    yh = lax.axis_index("yh")
    q = lax.axis_index(("yl", "core"))
    place = jnp.stack([yh, z, q, x, yh]).astype(jnp.int32)
    taps = taps.reshape(1, -1)
    parts = lax.all_gather(raw, ("yl", "core"), axis=0, tiled=False)
    given = run_piece_filter(place, taps, parts)
    base = jnp.concatenate([spread(given, 2), spread(given, 0)], axis=0)
    order = (2, 3, 0, 1)
    units, steps = [base], [[(part, 0) for part in order]]
    first = (around(base, "z", 1), around(base, "z", -1))
    second = (around(first[0], "z", 1), around(first[1], "z", -1))
    full, mine = run_row_filter(place, taps, after(parts, given))
    row_y = cross_y(full)
    row_x = cross_x(full)
    row_xy = cross_x(after(row_y, *first))
    far_y = run_lags(after(row_y, *first))
    third = (around(after(second[0], far_y), "z", 1), around(after(second[1], far_y), "z", -1))
    far_x = run_lags(after(row_x, *second))
    ready = after(third[0], far_x), after(third[1], far_x)
    units += [*first, *second, *third, around(ready[0][0:2], "z", 1), around(ready[1][2:4], "z", -1)]
    for step in (1, 2, 3):
        steps += [[(part, -step) for part in order], [(part, step) for part in order]]
    steps += [[(part, 4) for part in order[0:2]], [(part, 4) for part in order[2:4]]]
    far_xy = run_lags(after(row_xy, *third))
    columns, scale, send_xy = run_columns(place, far_xy, units, steps)
    send_xy = send_xy.astype(SENT)
    send_x = run_weigh(far_x, columns, after(scale, send_xy), SCALE).astype(SENT)
    send_y = run_weigh(far_y, columns, scale, SCALE).astype(SENT)
    came_xy = cross_xy(send_xy)
    came_x = cross_x(send_x)
    came_y = cross_y(send_y)
    got_xy = came_xy.astype(jnp.float32)
    got_x = after(came_x, got_xy).astype(jnp.float32)
    base = run_join(place, 1, got_x, got_xy)
    got_y = after(came_y, base).astype(jnp.float32)
    own = run_lags(after(full, scale))
    kept = run_weigh(own, columns, scale, 1)
    information = run_join(place, 0, kept, got_y, base)
    return (information, mine)


def solution(mesh):
    fine = Mesh(mesh.devices.reshape(8, 4, 2, 2, 2), ("z", "x", "yh", "yl", "core"))
    rows, bins = ("z", "x", "yh"), ("yl", "core")
    return jax.shard_map(
        shards,
        mesh=fine,
        in_specs=(P(rows, bins), P()),
        out_specs=(P(None, rows, bins), P(rows, bins)),
        check_vma=False,
    )
```

```python
import jax
import jax.numpy as jnp
import numpy as np
from jax import lax
from jax.experimental import pallas as pl
from jax.experimental.pallas import tpu as pltpu
from jax.sharding import Mesh, PartitionSpec as P

LAGS = 9
REACH = 4
HALF = 32
NT = (((1,), (1,)), ((), ()))
MB = 1 << 20
SENT = jnp.float16
SCALE = 65536.0


def band(taps, line, weights):
    line[...] = jnp.zeros(line.shape, jnp.float32)
    line[0:1, 0 : taps.shape[1]] = taps[...]
    wide = jnp.broadcast_to(line[0:1, :], (128, 384))
    full = pltpu.roll(wide, 128 - HALF, axis=1, stride=1, stride_axis=0)
    high = full.astype(jnp.bfloat16)
    rest = full - high.astype(jnp.float32)
    middle = rest.astype(jnp.bfloat16)
    low = (rest - middle.astype(jnp.float32)).astype(jnp.bfloat16)
    weights[0:128] = high
    weights[128:256] = middle
    weights[256:384] = low


def filtered_blocks(window, weights):
    total = None
    for k in range(3):
        piece = window(k)
        piece = piece.reshape(piece.shape[0] * piece.shape[1], 128)
        term = lax.dot_general(
            piece, weights[:, k * 128 : (k + 1) * 128], NT, preferred_element_type=jnp.float32
        )
        total = term if total is None else total + term
    value = (total[:, 256:384] + total[:, 128:256]) + total[:, 0:128]
    return value.astype(jnp.bfloat16)


def piece_filter_kernel(place, taps, parts, out, blocks, weights, line):
    count, bins = parts.shape[0], parts.shape[2]
    per = bins // 128
    count = count * per
    at = pl.multiple_of(place[2] * 16, 16)
    blocks[0] = jnp.zeros((16, 128), jnp.bfloat16)
    blocks[count + 1] = jnp.zeros((16, 128), jnp.bfloat16)
    for n in range(count):
        b = n % per
        blocks[1 + n] = parts[n // per, pl.ds(at, 16), b * 128 : (b + 1) * 128]
    band(taps, line, weights)
    value = filtered_blocks(lambda k: blocks[k : k + count], weights)
    for n in range(count):
        for h in range(2):
            lo = n * 16 + h * 8
            out[h, :, n * 128 : (n + 1) * 128] = value[lo : lo + 8]


def run_piece_filter(place, taps, parts):
    count, _, bins = parts.shape
    vmem = pl.BlockSpec(memory_space=pltpu.VMEM)
    return pl.pallas_call(
        piece_filter_kernel,
        in_specs=[pl.BlockSpec(memory_space=pltpu.SMEM), vmem, vmem],
        out_specs=vmem,
        out_shape=jax.ShapeDtypeStruct((2, 8, count * bins), jnp.bfloat16),
        scratch_shapes=[
            pltpu.VMEM((count * bins // 128 + 2, 16, 128), jnp.bfloat16),
            pltpu.VMEM((384, 384), jnp.bfloat16),
            pltpu.VMEM((8, 384), jnp.float32),
        ],
        compiler_params=pltpu.CompilerParams(vmem_limit_bytes=8 * MB),
        name="pieces",
    )(place, taps, parts)


def row_filter_kernel(place, taps, parts, out, mine, blocks, weights, line):
    rows, bins = parts.shape[1:]
    per = bins // 128
    count = parts.shape[0] * per
    blocks[0] = jnp.zeros((rows, 128), jnp.bfloat16)
    blocks[count + 1] = jnp.zeros((rows, 128), jnp.bfloat16)
    for n in range(count):
        b = n % per
        blocks[1 + n] = parts[n // per, :, b * 128 : (b + 1) * 128]
    band(taps, line, weights)
    group = 8
    for g in range(0, count, group):
        value = filtered_blocks(lambda k: blocks[g + k : g + k + group], weights)
        for b in range(group):
            n = g + b
            out[:, n * 128 : (n + 1) * 128] = value[b * rows : (b + 1) * rows]
    mine[...] = out[:, pl.ds(pl.multiple_of(place[2] * bins, 128), bins)]


def run_row_filter(place, taps, parts):
    count, rows, bins = parts.shape
    vmem = pl.BlockSpec(memory_space=pltpu.VMEM)
    return pl.pallas_call(
        row_filter_kernel,
        in_specs=[pl.BlockSpec(memory_space=pltpu.SMEM), vmem, vmem],
        out_specs=[vmem, vmem],
        out_shape=[
            jax.ShapeDtypeStruct((rows, count * bins), jnp.bfloat16),
            jax.ShapeDtypeStruct((rows, bins), jnp.bfloat16),
        ],
        scratch_shapes=[
            pltpu.VMEM((count * bins // 128 + 2, rows, 128), jnp.bfloat16),
            pltpu.VMEM((384, 384), jnp.bfloat16),
            pltpu.VMEM((8, 384), jnp.float32),
        ],
        compiler_params=pltpu.CompilerParams(vmem_limit_bytes=8 * MB),
        cost_estimate=pl.CostEstimate(flops=1 << 30, bytes_accessed=4 * MB, transcendentals=0),
        name="rows",
    )(place, taps, parts)


def lag_kernel(rows_ref, out, energy):
    bins = rows_ref.shape[1]
    at = lax.broadcasted_iota(jnp.int32, (16, bins), 1)
    for part in range(rows_ref.shape[0] // 16):
        span = slice(part * 16, (part + 1) * 16)
        value = rows_ref[span].astype(jnp.float32)
        total = jnp.sum(value * value, axis=1, keepdims=True)
        energy[span] = jnp.broadcast_to(total, (16, 128))
        for lag in range(LAGS):
            step = lag - REACH
            if step == 0:
                moved = value
            else:
                moved = pltpu.roll(value, step % bins, axis=1)
                inside = at >= step if step > 0 else at < bins + step
                moved = jnp.where(inside, moved, 0.0)
            out[lag, span] = moved.astype(jnp.bfloat16)


def run_lags(rows):
    count, bins = rows.shape
    vmem = pl.BlockSpec(memory_space=pltpu.VMEM)
    return pl.pallas_call(
        lag_kernel,
        in_specs=[vmem],
        out_specs=[vmem, vmem],
        out_shape=[
            jax.ShapeDtypeStruct((LAGS, count, bins), jnp.bfloat16),
            jax.ShapeDtypeStruct((count, 128), jnp.float32),
        ],
        compiler_params=pltpu.CompilerParams(vmem_limit_bytes=8 * MB),
        cost_estimate=pl.CostEstimate(flops=10 * MB, bytes_accessed=6 * MB, transcendentals=0),
        name="lags",
    )(rows)


def weigh(lagged, energy, right, across, emit):
    lags, count, bins = lagged.shape
    left = lagged[...].reshape(lags * count, bins)
    moments = lax.dot_general(left, right, NT, preferred_element_type=jnp.float32)
    norms = (1.0 / jnp.sqrt(energy[:, 0:1] + 1e-05)) * across
    for lag in range(lags):
        ratio = moments[lag * count : (lag + 1) * count] * norms
        emit(lag, -0.5 * jnp.log(1.0 - ratio * ratio))


def columns_kernel(steps, place, lagged, energy, *refs):
    units = refs[: len(steps)]
    columns, scale, out = refs[len(steps) :]
    z = place[1]
    slab = place[2]
    for ref, moves in zip(units, steps):
        for k, (part, z_step) in enumerate(moves):
            up = (z + z_step - 2 * slab - 1) & 7
            e = (up < 4).astype(jnp.int32)
            giver = (3 - jnp.where(up < 4, up, 7 - up)) ^ slab
            columns[e * 16 + (part >> 1) * 8 + giver * 2 + (part & 1)] = ref[k]
    lags, count, bins = lagged.shape
    left = lagged[...].reshape(lags * count, bins)
    right = columns[...].reshape(-1, bins)
    moments = lax.dot_general(left, right, NT, preferred_element_type=jnp.float32)
    for g in range(right.shape[0] // 128):
        block = right[g * 128 : (g + 1) * 128].astype(jnp.float32)
        total = jnp.sum(block * block, axis=1, keepdims=True)
        root = 0.8 / jnp.sqrt(total + 1e-05)
        root = jnp.transpose(jnp.broadcast_to(root, (128, 128)))
        scale[:, g * 128 : (g + 1) * 128] = root[0:8]
    emit(moments, energy, scale, SCALE, out)


def run_columns(place, rows, units, steps):
    slots = sum(len(moves) for moves in steps)
    lags, count, bins = rows[0].shape

    def body(*refs):
        columns_kernel(steps, *refs)

    vmem = pl.BlockSpec(memory_space=pltpu.VMEM)
    return pl.pallas_call(
        body,
        in_specs=[pl.BlockSpec(memory_space=pltpu.SMEM)] + [vmem] * (2 + len(units)),
        out_specs=[vmem] * 3,
        out_shape=[
            jax.ShapeDtypeStruct((slots, 8, bins), jnp.bfloat16),
            jax.ShapeDtypeStruct((8, slots * 8), jnp.float32),
            jax.ShapeDtypeStruct((lags, count, slots * 8), jnp.float32),
        ],
        compiler_params=pltpu.CompilerParams(vmem_limit_bytes=8 * MB),
        cost_estimate=pl.CostEstimate(flops=1 << 30, bytes_accessed=4 * MB, transcendentals=0),
        name="columns",
    )(place, *rows, *units)


def emit(moments, energy, scale, factor, out):
    lags, count = out.shape[:2]
    norms = (1.0 / jnp.sqrt(energy[:, 0:1] + 1e-05)) * scale[0:1, :]
    for lag in range(lags):
        ratio = moments[lag * count : (lag + 1) * count] * norms
        value = -0.5 * jnp.log(1.0 - ratio * ratio)
        out[lag] = value if factor == 1 else value * factor


def weigh_kernel(factor, lagged, energy, columns, scale, out):
    lags, count, bins = lagged.shape
    left = lagged[...].reshape(lags * count, bins)
    right = columns[...].reshape(-1, bins)
    moments = lax.dot_general(left, right, NT, preferred_element_type=jnp.float32)
    emit(moments, energy, scale, factor, out)


def run_weigh(rows, columns, scale, factor):
    lagged, energy = rows
    lags, count, bins = lagged.shape
    width = scale.shape[1]

    def body(*refs):
        weigh_kernel(factor, *refs)

    vmem = pl.BlockSpec(memory_space=pltpu.VMEM)
    return pl.pallas_call(
        body,
        in_specs=[vmem] * 4,
        out_specs=vmem,
        out_shape=jax.ShapeDtypeStruct((lags, count, width), jnp.float32),
        compiler_params=pltpu.CompilerParams(vmem_limit_bytes=8 * MB),
        cost_estimate=pl.CostEstimate(
            flops=2 * lags * count * width * bins,
            bytes_accessed=4 * lags * count * width,
            transcendentals=lags * count * width,
        ),
        name="weigh",
    )(lagged, energy, columns, scale)


def join_kernel(flip, place, same, cross, *refs):
    out, tiles, sems = refs[-3:]
    low = place[4] == 0
    here_x = place[3] ^ flip
    lags, rows, width = same.shape
    lane = lax.broadcasted_iota(jnp.int32, (rows, 128), 1) < 64
    copies = []
    for group in range(0, lags, 3):
        for half in range(width // 128):
            span = slice(half * 128, (half + 1) * 128)
            for lag in range(group, group + 3):
                here = same[lag, :, span] * (1.0 / SCALE) if flip else same[lag, :, span]
                there = cross[lag, :, span] * (1.0 / SCALE)
                one = jnp.where(low, here, there)
                two = jnp.where(low, there, here)
                tiles[half * 2, lag] = jnp.where(lane, one, pltpu.roll(two, 64, axis=1))
                tiles[half * 2 + 1, lag] = jnp.where(lane, pltpu.roll(one, 64, axis=1), two)
            for k, to_x in enumerate((here_x, here_x ^ 2)):
                at = pl.multiple_of((half * 4 + to_x) * 128, 128)
                source = tiles.at[half * 2 + k, pl.ds(group, 3)]
                target = out.at[pl.ds(group, 3), :, pl.ds(at, 128)]
                copies.append(pltpu.make_async_copy(source, target, sems.at[len(copies)]))
                copies[-1].start()
    for copy in copies:
        copy.wait()


def run_join(place, flip, same, cross, *base):
    lags, rows, width = same.shape
    vmem = pl.BlockSpec(memory_space=pltpu.VMEM)
    hbm = pl.BlockSpec(memory_space=pltpu.HBM)

    def body(*refs):
        join_kernel(flip, *refs)

    return pl.pallas_call(
        body,
        in_specs=[pl.BlockSpec(memory_space=pltpu.SMEM), vmem, vmem] + [hbm] * len(base),
        out_specs=hbm,
        out_shape=jax.ShapeDtypeStruct((lags, rows, 4 * width), jnp.float32),
        input_output_aliases={3: 0} if base else {},
        scratch_shapes=[
            pltpu.VMEM((width // 64, lags, rows, 128), jnp.float32),
            pltpu.SemaphoreType.DMA((width // 64 * (lags // 3),)),
        ],
        compiler_params=pltpu.CompilerParams(vmem_limit_bytes=8 * MB),
        name="join",
    )(place, same, cross, *base)


def around(value, axis, step):
    size = lax.axis_size(axis)
    return lax.ppermute(value, axis, [(i, (i + step) % size) for i in range(size)])


def cross_y(value):
    return lax.ppermute(value, "yh", [(0, 1), (1, 0)])


def cross_x(value):
    return lax.ppermute(value, "x", [(0, 1), (1, 0), (2, 3), (3, 2)])


def cross_xy(value):
    return lax.ppermute(value, ("x", "yh"), [(i, i ^ 3) for i in range(8)])


def spread(value, across):
    pairs = []
    for z in range(8):
        a, e = z >> 1, z & 1
        for x in range(4):
            for q in range(4):
                far = 3 - (q ^ a)
                to = (z + far if e else z - far) % 8
                pairs.append(((z * 4 + x) * 4 + q, (to * 4 + (x ^ across)) * 4 + a))
    return lax.ppermute(value, ("z", "x", "yl", "core"), pairs)


def after(value, *others):
    return lax.optimization_barrier((value, *others))[0]


def shards(raw, taps):
    z = lax.axis_index("z")
    x = lax.axis_index("x")
    yh = lax.axis_index("yh")
    q = lax.axis_index(("yl", "core"))
    place = jnp.stack([yh, z, q, x, yh]).astype(jnp.int32)
    taps = taps.reshape(1, -1)
    parts = lax.all_gather(raw, ("yl", "core"), axis=0, tiled=False)
    given = run_piece_filter(place, taps, parts)
    base = jnp.concatenate([spread(given, 2), spread(given, 0)], axis=0)
    order = (2, 3, 0, 1)
    units, steps = [base], [[(part, 0) for part in order]]
    first = (around(base, "z", 1), around(base, "z", -1))
    second = (around(first[0], "z", 1), around(first[1], "z", -1))
    full, mine = run_row_filter(place, taps, after(parts, given))
    row_y = cross_y(full)
    row_x = cross_x(full)
    row_xy = cross_x(after(row_y, first[0]))
    far_y = run_lags(after(row_y, *second))
    third = (around(second[0], "z", 1), around(second[1], "z", -1))
    far_x = run_lags(after(row_x, *third))
    ready = after(third[0], far_y), after(third[1], far_y)
    units += [*first, *second, *third, around(ready[0][0:2], "z", 1), around(ready[1][2:4], "z", -1)]
    for step in (1, 2, 3):
        steps += [[(part, -step) for part in order], [(part, step) for part in order]]
    steps += [[(part, 4) for part in order[0:2]], [(part, 4) for part in order[2:4]]]
    far_xy = run_lags(after(row_xy, *third))
    columns, scale, send_xy = run_columns(place, far_xy, units, steps)
    send_xy = send_xy.astype(SENT)
    send_x = run_weigh(far_x, columns, after(scale, send_xy), SCALE).astype(SENT)
    send_y = run_weigh(far_y, columns, scale, SCALE).astype(SENT)
    came_xy = cross_xy(send_xy)
    came_x = cross_x(send_x)
    came_y = cross_y(send_y)
    got_xy = came_xy.astype(jnp.float32)
    got_x = after(came_x, got_xy).astype(jnp.float32)
    base = run_join(place, 1, got_x, got_xy)
    got_y = after(came_y, base).astype(jnp.float32)
    own = run_lags(after(full, scale))
    kept = run_weigh(own, columns, scale, 1)
    information = run_join(place, 0, kept, got_y, base)
    return (information, mine)


def solution(mesh):
    fine = Mesh(mesh.devices.reshape(8, 4, 2, 2, 2), ("z", "x", "yh", "yl", "core"))
    rows, bins = ("z", "x", "yh"), ("yl", "core")
    return jax.shard_map(
        shards,
        mesh=fine,
        in_specs=(P(rows, bins), P()),
        out_specs=(P(None, rows, bins), P(rows, bins)),
        check_vma=False,
    )
```
